128 devices in a mesh: ctx: 16 (over y, z_hi, core), dp: 8 (over x, z_lo).
Axes of the slice: x: 4, y: 4, z: 4 (z_hi: 2, z_lo: 2; z = z_hi * 2 + z_lo), core: 2. Of those that a mesh axis runs over, the one named last changes fastest.
Arguments:
- tokens: bfloat16 [8, 4096, 16384], P('dp', 'ctx'), may hold values from -6 to 6
- queries: bfloat16 [8, 4096, 1024], P('dp', 'ctx'), may hold values from -200 to 200
- cotangent: bfloat16 [8, 4096, 1024], P('dp', 'ctx'), may hold values from -6 to 6
- latent_key: float32 [16384, 128], P(('ctx', 'dp')), may hold values from -1 to 1
- latent_value: float32 [16384, 128], P(('ctx', 'dp')), may hold values from -1 to 1
- lengths: int32 [8, 8], P('dp'), may hold values from 1 to 2048, 4096 in all within a row
- block_order: int32 [8, 32], P('dp'), may hold values from 0 to 31, each once within a row
Outputs:
- attn_out: bfloat16 [8, 4096, 1024], P('dp', 'ctx')
- query_grad: bfloat16 [8, 4096, 1024], P('dp', 'ctx')
- token_grad: bfloat16 [8, 4096, 16384], P('dp', 'ctx')
- key_weight_grad: float32 [16384, 128], P(('ctx', 'dp'))
- value_weight_grad: float32 [16384, 128], P(('ctx', 'dp'))
The draws below stay inside these ranges and needn't reach their ends.
Inputs may be any that keep to these rules, and one draw needn't show every extreme that they name: Each row holds the lengths of the 8 documents packed into one sequence, in order; they sum to 4096 and the largest is exactly 2048. Each row is a permutation; stored block b of a sequence (rows b * 128 to (b + 1) * 128 - 1) holds the tokens at positions block_order[b] * 128 to block_order[b] * 128 + 127.
All inputs are finite; a program needn't handle non-finite values. Where the reference program divides by a largest or mean magnitude, that divisor is 1e-20 or more.
Results may differ from the reference program's by a relative error of at most 0.02.
The reference program's roundings to bfloat16 on the way (of `weights` and `score_grad`) count: a program that leaves them out, or rounds other values in their place, can miss the bound.
Values may be sent and summed in bfloat16 or wider, within the bound.
No kernel may reach another device: no remote copies, remote signals or barrier semaphores. Data moves between devices by JAX's collectives and lax.ppermute only.
A program may use at most 128 MiB of HBM per device.

```python
import functools
import math
import jax
import jax.numpy as jnp
import numpy as np
from jax import lax

D = 16384
HD = 128
HEADS = 8
DOCS = 8
SEQS = 8
LEN = 4096
BLK = 128
BLOCKS = 32
MOST = 2048


def latent_matrix(key, salt):
    mixed_key = jax.random.fold_in(key, salt)
    entry_key, row_key, column_key = jax.random.split(mixed_key, 3)
    row_ramp = jnp.arange(D, dtype=jnp.float32) / D
    row_scale = jnp.exp(math.log(10.0) * (0.5 * row_ramp + 0.5 * jax.random.uniform(row_key, (D,), jnp.float32)))
    column_scale = jnp.exp(math.log(10.0) * jax.random.uniform(column_key, (HD,), jnp.float32))
    entries = jax.random.normal(entry_key, (D, HD), jnp.float32)
    raw = entries * row_scale[:, None] * column_scale[None, :]
    normed = raw / jnp.mean(jnp.abs(raw))
    magnitude = jnp.abs(normed)
    inside = (magnitude > 0.38) & (magnitude < 0.62)
    moved = jnp.where(inside, jnp.where(magnitude < 0.5, magnitude - 0.12, magnitude + 0.12), magnitude)
    shaped = jnp.where(normed < 0.0, -moved, moved)
    return shaped / jnp.max(jnp.abs(shaped))


def draw_latent_key(key, part):
    return latent_matrix(key, 11)


def draw_latent_value(key, part):
    return latent_matrix(key, 23)


def draw_queries(key, part):
    shaped_key = jax.random.fold_in(key, 37)
    entries = jax.random.normal(shaped_key, (SEQS, LEN, HEADS * HD), jnp.float32)
    return jnp.clip(entries, -200.0, 200.0).astype(jnp.bfloat16)


def steps_of(key, dims, cuts, smallest, high):
    loudness = 1.0
    for dim, blocks in cuts:
        draws = jax.random.uniform(jax.random.fold_in(jax.random.fold_in(key, 6), dim), (blocks,), jnp.float32, smallest / len(cuts), high / len(cuts))
        loudness = loudness * jnp.repeat(jnp.exp(draws), dims[dim] // blocks).reshape((-1,) + (1,) * (len(dims) - 1 - dim))
    return loudness


def split_up(count, total, most, skew):
    weights = [(1 << 20) // math.isqrt(grade ** skew) + 1 for grade in range(2, count + 1)]
    surplus, counts = total - most - (count - 1), [1] * (count - 1)
    while surplus > 0:
        free = [i for i in range(count - 1) if counts[i] < most]
        whole, left = sum([weights[i] for i in free]), surplus
        for i in free:
            addition = min(most - counts[i], max(1, left * weights[i] // whole), surplus)
            counts[i] = counts[i] + addition
            surplus = surplus - addition
    return np.array([most] + counts)


def uneven(stream_key, number_of, total, limit, lean):
    if number_of == 2:
        one = jax.random.randint(stream_key, (), max(1, total - limit), min(limit, total - 1) + 1)
        return jnp.stack([one, total - one])
    tallies = jnp.asarray(split_up(number_of, total, limit, lean), jnp.int32)
    pairs = (number_of - 1) // 2
    source_of, taker = tallies[1:1 + 2 * pairs:2], tallies[2:2 + 2 * pairs:2]
    margin = jnp.minimum(source_of - 1, limit - taker)
    passed = jax.random.randint(jax.random.fold_in(stream_key, 1), (pairs,), 0, 1 << 20) % (margin + 1)
    tallies = tallies.at[1:1 + 2 * pairs:2].set(source_of - passed).at[2:2 + 2 * pairs:2].set(taker + passed)
    return tallies[jax.random.permutation(jax.random.fold_in(stream_key, 2), number_of)]


def centred(stream_key, dims, width, limit, pieces=(), held_as=jnp.bfloat16):
    loudness = steps_of(stream_key, dims, pieces, -0.22, 0.18) if pieces else 1.0
    values = jax.random.normal(stream_key, dims, jnp.float32) * width * loudness
    return jnp.minimum(jnp.maximum(values, -limit), limit).astype(held_as)


def setup_inputs(seed: int = 0) -> dict:
    key_of = jax.random.split(jax.random.key(seed), 8)
    return {
        "tokens": centred(key_of[0], (SEQS, LEN, D), 1.0, 6.0, ((0, 8), (1, 16))),
        "queries": draw_queries(jax.random.fold_in(key_of[7], 71), 0),
        "cotangent": centred(key_of[2], (SEQS, LEN, HEADS * HD), 1.0, 6.0, ((0, 8), (1, 16))),
        "latent_key": draw_latent_key(jax.random.fold_in(key_of[7], 71), 0),
        "latent_value": draw_latent_value(jax.random.fold_in(key_of[7], 71), 0),
        "lengths": jax.vmap(lambda own: uneven(own, DOCS, LEN, MOST, 2))(jax.random.split(key_of[5], SEQS)).reshape((SEQS, DOCS)).astype(jnp.int32),
        "block_order": jax.vmap(lambda own: jax.random.permutation(own, BLOCKS))(jax.random.split(key_of[6], SEQS)).reshape((SEQS, BLOCKS)).astype(jnp.int32),
    }


EPSILON = 1e-5
NEGATIVE = -1e30


def rounded(value):
    return lax.optimization_barrier(value.astype(jnp.bfloat16)).astype(jnp.float32)


def levels(ratio):
    return jnp.where(ratio >= 0.5, 1.0, jnp.where(ratio <= -0.5, -1.0, 0.0)).astype(ratio.dtype)


def ternary(latent):
    scale_value = jnp.mean(jnp.abs(latent)) + EPSILON
    return (scale_value * levels(latent / scale_value)).astype(jnp.bfloat16)


def layout(lengths_row, order_row):
    stored = jnp.arange(LEN, dtype=jnp.int32)
    owner = order_row[stored // BLK].astype(jnp.int32)
    position = owner * BLK + stored % BLK
    doc_starts = (jnp.cumsum(lengths_row, dtype=jnp.int32) - lengths_row).astype(jnp.int32)
    document = jnp.sum((position[:, None] >= doc_starts[None, :]).astype(jnp.int32), axis=1).astype(jnp.int32)
    return position, document


def one_sequence(items, both):
    token_rows, query_rows, cot_rows, lengths_row, order_row = items
    projected = rounded(jnp.dot(token_rows, both, preferred_element_type=jnp.float32))
    keys = projected[:, :HD]
    values = projected[:, HD:]
    position, document = layout(lengths_row, order_row)
    block_size = math.gcd(LEN, 512)
    block_count = LEN // block_size
    scale_factor = HD ** -0.5
    query_blocks = query_rows.astype(jnp.float32).reshape(block_count, block_size, HEADS, HD)
    cot_blocks = cot_rows.astype(jnp.float32).reshape(block_count, block_size, HEADS, HD)
    pos_blocks = position.reshape(block_count, block_size)
    doc_blocks = document.reshape(block_count, block_size)

    def scores_of(query_block, pos_block, doc_block):
        scores = jnp.einsum("thd,sd->hts", query_block, keys) * scale_factor
        visible = (position[None, :] <= pos_block[:, None]) & (document[None, :] == doc_block[:, None])
        return jnp.where(visible[None], scores, NEGATIVE), visible

    def forward(block_item):
        query_block, pos_block, doc_block = block_item
        scores, visible = scores_of(query_block, pos_block, doc_block)
        highest = jnp.max(scores, axis=2)
        weights = jnp.where(visible[None], jnp.exp(scores - highest[:, :, None]), 0.0)
        total = jnp.sum(weights, axis=2)
        mixed = jnp.einsum("hts,sd->thd", rounded(weights), values) / total.T[:, :, None]
        return mixed.astype(jnp.bfloat16), highest + jnp.log(total)

    outputs, log_totals = lax.map(forward, (query_blocks, pos_blocks, doc_blocks))

    def backward(accum, block_item):
        query_block, cot_block, out_block, log_total, pos_block, doc_block = block_item
        scores, visible = scores_of(query_block, pos_block, doc_block)
        probability = jnp.where(visible[None], jnp.exp(scores - log_total[:, :, None]), 0.0)
        prob_grad = jnp.einsum("thd,sd->hts", cot_block, values)
        expected = jnp.sum(cot_block * out_block.astype(jnp.float32), axis=2).T
        score_grad = rounded(probability * (prob_grad - expected[:, :, None]))
        query_grad = (jnp.einsum("hts,sd->thd", score_grad, keys) * scale_factor).astype(jnp.bfloat16)
        key_part = jnp.einsum("hts,thd->sd", score_grad, query_block) * scale_factor
        value_part = jnp.einsum("hts,thd->sd", rounded(probability), cot_block)
        return (accum[0] + key_part, accum[1] + value_part), query_grad

    start_acc = (jnp.zeros((LEN, HD), jnp.float32), jnp.zeros((LEN, HD), jnp.float32))
    (key_cot, value_cot), query_grads = lax.scan(
        backward, start_acc, (query_blocks, cot_blocks, outputs, log_totals, pos_blocks, doc_blocks))
    cot_both = jnp.concatenate([key_cot.astype(jnp.bfloat16), value_cot.astype(jnp.bfloat16)], axis=1)
    token_grad = lax.dot_general(cot_both, both, (((1,), (1,)), ((), ())),
                                 preferred_element_type=jnp.float32).astype(jnp.bfloat16)
    weight_term = lax.dot_general(token_rows, cot_both, (((0,), (0,)), ((), ())),
                                  preferred_element_type=jnp.float32)
    return (outputs.reshape(LEN, HEADS * HD), query_grads.reshape(LEN, HEADS * HD), token_grad, weight_term)


def reference(tokens, queries, cotangent, latent_key, latent_value, lengths, block_order):
    key_ternary = ternary(latent_key)
    value_ternary = ternary(latent_value)
    both = jnp.concatenate([key_ternary, value_ternary], axis=1)
    attn_out, query_grad, token_grad, weight_terms = lax.map(
        functools.partial(one_sequence, both=both), (tokens, queries, cotangent, lengths, block_order))
    summed = jnp.sum(weight_terms, axis=0)
    key_weight_grad = summed[:, :HD]
    value_weight_grad = summed[:, HD:]
    return (attn_out, query_grad, token_grad, key_weight_grad, value_weight_grad)
```

```python
import functools

import jax
import jax.numpy as jnp
import numpy as np
from jax import lax
from jax.experimental import pallas as pl
from jax.experimental.pallas import tpu as pltpu
from jax.sharding import Mesh
from jax.sharding import PartitionSpec as P

AXES = ("y", "zh", "core", "x", "zl")
SIZES = (4, 2, 2, 4, 2)
CTX = ("y", "zh", "core")
DP = ("x", "zl")
SAME_CORE_CTX = ("y", "zh")
DEVICES = int(np.prod(SIZES))

EPSILON = 1e-05
NEGATIVE = -1e30
KEY_CHUNK = 256

RING_ORDER = {0: ("x", "y", "z"), 1: ("y", "z", "x")}
OFFSETS = (0, -1, 1, 2)


def coordinates(device):
    y, zh, core, x, zl = (int(v) for v in np.unravel_index(device, SIZES))
    return {"y": y, "z": zh * 2 + zl, "x": x, "core": core}


def device_of(place):
    return int(
        np.ravel_multi_index(
            (place["y"], place["z"] // 2, place["core"], place["x"], place["z"] % 2), SIZES
        )
    )


def moved(change):
    pairs = []
    for device in range(DEVICES):
        place = coordinates(device)
        change(place)
        pairs.append((device, device_of(place)))
    return pairs


def along_ring(phase, step):
    def change(place):
        axis = RING_ORDER[place["core"]][phase]
        place[axis] = (place[axis] + step) % 4

    return moved(change)


def to_other_core(place):
    place["core"] = 1 - place["core"]


def swap_cores(value):
    return lax.ppermute(value, AXES, moved(to_other_core))


def block_table():
    table = np.zeros((DEVICES, DEVICES), np.int32)
    for device in range(DEVICES):
        here = coordinates(device)
        at = 0
        for core in (here["core"], 1 - here["core"]):
            order = RING_ORDER[core]
            for last in OFFSETS:
                for middle in OFFSETS:
                    for first in OFFSETS:
                        place = dict(here, core=core)
                        for axis, step in zip(order, (first, middle, last)):
                            place[axis] = (place[axis] + step) % 4
                        table[device, at] = device_of(place)
                        at += 1
    return table


def gather_ring(value, phase):
    return [value] + [
        lax.ppermute(value, AXES, along_ring(phase, -offset)) for offset in OFFSETS[1:]
    ]


def reduce_ring(pieces, phase):
    total = pieces[0]
    for piece, offset in zip(pieces[1:], OFFSETS[1:]):
        sent = lax.ppermute(piece.astype(jnp.bfloat16), AXES, along_ring(phase, offset))
        total = total + sent.astype(jnp.float32)
    return total


def levels(ratio):
    return jnp.where(ratio >= 0.5, 1.0, jnp.where(ratio <= -0.5, -1.0, 0.0)).astype(jnp.float32)


def shuffle_kernel(table, tokens, own, other, own_sem, other_sem):
    width = own.shape[1] * 2 // DEVICES
    for half, (out, sem) in enumerate(((other, other_sem), (own, own_sem))):
        first = 0 if half else DEVICES // 2

        def start(j, _, out=out, sem=sem, first=first):
            source = pl.ds(pl.multiple_of(table[first + j] * width, width), width)
            target = pl.ds(pl.multiple_of(j * width, width), width)
            pltpu.make_async_copy(tokens.at[:, source], out.at[:, target], sem).start()
            return 0

        lax.fori_loop(0, DEVICES // 2, start, 0)
    pltpu.make_async_copy(other, other, other_sem).wait()
    pltpu.make_async_copy(own, own, own_sem).wait()


def shuffle(table, tokens):
    rows, features = tokens.shape
    half = jax.ShapeDtypeStruct((rows, features // 2), tokens.dtype)
    anywhere = pl.BlockSpec(memory_space=pl.ANY)
    return pl.pallas_call(
        shuffle_kernel,
        out_shape=(half, half),
        in_specs=[pl.BlockSpec(memory_space=pltpu.SMEM), anywhere],
        out_specs=(anywhere, anywhere),
        scratch_shapes=[pltpu.SemaphoreType.DMA, pltpu.SemaphoreType.DMA],
        cost_estimate=pl.CostEstimate(
            flops=0, bytes_accessed=4 * rows * features, transcendentals=0
        ),
        name="shuffle_tokens",
    )(table, tokens)


def token_grad_kernel(table, grads, *rest, count):
    weights, out = rest[:count], rest[count]
    buffers, sems = rest[count + 1 :]
    rows, step_width = buffers.shape[1:]
    width = out.shape[1] // DEVICES
    per_step = step_width // width
    steps_each = weights[0].shape[0] // step_width
    for step in range(count * steps_each):
        slot = step % 2
        buffer, sem = buffers.at[slot], sems.at[slot]
        if step >= 2:
            pltpu.make_async_copy(buffer, buffer, sem).wait()
        part = (step % steps_each) * step_width
        buffers[slot] = lax.dot_general(
            grads[...],
            weights[step // steps_each][part : part + step_width, :],
            (((1,), (1,)), ((), ())),
            preferred_element_type=jnp.float32,
        ).astype(jnp.bfloat16)
        for j in range(per_step):
            target = pl.ds(pl.multiple_of(table[step * per_step + j] * width, width), width)
            pltpu.make_async_copy(
                buffer.at[:, j * width : (j + 1) * width], out.at[:, target], sem
            ).start()
    for slot in range(2):
        pltpu.make_async_copy(buffers.at[slot], buffers.at[slot], sems.at[slot]).wait()


def token_gradient(table, grads, weights):
    rows, both = grads.shape
    features = sum(w.shape[0] for w in weights)
    step_width = 1024
    in_vmem = pl.BlockSpec(memory_space=pltpu.VMEM)
    return pl.pallas_call(
        functools.partial(token_grad_kernel, count=len(weights)),
        out_shape=jax.ShapeDtypeStruct((rows, features), jnp.bfloat16),
        in_specs=[pl.BlockSpec(memory_space=pltpu.SMEM)] + [in_vmem] * (1 + len(weights)),
        out_specs=pl.BlockSpec(memory_space=pl.ANY),
        scratch_shapes=[
            pltpu.VMEM((2, rows, step_width), jnp.bfloat16),
            pltpu.SemaphoreType.DMA((2,)),
        ],
        compiler_params=pltpu.CompilerParams(vmem_limit_bytes=32 << 20),
        cost_estimate=pl.CostEstimate(
            flops=2 * rows * both * features,
            bytes_accessed=2 * features * (rows + both),
            transcendentals=0,
        ),
        name="token_gradient",
    )(table, grads, *weights)


def attention_kernel(
    meta, queries, cotangent, kv_same, kv_other, mixed_out, query_grad, same_out, other_out,
    keys, values, key_acc, value_acc, scores, q_columns, c_columns, q_rows, c_rows,
    *, heads, head_size, block, docs, blocks,
):
    scale = head_size ** (-0.5)
    columns = heads * block
    ctx, core = meta[docs + blocks], meta[docs + blocks + 1]
    sides = ((kv_same, core, same_out), (kv_other, 1 - core, other_out))

    def rows_at(index, size):
        return pl.ds(pl.multiple_of(index * size, size), size)

    def true_block(core_of, j):
        return meta[docs + ((j // 2) * 2 + core_of) * 2 + j % 2]

    for ref, core_of, _ in sides:
        for j in range(blocks // 2):
            target = rows_at(true_block(core_of, j), block)
            keys[target, :] = ref[j * block : (j + 1) * block, :head_size]
            values[target, :] = ref[j * block : (j + 1) * block, head_size:]
    key_acc[...] = jnp.zeros_like(key_acc)
    value_acc[...] = jnp.zeros_like(value_acc)

    def one_block(i, _):
        here = rows_at(i, block)
        for h in range(heads):
            head = slice(h * head_size, (h + 1) * head_size)
            part = slice(h * block, (h + 1) * block)
            q, c = queries[here, head], cotangent[here, head]
            q_rows[part, :], c_rows[part, :] = q, c
            q_columns[:, part], c_columns[:, part] = q.T, c.T
        start = meta[docs + 2 * ctx + i] * block
        position = start + lax.rem(lax.broadcasted_iota(jnp.int32, (1, columns), 1), block)
        own_start = jnp.zeros((1, columns), jnp.int32)
        first = jnp.int32(0)
        for d in range(docs):
            doc_start = meta[d]
            own_start = jnp.maximum(own_start, jnp.where(position >= doc_start, doc_start, 0))
            first = jnp.maximum(first, jnp.where(start >= doc_start, doc_start, 0))
        lowest = first // KEY_CHUNK
        count = (start + block - 1) // KEY_CHUNK - lowest + 1

        def score(c, best):
            s = scale * jnp.dot(
                keys[rows_at(lowest + c, KEY_CHUNK), :],
                q_columns[...],
                preferred_element_type=jnp.float32,
            )
            key_pos = (lowest + c) * KEY_CHUNK + lax.broadcasted_iota(
                jnp.int32, (KEY_CHUNK, columns), 0
            )
            s = jnp.where((key_pos >= own_start) & (key_pos <= position), s, NEGATIVE)
            scores[c] = s
            return jnp.maximum(best, jnp.max(s.reshape(KEY_CHUNK // 8, 8, columns), axis=0))

        best = lax.fori_loop(
            0, count, score, jnp.full((8, columns), NEGATIVE, jnp.float32)
        )
        best = jnp.max(best, axis=0, keepdims=True)

        def mix(c, carried):
            total, acc = carried
            w = jnp.exp(scores[c] - best)
            scores[c] = w
            total = total + jnp.sum(w.reshape(KEY_CHUNK // 8, 8, columns), axis=0)
            acc = acc + lax.dot_general(
                values[rows_at(lowest + c, KEY_CHUNK), :],
                w.astype(jnp.bfloat16),
                (((0,), (0,)), ((), ())),
                preferred_element_type=jnp.float32,
            )
            return total, acc

        total, acc = lax.fori_loop(
            0,
            count,
            mix,
            (jnp.zeros((8, columns), jnp.float32), jnp.zeros((head_size, columns), jnp.float32)),
        )
        total = jnp.sum(total, axis=0, keepdims=True)
        mixed = (acc / total).astype(jnp.bfloat16)
        expected = jnp.sum(
            mixed.astype(jnp.float32) * c_columns[...].astype(jnp.float32), axis=0, keepdims=True
        )
        per_total = 1.0 / total
        for h in range(heads):
            mixed_out[here, h * head_size : (h + 1) * head_size] = mixed[
                :, h * block : (h + 1) * block
            ].T

        def back(c, q_acc):
            at = rows_at(lowest + c, KEY_CHUNK)
            probability = scores[c] * per_total
            prob_grad = jnp.dot(values[at, :], c_columns[...], preferred_element_type=jnp.float32)
            score_grad = (probability * (prob_grad - expected)).astype(jnp.bfloat16)
            key_acc[at, :] += jnp.dot(score_grad, q_rows[...], preferred_element_type=jnp.float32)
            value_acc[at, :] += jnp.dot(
                probability.astype(jnp.bfloat16), c_rows[...], preferred_element_type=jnp.float32
            )
            return q_acc + lax.dot_general(
                keys[at, :],
                score_grad,
                (((0,), (0,)), ((), ())),
                preferred_element_type=jnp.float32,
            )

        q_acc = lax.fori_loop(
            0, count, back, jnp.zeros((head_size, columns), jnp.float32)
        )
        q_grad = (q_acc * scale).astype(jnp.bfloat16)
        for h in range(heads):
            query_grad[here, h * head_size : (h + 1) * head_size] = q_grad[
                :, h * block : (h + 1) * block
            ].T
        return 0

    lax.fori_loop(0, queries.shape[0] // block, one_block, 0)
    for _, core_of, out in sides:
        for j in range(blocks // 2):
            source = rows_at(true_block(core_of, j), block)
            part = slice(j * block, (j + 1) * block)
            out[part, :head_size] = (key_acc[source, :] * scale).astype(out.dtype)
            out[part, head_size:] = value_acc[source, :].astype(out.dtype)


def attention(meta, queries, cotangent, kv_same, kv_other, head_size, docs, blocks):
    rows, width = queries.shape
    heads = width // head_size
    length = kv_same.shape[0] + kv_other.shape[0]
    block = length // blocks
    columns = heads * block
    in_vmem = pl.BlockSpec(memory_space=pltpu.VMEM)
    most_chunks = 10
    visible = 9 * KEY_CHUNK
    return pl.pallas_call(
        functools.partial(
            attention_kernel, heads=heads, head_size=head_size, block=block, docs=docs, blocks=blocks
        ),
        out_shape=(
            jax.ShapeDtypeStruct((rows, width), jnp.bfloat16),
            jax.ShapeDtypeStruct((rows, width), jnp.bfloat16),
            jax.ShapeDtypeStruct(kv_same.shape, jnp.float32),
            jax.ShapeDtypeStruct(kv_other.shape, jnp.bfloat16),
        ),
        in_specs=[pl.BlockSpec(memory_space=pltpu.SMEM)] + [in_vmem] * 4,
        out_specs=(in_vmem,) * 4,
        scratch_shapes=[
            pltpu.VMEM((length, head_size), jnp.bfloat16),
            pltpu.VMEM((length, head_size), jnp.bfloat16),
            pltpu.VMEM((length, head_size), jnp.float32),
            pltpu.VMEM((length, head_size), jnp.float32),
            pltpu.VMEM((most_chunks, KEY_CHUNK, columns), jnp.float32),
            pltpu.VMEM((head_size, columns), jnp.bfloat16),
            pltpu.VMEM((head_size, columns), jnp.bfloat16),
            pltpu.VMEM((columns, head_size), jnp.bfloat16),
            pltpu.VMEM((columns, head_size), jnp.bfloat16),
        ],
        compiler_params=pltpu.CompilerParams(vmem_limit_bytes=40 << 20),
        cost_estimate=pl.CostEstimate(
            flops=14 * rows * heads * visible * head_size,
            bytes_accessed=8 * rows * width + 8 * length * head_size,
            transcendentals=rows * heads * visible,
        ),
        name="masked_attention",
    )(meta, queries, cotangent, kv_same, kv_other)


def exchange_sums(row):
    tile = jnp.broadcast_to(row[None], (DEVICES, 8, row.shape[1])).reshape(-1, row.shape[1])
    everyones = lax.all_to_all(tile, AXES, split_axis=0, concat_axis=0, tiled=True)
    return jnp.sum(everyones.reshape(DEVICES, 8, row.shape[1]), axis=0)[:1]


def body(tokens, queries, cotangent, latent_key, latent_value, lengths, block_order):
    token_rows = tokens[0]
    rows_here, features = token_rows.shape
    head_size = latent_key.shape[1]
    docs, blocks = lengths.shape[1], block_order.shape[1]
    me = lax.axis_index(AXES)
    table = lax.dynamic_index_in_dim(jnp.asarray(block_table()), me, keepdims=False)
    before = np.arange(docs)[:, None] < np.arange(docs)[None, :]
    doc_starts = jnp.sum(jnp.where(before, lengths[0][:, None], 0), axis=0)
    meta = jnp.concatenate(
        [
            doc_starts.astype(jnp.int32),
            block_order[0],
            jnp.stack([lax.axis_index(CTX), lax.axis_index("core")]).astype(jnp.int32),
        ]
    )

    lane = lax.broadcasted_iota(jnp.int32, (1, 128), 1)
    sums = exchange_sums(
        jnp.where(
            lane == 0,
            jnp.sum(jnp.abs(latent_key)),
            jnp.where(lane == 1, jnp.sum(jnp.abs(latent_value)), 0.0),
        )
    )
    entry_count = features * head_size
    key_scale = sums[0, 0] / entry_count + EPSILON
    value_scale = sums[0, 1] / entry_count + EPSILON
    weights = jnp.concatenate(
        [
            (key_scale * levels(latent_key / key_scale)).astype(jnp.bfloat16),
            (value_scale * levels(latent_value / value_scale)).astype(jnp.bfloat16),
        ],
        axis=1,
    )

    tokens_own, tokens_other = shuffle(table, token_rows)
    tokens_peer = swap_cores(tokens_other)
    for phase in range(2):
        weights = jnp.concatenate(gather_ring(weights, phase), axis=0)
    weight_parts = gather_ring(weights, 2)
    part_rows = weights.shape[0]

    def project(rows):
        total = 0.0
        for i, part in enumerate(weight_parts):
            total = total + jnp.dot(
                rows[:, i * part_rows : (i + 1) * part_rows],
                part,
                preferred_element_type=jnp.float32,
            )
        return total

    peers_share = swap_cores(project(tokens_peer))
    kv_here = (project(tokens_own) + peers_share).astype(jnp.bfloat16)
    groups = lax.axis_size(SAME_CORE_CTX)
    kv_same = lax.all_to_all(
        jnp.broadcast_to(kv_here[None], (groups,) + kv_here.shape).reshape(-1, 2 * head_size),
        SAME_CORE_CTX,
        split_axis=0,
        concat_axis=0,
        tiled=True,
    )
    kv_other = swap_cores(kv_same)
    other_parts = [swap_cores(part) for part in weight_parts]

    mixed, query_grad, same_terms, other_terms = attention(
        meta, queries[0], cotangent[0], kv_same, kv_other, head_size, docs, blocks
    )
    chip_terms = (same_terms + swap_cores(other_terms).astype(jnp.float32)).astype(jnp.bfloat16)
    terms = lax.all_to_all(chip_terms, SAME_CORE_CTX, split_axis=0, concat_axis=0, tiled=True)
    grads = jnp.sum(
        terms.reshape(groups, rows_here, 2 * head_size).astype(jnp.float32), axis=0
    ).astype(jnp.bfloat16)
    peer_grads = swap_cores(grads)

    def weight_term(i):
        cut = slice(i * part_rows, (i + 1) * part_rows)
        return sum(
            lax.dot_general(
                rows[:, cut], g, (((0,), (0,)), ((), ())), preferred_element_type=jnp.float32
            )
            for rows, g in ((tokens_own, grads), (tokens_peer, peer_grads))
        )

    summed = reduce_ring([weight_term(i) for i in range(4)], 2)
    token_grad = token_gradient(table, grads, weight_parts + other_parts)
    for phase in (1, 0):
        summed = reduce_ring(jnp.split(summed, 4, axis=0), phase)
    return (
        mixed[None],
        query_grad[None],
        token_grad[None],
        summed[:, :head_size],
        summed[:, head_size:],
    )


def solution(mesh):
    torus = Mesh(mesh.devices.reshape(SIZES), AXES)
    whole = CTX + DP
    in_specs = (
        P(DP, CTX, None),
        P(DP, CTX, None),
        P(DP, CTX, None),
        P(whole, None),
        P(whole, None),
        P(DP, None),
        P(DP, None),
    )
    out_specs = (
        P(DP, CTX, None),
        P(DP, CTX, None),
        P(DP, CTX, None),
        P(whole, None),
        P(whole, None),
    )
    return jax.shard_map(body, mesh=torus, in_specs=in_specs, out_specs=out_specs, check_vma=False)
```

```python
import functools

import jax
import jax.numpy as jnp
import numpy as np
from jax import lax
from jax.experimental import pallas as pl
from jax.experimental.pallas import tpu as pltpu
from jax.sharding import Mesh
from jax.sharding import PartitionSpec as P

AXES = ("y", "zh", "core", "x", "zl")
SIZES = (4, 2, 2, 4, 2)
CTX = ("y", "zh", "core")
DP = ("x", "zl")
SAME_CORE_CTX = ("y", "zh")
DEVICES = int(np.prod(SIZES))

EPSILON = 1e-05
NEGATIVE = -1e30
KEY_CHUNK = 256

RING_ORDER = {0: ("x", "y", "z"), 1: ("y", "z", "x")}
OFFSETS = (0, -1, 1, 2)


def coordinates(device):
    y, zh, core, x, zl = (int(v) for v in np.unravel_index(device, SIZES))
    return {"y": y, "z": zh * 2 + zl, "x": x, "core": core}


def device_of(place):
    return int(
        np.ravel_multi_index(
            (place["y"], place["z"] // 2, place["core"], place["x"], place["z"] % 2), SIZES
        )
    )


def moved(change):
    pairs = []
    for device in range(DEVICES):
        place = coordinates(device)
        change(place)
        pairs.append((device, device_of(place)))
    return pairs


def along_ring(phase, step):
    def change(place):
        axis = RING_ORDER[place["core"]][phase]
        place[axis] = (place[axis] + step) % 4

    return moved(change)


def to_other_core(place):
    place["core"] = 1 - place["core"]


def swap_cores(value):
    return lax.ppermute(value, AXES, moved(to_other_core))


def block_table():
    table = np.zeros((DEVICES, DEVICES), np.int32)
    for device in range(DEVICES):
        here = coordinates(device)
        at = 0
        for core in (here["core"], 1 - here["core"]):
            order = RING_ORDER[core]
            for last in OFFSETS:
                for middle in OFFSETS:
                    for first in OFFSETS:
                        place = dict(here, core=core)
                        for axis, step in zip(order, (first, middle, last)):
                            place[axis] = (place[axis] + step) % 4
                        table[device, at] = device_of(place)
                        at += 1
    return table


def gather_ring(value, phase):
    return [value] + [
        lax.ppermute(value, AXES, along_ring(phase, -offset)) for offset in OFFSETS[1:]
    ]


def reduce_ring(pieces, phase):
    total = pieces[0]
    for piece, offset in zip(pieces[1:], OFFSETS[1:]):
        sent = lax.ppermute(piece.astype(jnp.bfloat16), AXES, along_ring(phase, offset))
        total = total + sent.astype(jnp.float32)
    return total


def levels(ratio):
    return jnp.where(ratio >= 0.5, 1.0, jnp.where(ratio <= -0.5, -1.0, 0.0)).astype(jnp.float32)


def shuffle_kernel(table, tokens, own, other):
    width = own.shape[1] * 2 // DEVICES
    half = DEVICES // 2

    def move(j, _):
        target = pl.ds(pl.multiple_of(j * width, width), width)
        for first, out in ((0, own), (half, other)):
            source = pl.ds(pl.multiple_of(table[first + j] * width, width), width)
            out[:, target] = tokens[:, source]
        return 0

    lax.fori_loop(0, half, move, 0, unroll=8)


def shuffle(table, tokens):
    rows, features = tokens.shape
    step_rows = 32
    half = jax.ShapeDtypeStruct((rows, features // 2), tokens.dtype)
    half_spec = pl.BlockSpec((step_rows, features // 2), lambda i: (i, 0))
    return pl.pallas_call(
        shuffle_kernel,
        grid=(rows // step_rows,),
        out_shape=(half, half),
        in_specs=[
            pl.BlockSpec(memory_space=pltpu.SMEM),
            pl.BlockSpec((step_rows, features), lambda i: (i, 0)),
        ],
        out_specs=(half_spec, half_spec),
        compiler_params=pltpu.CompilerParams(vmem_limit_bytes=16 << 20),
        cost_estimate=pl.CostEstimate(
            flops=0, bytes_accessed=4 * rows * features, transcendentals=0
        ),
        name="shuffle_tokens",
    )(table, tokens)


def token_grad_kernel(table, grads, *rest, count):
    weights, out = rest[:count], rest[count]
    buffers, sems = rest[count + 1 :]
    rows, step_width = buffers.shape[1:]
    width = out.shape[1] // DEVICES
    per_step = step_width // width
    steps_each = weights[0].shape[0] // step_width
    for step in range(count * steps_each):
        slot = step % 2
        buffer, sem = buffers.at[slot], sems.at[slot]
        if step >= 2:
            pltpu.make_async_copy(buffer, buffer, sem).wait()
        part = (step % steps_each) * step_width
        buffers[slot] = lax.dot_general(
            grads[...],
            weights[step // steps_each][part : part + step_width, :],
            (((1,), (1,)), ((), ())),
            preferred_element_type=jnp.float32,
        ).astype(jnp.bfloat16)
        for j in range(per_step):
            target = pl.ds(pl.multiple_of(table[step * per_step + j] * width, width), width)
            pltpu.make_async_copy(
                buffer.at[:, j * width : (j + 1) * width], out.at[:, target], sem
            ).start()
    for slot in range(2):
        pltpu.make_async_copy(buffers.at[slot], buffers.at[slot], sems.at[slot]).wait()


def token_gradient(table, grads, weights):
    rows, both = grads.shape
    features = sum(w.shape[0] for w in weights)
    step_width = 1024
    in_vmem = pl.BlockSpec(memory_space=pltpu.VMEM)
    return pl.pallas_call(
        functools.partial(token_grad_kernel, count=len(weights)),
        out_shape=jax.ShapeDtypeStruct((rows, features), jnp.bfloat16),
        in_specs=[pl.BlockSpec(memory_space=pltpu.SMEM)] + [in_vmem] * (1 + len(weights)),
        out_specs=pl.BlockSpec(memory_space=pl.ANY),
        scratch_shapes=[
            pltpu.VMEM((2, rows, step_width), jnp.bfloat16),
            pltpu.SemaphoreType.DMA((2,)),
        ],
        compiler_params=pltpu.CompilerParams(vmem_limit_bytes=32 << 20),
        cost_estimate=pl.CostEstimate(
            flops=2 * rows * both * features,
            bytes_accessed=2 * features * (rows + both),
            transcendentals=0,
        ),
        name="token_gradient",
    )(table, grads, *weights)


def attention_kernel(
    meta, queries, cotangent, kv_same, kv_other, mixed_out, query_grad, same_out, other_out,
    keys, values, key_acc, value_acc, scores, q_columns, c_columns, q_rows, c_rows,
    *, heads, head_size, block, docs, blocks,
):
    scale = head_size ** (-0.5)
    columns = heads * block
    ctx, core = meta[docs + blocks], meta[docs + blocks + 1]
    sides = ((kv_same, core, same_out), (kv_other, 1 - core, other_out))

    def rows_at(index, size):
        return pl.ds(pl.multiple_of(index * size, size), size)

    def true_block(core_of, j):
        return meta[docs + ((j // 2) * 2 + core_of) * 2 + j % 2]

    for ref, core_of, _ in sides:
        for j in range(blocks // 2):
            target = rows_at(true_block(core_of, j), block)
            keys[target, :] = ref[j * block : (j + 1) * block, :head_size]
            values[target, :] = ref[j * block : (j + 1) * block, head_size:]
    key_acc[...] = jnp.zeros_like(key_acc)
    value_acc[...] = jnp.zeros_like(value_acc)

    def one_block(i, _):
        here = rows_at(i, block)
        for h in range(heads):
            head = slice(h * head_size, (h + 1) * head_size)
            part = slice(h * block, (h + 1) * block)
            q, c = queries[here, head], cotangent[here, head]
            q_rows[part, :], c_rows[part, :] = q, c
            q_columns[:, part], c_columns[:, part] = q.T, c.T
        start = meta[docs + 2 * ctx + i] * block
        position = start + lax.rem(lax.broadcasted_iota(jnp.int32, (1, columns), 1), block)
        own_start = jnp.zeros((1, columns), jnp.int32)
        first = jnp.int32(0)
        for d in range(docs):
            doc_start = meta[d]
            own_start = jnp.maximum(own_start, jnp.where(position >= doc_start, doc_start, 0))
            first = jnp.maximum(first, jnp.where(start >= doc_start, doc_start, 0))
        lowest = first // KEY_CHUNK
        count = (start + block - 1) // KEY_CHUNK - lowest + 1

        def score(c, best):
            s = scale * jnp.dot(
                keys[rows_at(lowest + c, KEY_CHUNK), :],
                q_columns[...],
                preferred_element_type=jnp.float32,
            )
            key_pos = (lowest + c) * KEY_CHUNK + lax.broadcasted_iota(
                jnp.int32, (KEY_CHUNK, columns), 0
            )
            s = jnp.where((key_pos >= own_start) & (key_pos <= position), s, NEGATIVE)
            scores[c] = s
            return jnp.maximum(best, jnp.max(s.reshape(KEY_CHUNK // 8, 8, columns), axis=0))

        best = lax.fori_loop(
            0, count, score, jnp.full((8, columns), NEGATIVE, jnp.float32)
        )
        best = jnp.max(best, axis=0, keepdims=True)

        def mix(c, carried):
            total, acc = carried
            w = jnp.exp(scores[c] - best)
            scores[c] = w
            total = total + jnp.sum(w.reshape(KEY_CHUNK // 8, 8, columns), axis=0)
            acc = acc + lax.dot_general(
                values[rows_at(lowest + c, KEY_CHUNK), :],
                w.astype(jnp.bfloat16),
                (((0,), (0,)), ((), ())),
                preferred_element_type=jnp.float32,
            )
            return total, acc

        total, acc = lax.fori_loop(
            0,
            count,
            mix,
            (jnp.zeros((8, columns), jnp.float32), jnp.zeros((head_size, columns), jnp.float32)),
        )
        total = jnp.sum(total, axis=0, keepdims=True)
        mixed = (acc / total).astype(jnp.bfloat16)
        expected = jnp.sum(
            mixed.astype(jnp.float32) * c_columns[...].astype(jnp.float32), axis=0, keepdims=True
        )
        per_total = 1.0 / total
        for h in range(heads):
            mixed_out[here, h * head_size : (h + 1) * head_size] = mixed[
                :, h * block : (h + 1) * block
            ].T

        def back(c, q_acc):
            at = rows_at(lowest + c, KEY_CHUNK)
            probability = scores[c] * per_total
            prob_grad = jnp.dot(values[at, :], c_columns[...], preferred_element_type=jnp.float32)
            score_grad = (probability * (prob_grad - expected)).astype(jnp.bfloat16)
            key_acc[at, :] += jnp.dot(score_grad, q_rows[...], preferred_element_type=jnp.float32)
            value_acc[at, :] += jnp.dot(
                probability.astype(jnp.bfloat16), c_rows[...], preferred_element_type=jnp.float32
            )
            return q_acc + lax.dot_general(
                keys[at, :],
                score_grad,
                (((0,), (0,)), ((), ())),
                preferred_element_type=jnp.float32,
            )

        q_acc = lax.fori_loop(
            0, count, back, jnp.zeros((head_size, columns), jnp.float32)
        )
        q_grad = (q_acc * scale).astype(jnp.bfloat16)
        for h in range(heads):
            query_grad[here, h * head_size : (h + 1) * head_size] = q_grad[
                :, h * block : (h + 1) * block
            ].T
        return 0

    lax.fori_loop(0, queries.shape[0] // block, one_block, 0)
    for _, core_of, out in sides:
        for j in range(blocks // 2):
            source = rows_at(true_block(core_of, j), block)
            part = slice(j * block, (j + 1) * block)
            out[part, :head_size] = (key_acc[source, :] * scale).astype(out.dtype)
            out[part, head_size:] = value_acc[source, :].astype(out.dtype)


def attention(meta, queries, cotangent, kv_same, kv_other, head_size, docs, blocks):
    rows, width = queries.shape
    heads = width // head_size
    length = kv_same.shape[0] + kv_other.shape[0]
    block = length // blocks
    columns = heads * block
    in_vmem = pl.BlockSpec(memory_space=pltpu.VMEM)
    most_chunks = 10
    visible = 9 * KEY_CHUNK
    return pl.pallas_call(
        functools.partial(
            attention_kernel, heads=heads, head_size=head_size, block=block, docs=docs, blocks=blocks
        ),
        out_shape=(
            jax.ShapeDtypeStruct((rows, width), jnp.bfloat16),
            jax.ShapeDtypeStruct((rows, width), jnp.bfloat16),
            jax.ShapeDtypeStruct(kv_same.shape, jnp.float32),
            jax.ShapeDtypeStruct(kv_other.shape, jnp.bfloat16),
        ),
        in_specs=[pl.BlockSpec(memory_space=pltpu.SMEM)] + [in_vmem] * 4,
        out_specs=(in_vmem,) * 4,
        scratch_shapes=[
            pltpu.VMEM((length, head_size), jnp.bfloat16),
            pltpu.VMEM((length, head_size), jnp.bfloat16),
            pltpu.VMEM((length, head_size), jnp.float32),
            pltpu.VMEM((length, head_size), jnp.float32),
            pltpu.VMEM((most_chunks, KEY_CHUNK, columns), jnp.float32),
            pltpu.VMEM((head_size, columns), jnp.bfloat16),
            pltpu.VMEM((head_size, columns), jnp.bfloat16),
            pltpu.VMEM((columns, head_size), jnp.bfloat16),
            pltpu.VMEM((columns, head_size), jnp.bfloat16),
        ],
        compiler_params=pltpu.CompilerParams(vmem_limit_bytes=40 << 20),
        cost_estimate=pl.CostEstimate(
            flops=14 * rows * heads * visible * head_size,
            bytes_accessed=8 * rows * width + 8 * length * head_size,
            transcendentals=rows * heads * visible,
        ),
        name="masked_attention",
    )(meta, queries, cotangent, kv_same, kv_other)


def exchange_sums(row):
    tile = jnp.broadcast_to(row[None], (DEVICES, 8, row.shape[1])).reshape(-1, row.shape[1])
    everyones = lax.all_to_all(tile, AXES, split_axis=0, concat_axis=0, tiled=True)
    return jnp.sum(everyones.reshape(DEVICES, 8, row.shape[1]), axis=0)[:1]


def body(tokens, queries, cotangent, latent_key, latent_value, lengths, block_order):
    token_rows = tokens[0]
    rows_here, features = token_rows.shape
    head_size = latent_key.shape[1]
    docs, blocks = lengths.shape[1], block_order.shape[1]
    me = lax.axis_index(AXES)
    table = lax.dynamic_index_in_dim(jnp.asarray(block_table()), me, keepdims=False)
    before = np.arange(docs)[:, None] < np.arange(docs)[None, :]
    doc_starts = jnp.sum(jnp.where(before, lengths[0][:, None], 0), axis=0)
    meta = jnp.concatenate(
        [
            doc_starts.astype(jnp.int32),
            block_order[0],
            jnp.stack([lax.axis_index(CTX), lax.axis_index("core")]).astype(jnp.int32),
        ]
    )

    lane = lax.broadcasted_iota(jnp.int32, (1, 128), 1)
    row = jnp.where(
        lane == 0,
        jnp.sum(jnp.abs(latent_key)),
        jnp.where(lane == 1, jnp.sum(jnp.abs(latent_value)), 0.0),
    )
    row, shuffle_table = lax.optimization_barrier((row, table))
    sums = exchange_sums(row)
    tokens_own, tokens_other = shuffle(shuffle_table, token_rows)
    sums, tokens_own, tokens_other = lax.optimization_barrier((sums, tokens_own, tokens_other))
    tokens_peer = swap_cores(tokens_other)
    entry_count = features * head_size
    key_scale = sums[0, 0] / entry_count + EPSILON
    value_scale = sums[0, 1] / entry_count + EPSILON
    weights = jnp.concatenate(
        [
            (key_scale * levels(latent_key / key_scale)).astype(jnp.bfloat16),
            (value_scale * levels(latent_value / value_scale)).astype(jnp.bfloat16),
        ],
        axis=1,
    )

    for phase in range(2):
        weights = jnp.concatenate(gather_ring(weights, phase), axis=0)
    weight_parts = gather_ring(weights, 2)
    part_rows = weights.shape[0]

    def project(rows):
        total = 0.0
        for i, part in enumerate(weight_parts):
            total = total + jnp.dot(
                rows[:, i * part_rows : (i + 1) * part_rows],
                part,
                preferred_element_type=jnp.float32,
            )
        return total

    peers_share = swap_cores(project(tokens_peer))
    kv_here = (project(tokens_own) + peers_share).astype(jnp.bfloat16)
    groups = lax.axis_size(SAME_CORE_CTX)
    kv_same = lax.all_to_all(
        jnp.broadcast_to(kv_here[None], (groups,) + kv_here.shape).reshape(-1, 2 * head_size),
        SAME_CORE_CTX,
        split_axis=0,
        concat_axis=0,
        tiled=True,
    )
    kv_other = swap_cores(kv_same)
    other_parts = [swap_cores(part) for part in weight_parts]

    mixed, query_grad, same_terms, other_terms = attention(
        meta, queries[0], cotangent[0], kv_same, kv_other, head_size, docs, blocks
    )
    same_terms, other_terms, *other_parts = lax.optimization_barrier(
        (same_terms, other_terms, *other_parts)
    )
    chip_terms = (same_terms + swap_cores(other_terms).astype(jnp.float32)).astype(jnp.bfloat16)
    terms = lax.all_to_all(chip_terms, SAME_CORE_CTX, split_axis=0, concat_axis=0, tiled=True)
    grads = jnp.sum(
        terms.reshape(groups, rows_here, 2 * head_size).astype(jnp.float32), axis=0
    ).astype(jnp.bfloat16)
    peer_grads = swap_cores(grads)

    def weight_term(i):
        cut = slice(i * part_rows, (i + 1) * part_rows)
        return sum(
            lax.dot_general(
                g, rows[:, cut], (((0,), (0,)), ((), ())), preferred_element_type=jnp.float32
            )
            for rows, g in ((tokens_own, grads), (tokens_peer, peer_grads))
        )

    summed = reduce_ring([weight_term(i) for i in range(4)], 2)
    token_grad = token_gradient(table, grads, weight_parts + other_parts)
    summed, token_grad = lax.optimization_barrier((summed, token_grad))
    for phase in (1, 0):
        summed = reduce_ring(jnp.split(summed, 4, axis=1), phase)
    summed = summed.T
    return (
        mixed[None],
        query_grad[None],
        token_grad[None],
        summed[:, :head_size],
        summed[:, head_size:],
    )


def solution(mesh):
    torus = Mesh(mesh.devices.reshape(SIZES), AXES)
    whole = CTX + DP
    in_specs = (
        P(DP, CTX, None),
        P(DP, CTX, None),
        P(DP, CTX, None),
        P(whole, None),
        P(whole, None),
        P(DP, None),
        P(DP, None),
    )
    out_specs = (
        P(DP, CTX, None),
        P(DP, CTX, None),
        P(DP, CTX, None),
        P(whole, None),
        P(whole, None),
    )
    return jax.shard_map(body, mesh=torus, in_specs=in_specs, out_specs=out_specs, check_vma=False)
```

```python
import functools

import jax
import jax.numpy as jnp
import numpy as np
from jax import lax
from jax.experimental import pallas as pl
from jax.experimental.pallas import tpu as pltpu
from jax.sharding import Mesh
from jax.sharding import PartitionSpec as P

AXES = ("y", "zh", "core", "x", "zl")
SIZES = (4, 2, 2, 4, 2)
CTX = ("y", "zh", "core")
DP = ("x", "zl")
SAME_CORE_CTX = ("y", "zh")
DEVICES = int(np.prod(SIZES))

EPSILON = 1e-05
NEGATIVE = -1e30
KEY_CHUNK = 256
STRIP = 32

RING_ORDER = {0: ("x", "y", "z"), 1: ("y", "z", "x")}
OFFSETS = (0, -1, 1, 2)


def coordinates(device):
    y, zh, core, x, zl = (int(v) for v in np.unravel_index(device, SIZES))
    return {"y": y, "z": zh * 2 + zl, "x": x, "core": core}


def device_of(place):
    return int(
        np.ravel_multi_index(
            (place["y"], place["z"] // 2, place["core"], place["x"], place["z"] % 2), SIZES
        )
    )


def moved(change):
    pairs = []
    for device in range(DEVICES):
        place = coordinates(device)
        change(place)
        pairs.append((device, device_of(place)))
    return pairs


def along_ring(phase, step):
    def change(place):
        axis = RING_ORDER[place["core"]][phase]
        place[axis] = (place[axis] + step) % 4

    return moved(change)


def to_other_core(place):
    place["core"] = 1 - place["core"]


def swap_cores(value):
    return lax.ppermute(value, AXES, moved(to_other_core))


def block_table():
    table = np.zeros((DEVICES, DEVICES), np.int32)
    for device in range(DEVICES):
        here = coordinates(device)
        at = 0
        for core in (here["core"], 1 - here["core"]):
            order = RING_ORDER[core]
            for last in OFFSETS:
                for middle in OFFSETS:
                    for first in OFFSETS:
                        place = dict(here, core=core)
                        for axis, step in zip(order, (first, middle, last)):
                            place[axis] = (place[axis] + step) % 4
                        table[device, at] = device_of(place)
                        at += 1
    return table


def gather_ring(value, phase):
    return [value] + [
        lax.ppermute(value, AXES, along_ring(phase, -offset)) for offset in OFFSETS[1:]
    ]


def reduce_ring(pieces, phase):
    total = pieces[0]
    for piece, offset in zip(pieces[1:], OFFSETS[1:]):
        sent = lax.ppermute(piece.astype(jnp.bfloat16), AXES, along_ring(phase, offset))
        total = total + sent.astype(jnp.float32)
    return total


def levels(ratio):
    return jnp.where(ratio >= 0.5, 1.0, jnp.where(ratio <= -0.5, -1.0, 0.0)).astype(jnp.float32)


def shuffle_kernel(table, tokens, own, other):
    width = own.shape[1] * 2 // DEVICES
    half = DEVICES // 2

    def move(j, _):
        target = pl.ds(pl.multiple_of(j * width, width), width)
        for first, out in ((0, own), (half, other)):
            source = pl.ds(pl.multiple_of(table[first + j] * width, width), width)
            out[:, target] = tokens[:, source]
        return 0

    lax.fori_loop(0, half, move, 0, unroll=8)


def shuffle(table, tokens):
    rows, features = tokens.shape
    step_rows = 32
    half = jax.ShapeDtypeStruct((rows, features // 2), tokens.dtype)
    half_spec = pl.BlockSpec((step_rows, features // 2), lambda i: (i, 0))
    return pl.pallas_call(
        shuffle_kernel,
        grid=(rows // step_rows,),
        out_shape=(half, half),
        in_specs=[
            pl.BlockSpec(memory_space=pltpu.SMEM),
            pl.BlockSpec((step_rows, features), lambda i: (i, 0)),
        ],
        out_specs=(half_spec, half_spec),
        compiler_params=pltpu.CompilerParams(vmem_limit_bytes=56 << 20),
        cost_estimate=pl.CostEstimate(
            flops=0, bytes_accessed=4 * rows * features, transcendentals=0
        ),
        name="shuffle_tokens",
    )(table, tokens)


def token_grad_kernel(table, grads, *rest, count):
    weights, out = rest[:count], rest[count]
    buffers, sems = rest[count + 1 :]
    rows, step_width = buffers.shape[1:]
    width = out.shape[1] // DEVICES
    per_step = step_width // width
    steps_each = weights[0].shape[0] // step_width
    for step in range(count * steps_each):
        slot = step % 2
        buffer, sem = buffers.at[slot], sems.at[slot]
        if step >= 2:
            pltpu.make_async_copy(buffer, buffer, sem).wait()
        part = (step % steps_each) * step_width
        buffers[slot] = lax.dot_general(
            grads[...],
            weights[step // steps_each][part : part + step_width, :],
            (((1,), (1,)), ((), ())),
            preferred_element_type=jnp.float32,
        ).astype(jnp.bfloat16)
        for j in range(per_step):
            target = pl.ds(pl.multiple_of(table[step * per_step + j] * width, width), width)
            pltpu.make_async_copy(
                buffer.at[:, j * width : (j + 1) * width], out.at[:, target], sem
            ).start()
    for slot in range(2):
        pltpu.make_async_copy(buffers.at[slot], buffers.at[slot], sems.at[slot]).wait()


def token_gradient(table, grads, weights):
    rows, both = grads.shape
    features = sum(w.shape[0] for w in weights)
    step_width = 1024
    in_vmem = pl.BlockSpec(memory_space=pltpu.VMEM)
    return pl.pallas_call(
        functools.partial(token_grad_kernel, count=len(weights)),
        out_shape=jax.ShapeDtypeStruct((rows, features), jnp.bfloat16),
        in_specs=[pl.BlockSpec(memory_space=pltpu.SMEM)] + [in_vmem] * (1 + len(weights)),
        out_specs=pl.BlockSpec(memory_space=pl.ANY),
        scratch_shapes=[
            pltpu.VMEM((2, rows, step_width), jnp.bfloat16),
            pltpu.SemaphoreType.DMA((2,)),
        ],
        compiler_params=pltpu.CompilerParams(vmem_limit_bytes=32 << 20),
        cost_estimate=pl.CostEstimate(
            flops=2 * rows * both * features,
            bytes_accessed=2 * features * (rows + both),
            transcendentals=0,
        ),
        name="token_gradient",
    )(table, grads, *weights)


def attention_kernel(
    meta, queries, cotangent, peer_both, kv_same, kv_other,
    mixed_out, query_grad, same_out, other_out,
    q_held, c_held, peer_held, kv_held, key_acc, value_acc, scores, prob_grad, low,
    q_columns, c_columns, q_rows, c_rows, sems,
    *, heads, head_size, block, docs, blocks,
):
    scale = head_size ** (-0.5)
    columns = heads * block
    ctx, core = meta[docs + blocks], meta[docs + blocks + 1]
    own_blocks = q_held.shape[0] // block
    in_strip = lax.broadcasted_iota(jnp.int32, (STRIP, columns), 0)
    sides = ((kv_same, core, same_out), (kv_other, 1 - core, other_out))

    def rows_at(index, size):
        return pl.ds(pl.multiple_of(index * size, size), size)

    def true_block(core_of, j):
        return meta[docs + ((j // 2) * 2 + core_of) * 2 + j % 2]

    copies = [
        pltpu.make_async_copy(source, held, sems.at[n])
        for n, (source, held) in enumerate(
            ((queries, q_held), (cotangent, c_held), (peer_both, peer_held))
        )
    ]
    for copy in copies:
        copy.start()
    for n, (ref, core_of, _) in enumerate(sides):
        for j in range(blocks // 2):
            pltpu.make_async_copy(
                ref.at[j * block : (j + 1) * block, :],
                kv_held.at[rows_at(true_block(core_of, j), block), :],
                sems.at[len(copies) + n],
            ).start()
    key_acc[...] = jnp.zeros_like(key_acc)
    value_acc[...] = jnp.zeros_like(value_acc)
    for copy in copies:
        copy.wait()
    for i in range(2 * own_blocks):
        here = slice(i % own_blocks * block, (i % own_blocks + 1) * block)
        for h in range(heads):
            part = slice(h * block, (h + 1) * block)
            if i < own_blocks:
                head = rows_at(core * heads + h, head_size)
                q, c = q_held[here, head], c_held[here, head]
            else:
                q = peer_held[here, h * head_size : (h + 1) * head_size]
                c = peer_held[here, (heads + h) * head_size : (heads + h + 1) * head_size]
            q_rows[i, part, :], c_rows[i, part, :] = q, c
            q_columns[i, :, part], c_columns[i, :, part] = q.T, c.T
    for n, (ref, _, _) in enumerate(sides):
        pltpu.make_async_copy(
            ref, kv_held.at[: blocks // 2 * block, :], sems.at[len(copies) + n]
        ).wait()

    def keys_at(chunk):
        return kv_held[rows_at(chunk, KEY_CHUNK), :head_size]

    def values_at(chunk):
        return kv_held[rows_at(chunk, KEY_CHUNK), head_size:]

    def one_block(i, _):
        here = rows_at(i, block)
        ctx_of = jnp.where(i < own_blocks, ctx, ctx + 1 - 2 * core)
        start = meta[docs + own_blocks * ctx_of + lax.rem(i, own_blocks)] * block
        position = start + lax.rem(lax.broadcasted_iota(jnp.int32, (1, columns), 1), block)
        own_start = jnp.zeros((1, columns), jnp.int32)
        first = jnp.int32(0)
        for d in range(docs):
            doc_start = meta[d]
            own_start = jnp.maximum(own_start, jnp.where(position >= doc_start, doc_start, 0))
            first = jnp.maximum(first, jnp.where(start >= doc_start, doc_start, 0))
        lowest = first // KEY_CHUNK
        count = (start + block - 1) // KEY_CHUNK - lowest + 1

        def score(c, best):
            scores[c] = jnp.dot(
                keys_at(lowest + c),
                q_columns[i],
                preferred_element_type=jnp.float32,
            )
            first_key = (lowest + c) * KEY_CHUNK
            for at in range(0, KEY_CHUNK, STRIP):
                strip = slice(at, at + STRIP)
                key_pos = first_key + at + in_strip
                visible = (key_pos >= own_start) & (key_pos <= position)
                s = jnp.where(visible, scores[c, strip, :] * scale, NEGATIVE)
                scores[c, strip, :] = s
                best = jnp.maximum(best, jnp.max(s.reshape(STRIP // 8, 8, columns), axis=0))
            return best

        best = lax.fori_loop(
            0, count, score, jnp.full((8, columns), NEGATIVE, jnp.float32)
        )
        best = jnp.max(best, axis=0, keepdims=True)

        def mix(c, carried):
            total, acc = carried
            for at in range(0, KEY_CHUNK, STRIP):
                strip = slice(at, at + STRIP)
                w = jnp.exp(scores[c, strip, :] - best)
                scores[c, strip, :] = w
                low[0, strip, :] = w.astype(jnp.bfloat16)
                total = total + jnp.sum(w.reshape(STRIP // 8, 8, columns), axis=0)
            acc = acc + lax.dot_general(
                values_at(lowest + c),
                low[0],
                (((0,), (0,)), ((), ())),
                preferred_element_type=jnp.float32,
            )
            return total, acc

        total, acc = lax.fori_loop(
            0,
            count,
            mix,
            (jnp.zeros((8, columns), jnp.float32), jnp.zeros((head_size, columns), jnp.float32)),
        )
        total = jnp.sum(total, axis=0, keepdims=True)
        mixed = (acc / total).astype(jnp.bfloat16)
        expected = jnp.sum(
            mixed.astype(jnp.float32) * c_columns[i].astype(jnp.float32), axis=0, keepdims=True
        )
        per_total = 1.0 / total
        for h in range(heads):
            mixed_out[here, h * head_size : (h + 1) * head_size] = mixed[
                :, h * block : (h + 1) * block
            ].T

        def back(c, q_acc):
            chunk = rows_at(lowest + c, KEY_CHUNK)
            prob_grad[...] = jnp.dot(
                values_at(lowest + c), c_columns[i], preferred_element_type=jnp.float32
            )
            for at in range(0, KEY_CHUNK, STRIP):
                strip = slice(at, at + STRIP)
                probability = scores[c, strip, :] * per_total
                low[0, strip, :] = probability.astype(jnp.bfloat16)
                low[1, strip, :] = (probability * (prob_grad[strip, :] - expected)).astype(
                    jnp.bfloat16
                )
            value_acc[chunk, :] += jnp.dot(low[0], c_rows[i], preferred_element_type=jnp.float32)
            key_acc[chunk, :] += jnp.dot(low[1], q_rows[i], preferred_element_type=jnp.float32)
            return q_acc + lax.dot_general(
                keys_at(lowest + c),
                low[1],
                (((0,), (0,)), ((), ())),
                preferred_element_type=jnp.float32,
            )

        q_acc = lax.fori_loop(
            0, count, back, jnp.zeros((head_size, columns), jnp.float32)
        )
        q_grad = (q_acc * scale).astype(jnp.bfloat16)
        for h in range(heads):
            query_grad[here, h * head_size : (h + 1) * head_size] = q_grad[
                :, h * block : (h + 1) * block
            ].T
        return 0

    lax.fori_loop(0, 2 * own_blocks, one_block, 0)
    for _, core_of, out in sides:
        for j in range(blocks // 2):
            source = rows_at(true_block(core_of, j), block)
            part = slice(j * block, (j + 1) * block)
            out[part, :head_size] = (key_acc[source, :] * scale).astype(out.dtype)
            out[part, head_size:] = value_acc[source, :].astype(out.dtype)


def attention(meta, queries, cotangent, peer_both, kv_same, kv_other, head_size, docs, blocks):
    rows, width = queries.shape
    heads = width // head_size // 2
    length = kv_same.shape[0] + kv_other.shape[0]
    block = length // blocks
    columns = heads * block
    query_blocks = 2 * rows // block
    in_vmem = pl.BlockSpec(memory_space=pltpu.VMEM)
    most_chunks = 10
    visible = 9 * KEY_CHUNK
    return pl.pallas_call(
        functools.partial(
            attention_kernel, heads=heads, head_size=head_size, block=block, docs=docs, blocks=blocks
        ),
        out_shape=(
            jax.ShapeDtypeStruct((2 * rows, width // 2), jnp.bfloat16),
            jax.ShapeDtypeStruct((2 * rows, width // 2), jnp.bfloat16),
            jax.ShapeDtypeStruct(kv_same.shape, jnp.float32),
            jax.ShapeDtypeStruct(kv_other.shape, jnp.bfloat16),
        ),
        in_specs=[pl.BlockSpec(memory_space=pltpu.SMEM)] + [pl.BlockSpec(memory_space=pl.ANY)] * 5,
        out_specs=(in_vmem,) * 4,
        scratch_shapes=[
            pltpu.VMEM(queries.shape, jnp.bfloat16),
            pltpu.VMEM(cotangent.shape, jnp.bfloat16),
            pltpu.VMEM(peer_both.shape, jnp.bfloat16),
            pltpu.VMEM((length, 2 * head_size), jnp.bfloat16),
            pltpu.VMEM((length, head_size), jnp.float32),
            pltpu.VMEM((length, head_size), jnp.float32),
            pltpu.VMEM((most_chunks, KEY_CHUNK, columns), jnp.float32),
            pltpu.VMEM((KEY_CHUNK, columns), jnp.float32),
            pltpu.VMEM((2, KEY_CHUNK, columns), jnp.bfloat16),
            pltpu.VMEM((query_blocks, head_size, columns), jnp.bfloat16),
            pltpu.VMEM((query_blocks, head_size, columns), jnp.bfloat16),
            pltpu.VMEM((query_blocks, columns, head_size), jnp.bfloat16),
            pltpu.VMEM((query_blocks, columns, head_size), jnp.bfloat16),
            pltpu.SemaphoreType.DMA((5,)),
        ],
        compiler_params=pltpu.CompilerParams(vmem_limit_bytes=40 << 20),
        cost_estimate=pl.CostEstimate(
            flops=28 * rows * heads * visible * head_size,
            bytes_accessed=8 * rows * width + 8 * length * head_size,
            transcendentals=2 * rows * heads * visible,
        ),
        name="masked_attention",
    )(meta, queries, cotangent, peer_both, kv_same, kv_other)


def body(tokens, queries, cotangent, latent_key, latent_value, lengths, block_order):
    token_rows = tokens[0]
    rows_here, features = token_rows.shape
    head_size = latent_key.shape[1]
    docs, blocks = lengths.shape[1], block_order.shape[1]
    me = lax.axis_index(AXES)
    table = lax.dynamic_index_in_dim(jnp.asarray(block_table()), me, keepdims=False)
    before = np.arange(docs)[:, None] < np.arange(docs)[None, :]
    doc_starts = jnp.sum(jnp.where(before, lengths[0][:, None], 0), axis=0)
    meta = jnp.concatenate(
        [
            doc_starts.astype(jnp.int32),
            block_order[0],
            jnp.stack([lax.axis_index(CTX), lax.axis_index("core")]).astype(jnp.int32),
        ]
    )

    core = lax.axis_index("core")
    peer_both = swap_cores(
        jnp.concatenate(
            [
                lax.dynamic_slice_in_dim(a[0], (1 - core) * a.shape[2] // 2, a.shape[2] // 2, 1)
                for a in (queries, cotangent)
            ],
            axis=1,
        )
    )
    latents = jnp.concatenate([latent_key, latent_value], axis=1)
    for phase in range(2):
        latents = jnp.concatenate(gather_ring(latents, phase), axis=0)
    tokens_own, tokens_other = shuffle(table, token_rows)
    latents, tokens_own, tokens_other, peer_both, meta = lax.optimization_barrier(
        (latents, tokens_own, tokens_other, peer_both, meta)
    )
    tokens_peer = swap_cores(tokens_other)
    sums = jnp.broadcast_to(jnp.sum(jnp.abs(latents), axis=0, keepdims=True), (8, 2 * head_size))
    sums = sum(gather_ring(sums, 2))
    sums = sums + swap_cores(sums)
    entry_count = features * head_size
    key_scale = jnp.sum(sums[0, :head_size]) / entry_count + EPSILON
    value_scale = jnp.sum(sums[0, head_size:]) / entry_count + EPSILON
    weights = jnp.concatenate(
        [
            (scale * levels(latent / scale)).astype(jnp.bfloat16)
            for latent, scale in (
                (latents[:, :head_size], key_scale),
                (latents[:, head_size:], value_scale),
            )
        ],
        axis=1,
    )
    weight_parts = gather_ring(weights, 2)
    part_rows = weights.shape[0]

    def project(rows):
        total = 0.0
        for i, part in enumerate(weight_parts):
            total = total + jnp.dot(
                rows[:, i * part_rows : (i + 1) * part_rows],
                part,
                preferred_element_type=jnp.float32,
            )
        return total

    peers_share = swap_cores(project(tokens_peer))
    kv_here = (project(tokens_own) + peers_share).astype(jnp.bfloat16)
    groups = lax.axis_size(SAME_CORE_CTX)
    kv_same = lax.all_to_all(
        jnp.broadcast_to(kv_here[None], (groups,) + kv_here.shape).reshape(-1, 2 * head_size),
        SAME_CORE_CTX,
        split_axis=0,
        concat_axis=0,
        tiled=True,
    )
    kv_other = swap_cores(kv_same)
    other_parts = [swap_cores(part) for part in weight_parts]

    mixed, query_grad, same_terms, other_terms = attention(
        meta, queries[0], cotangent[0], peer_both, kv_same, kv_other, head_size, docs, blocks
    )
    same_terms, other_terms, *other_parts = lax.optimization_barrier(
        (same_terms, other_terms, *other_parts)
    )
    chip_terms = (same_terms + swap_cores(other_terms).astype(jnp.float32)).astype(jnp.bfloat16)
    terms = lax.all_to_all(chip_terms, SAME_CORE_CTX, split_axis=0, concat_axis=0, tiled=True)
    grads = jnp.sum(
        terms.reshape(groups, rows_here, 2 * head_size).astype(jnp.float32), axis=0
    ).astype(jnp.bfloat16)
    peer_grads = swap_cores(grads)

    def weight_term(i):
        cut = slice(i * part_rows, (i + 1) * part_rows)
        return sum(
            lax.dot_general(
                g, rows[:, cut], (((0,), (0,)), ((), ())), preferred_element_type=jnp.float32
            )
            for rows, g in ((tokens_own, grads), (tokens_peer, peer_grads))
        )

    summed = reduce_ring([weight_term(i) for i in range(4)], 2)
    token_grad = token_gradient(table, grads, weight_parts + other_parts)
    summed, token_grad = lax.optimization_barrier((summed, token_grad))
    from_peer = swap_cores(jnp.concatenate([mixed[rows_here:], query_grad[rows_here:]], axis=1))

    def both_halves(own, peers):
        return jnp.concatenate(
            [jnp.where(core == 0, own, peers), jnp.where(core == 0, peers, own)], axis=1
        )

    half_width = mixed.shape[1]
    mixed = both_halves(mixed[:rows_here], from_peer[:, :half_width])
    query_grad = both_halves(query_grad[:rows_here], from_peer[:, half_width:])
    for phase in (1, 0):
        summed = reduce_ring(jnp.split(summed, 4, axis=1), phase)
    summed = summed.T
    return (
        mixed[None],
        query_grad[None],
        token_grad[None],
        summed[:, :head_size],
        summed[:, head_size:],
    )


def solution(mesh):
    torus = Mesh(mesh.devices.reshape(SIZES), AXES)
    whole = CTX + DP
    in_specs = (
        P(DP, CTX, None),
        P(DP, CTX, None),
        P(DP, CTX, None),
        P(whole, None),
        P(whole, None),
        P(DP, None),
        P(DP, None),
    )
    out_specs = (
        P(DP, CTX, None),
        P(DP, CTX, None),
        P(DP, CTX, None),
        P(whole, None),
        P(whole, None),
    )
    return jax.shard_map(body, mesh=torus, in_specs=in_specs, out_specs=out_specs, check_vma=False)
```

```python
import functools

import jax
import jax.numpy as jnp
import numpy as np
from jax import lax
from jax.experimental import pallas as pl
from jax.experimental.pallas import tpu as pltpu
from jax.sharding import Mesh
from jax.sharding import PartitionSpec as P

AXES = ("y", "zh", "core", "x", "zl")
SIZES = (4, 2, 2, 4, 2)
CTX = ("y", "zh", "core")
DP = ("x", "zl")
SAME_CORE_CTX = ("y", "zh")
DEVICES = int(np.prod(SIZES))

EPSILON = 1e-05
NEGATIVE = -1e30
KEY_CHUNK = 256
STRIP = 32

RING_ORDER = {0: ("x", "y", "z"), 1: ("y", "z", "x")}
OFFSETS = (0, -1, 1, 2)


def coordinates(device):
    y, zh, core, x, zl = (int(v) for v in np.unravel_index(device, SIZES))
    return {"y": y, "z": zh * 2 + zl, "x": x, "core": core}


def device_of(place):
    return int(
        np.ravel_multi_index(
            (place["y"], place["z"] // 2, place["core"], place["x"], place["z"] % 2), SIZES
        )
    )


def moved(change):
    pairs = []
    for device in range(DEVICES):
        place = coordinates(device)
        change(place)
        pairs.append((device, device_of(place)))
    return pairs


def along_ring(phase, step):
    def change(place):
        axis = RING_ORDER[place["core"]][phase]
        place[axis] = (place[axis] + step) % 4

    return moved(change)


def to_other_core(place):
    place["core"] = 1 - place["core"]


def swap_cores(value):
    return lax.ppermute(value, AXES, moved(to_other_core))


def block_table():
    table = np.zeros((DEVICES, DEVICES), np.int32)
    for device in range(DEVICES):
        here = coordinates(device)
        at = 0
        for core in (here["core"], 1 - here["core"]):
            order = RING_ORDER[core]
            for last in OFFSETS:
                for middle in OFFSETS:
                    for first in OFFSETS:
                        place = dict(here, core=core)
                        for axis, step in zip(order, (first, middle, last)):
                            place[axis] = (place[axis] + step) % 4
                        table[device, at] = device_of(place)
                        at += 1
    return table


def gather_ring(value, phase):
    return [value] + [
        lax.ppermute(value, AXES, along_ring(phase, -offset)) for offset in OFFSETS[1:]
    ]


def reduce_ring(pieces, phase):
    total = pieces[0]
    for piece, offset in zip(pieces[1:], OFFSETS[1:]):
        sent = lax.ppermute(piece.astype(jnp.bfloat16), AXES, along_ring(phase, offset))
        total = total + sent.astype(jnp.float32)
    return total


def levels(ratio):
    return jnp.where(ratio >= 0.5, 1.0, jnp.where(ratio <= -0.5, -1.0, 0.0)).astype(jnp.float32)


def shuffle_kernel(table, tokens, own, other):
    width = own.shape[1] * 2 // DEVICES
    half = DEVICES // 2

    def move(j, _):
        target = pl.ds(pl.multiple_of(j * width, width), width)
        for first, out in ((0, own), (half, other)):
            source = pl.ds(pl.multiple_of(table[first + j] * width, width), width)
            out[:, target] = tokens[:, source]
        return 0

    lax.fori_loop(0, half, move, 0, unroll=8)


def shuffle(table, tokens):
    rows, features = tokens.shape
    step_rows = 32
    half = jax.ShapeDtypeStruct((rows, features // 2), tokens.dtype)
    half_spec = pl.BlockSpec((step_rows, features // 2), lambda i: (i, 0))
    return pl.pallas_call(
        shuffle_kernel,
        grid=(rows // step_rows,),
        out_shape=(half, half),
        in_specs=[
            pl.BlockSpec(memory_space=pltpu.SMEM),
            pl.BlockSpec((step_rows, features), lambda i: (i, 0)),
        ],
        out_specs=(half_spec, half_spec),
        compiler_params=pltpu.CompilerParams(vmem_limit_bytes=16 << 20),
        cost_estimate=pl.CostEstimate(
            flops=0, bytes_accessed=4 * rows * features, transcendentals=0
        ),
        name="shuffle_tokens",
    )(table, tokens)


def weight_terms_kernel(grads, peer_grads, tokens, peer_tokens, *rest):
    outs, turned = rest[:-1], rest[-1]
    step = pl.program_id(0)

    @pl.when(step == 0)
    def _():
        turned[0] = grads[...].T
        turned[1] = peer_grads[...].T

    term = jnp.dot(turned[0], tokens[...], preferred_element_type=jnp.float32) + jnp.dot(
        turned[1], peer_tokens[...], preferred_element_type=jnp.float32
    )
    for n, out in enumerate(outs):

        @pl.when(step // 2 == n)
        def _(out=out):
            out[...] = term.astype(out.dtype)


def weight_terms(grads, peer_grads, tokens, peer_tokens):
    rows, features = tokens.shape
    both = grads.shape[1]
    pieces = len(OFFSETS)
    width = features // pieces // 2
    whole = pl.BlockSpec((rows, both), lambda i: (0, 0))
    cut = pl.BlockSpec((rows, width), lambda i: (0, i))
    return pl.pallas_call(
        weight_terms_kernel,
        grid=(2 * pieces,),
        out_shape=tuple(
            jax.ShapeDtypeStruct((both, 2 * width), jnp.bfloat16 if n else jnp.float32)
            for n in range(pieces)
        ),
        in_specs=[whole, whole, cut, cut],
        out_specs=tuple(
            pl.BlockSpec((both, width), lambda i, n=n: (0, jnp.clip(i - 2 * n, 0, 1)))
            for n in range(pieces)
        ),
        scratch_shapes=[pltpu.VMEM((2, both, rows), jnp.bfloat16)],
        compiler_params=pltpu.CompilerParams(vmem_limit_bytes=56 << 20),
        cost_estimate=pl.CostEstimate(
            flops=4 * rows * both * features,
            bytes_accessed=4 * rows * features + 3 * both * features,
            transcendentals=0,
        ),
        name="weight_terms",
    )(grads, peer_grads, tokens, peer_tokens)


def token_grad_kernel(table, grads, *rest, count):
    weights, out = rest[:count], rest[count]
    buffers, sems = rest[count + 1 :]
    rows, step_width = buffers.shape[1:]
    width = out.shape[1] // DEVICES
    per_step = step_width // width
    steps_each = weights[0].shape[0] // step_width
    for step in range(count * steps_each):
        slot = step % 2
        buffer, sem = buffers.at[slot], sems.at[slot]
        if step >= 2:
            pltpu.make_async_copy(buffer, buffer, sem).wait()
        part = (step % steps_each) * step_width
        buffers[slot] = lax.dot_general(
            grads[...],
            weights[step // steps_each][part : part + step_width, :],
            (((1,), (1,)), ((), ())),
            preferred_element_type=jnp.float32,
        ).astype(jnp.bfloat16)
        for j in range(per_step):
            target = pl.ds(pl.multiple_of(table[step * per_step + j] * width, width), width)
            pltpu.make_async_copy(
                buffer.at[:, j * width : (j + 1) * width], out.at[:, target], sem
            ).start()
    for slot in range(2):
        pltpu.make_async_copy(buffers.at[slot], buffers.at[slot], sems.at[slot]).wait()


def token_gradient(table, grads, weights):
    rows, both = grads.shape
    features = sum(w.shape[0] for w in weights)
    step_width = 1024
    in_vmem = pl.BlockSpec(memory_space=pltpu.VMEM)
    return pl.pallas_call(
        functools.partial(token_grad_kernel, count=len(weights)),
        out_shape=jax.ShapeDtypeStruct((rows, features), jnp.bfloat16),
        in_specs=[pl.BlockSpec(memory_space=pltpu.SMEM)] + [in_vmem] * (1 + len(weights)),
        out_specs=pl.BlockSpec(memory_space=pl.ANY),
        scratch_shapes=[
            pltpu.VMEM((2, rows, step_width), jnp.bfloat16),
            pltpu.SemaphoreType.DMA((2,)),
        ],
        compiler_params=pltpu.CompilerParams(vmem_limit_bytes=32 << 20),
        cost_estimate=pl.CostEstimate(
            flops=2 * rows * both * features,
            bytes_accessed=2 * features * (rows + both),
            transcendentals=0,
        ),
        name="token_gradient",
    )(table, grads, *weights)


def attention_kernel(
    meta, queries, cotangent, peer_both, kv_same, kv_other,
    mixed_out, query_grad, same_out, other_out,
    q_held, c_held, peer_held, kv_held, key_acc, value_acc, scores, prob_grad, low,
    q_columns, c_columns, q_rows, c_rows, sems,
    *, heads, head_size, block, docs, blocks,
):
    scale = head_size ** (-0.5)
    columns = heads * block
    ctx, core = meta[docs + blocks], meta[docs + blocks + 1]
    own_blocks = q_held.shape[0] // block
    in_strip = lax.broadcasted_iota(jnp.int32, (STRIP, columns), 0)
    sides = ((kv_same, core, same_out), (kv_other, 1 - core, other_out))

    def rows_at(index, size):
        return pl.ds(pl.multiple_of(index * size, size), size)

    def true_block(core_of, j):
        return meta[docs + ((j // 2) * 2 + core_of) * 2 + j % 2]

    copies = [
        pltpu.make_async_copy(source, held, sems.at[n])
        for n, (source, held) in enumerate(
            ((queries, q_held), (cotangent, c_held), (peer_both, peer_held))
        )
    ]
    for copy in copies:
        copy.start()
    for n, (ref, core_of, _) in enumerate(sides):
        for j in range(blocks // 2):
            pltpu.make_async_copy(
                ref.at[j * block : (j + 1) * block, :],
                kv_held.at[rows_at(true_block(core_of, j), block), :],
                sems.at[len(copies) + n],
            ).start()
    key_acc[...] = jnp.zeros_like(key_acc)
    value_acc[...] = jnp.zeros_like(value_acc)
    for copy in copies:
        copy.wait()
    for i in range(2 * own_blocks):
        here = slice(i % own_blocks * block, (i % own_blocks + 1) * block)
        for h in range(heads):
            part = slice(h * block, (h + 1) * block)
            if i < own_blocks:
                head = rows_at(core * heads + h, head_size)
                q, c = q_held[here, head], c_held[here, head]
            else:
                q = peer_held[here, h * head_size : (h + 1) * head_size]
                c = peer_held[here, (heads + h) * head_size : (heads + h + 1) * head_size]
            q_rows[i, part, :], c_rows[i, part, :] = q, c
            q_columns[i, :, part], c_columns[i, :, part] = q.T, c.T
    for n, (ref, _, _) in enumerate(sides):
        pltpu.make_async_copy(
            ref, kv_held.at[: blocks // 2 * block, :], sems.at[len(copies) + n]
        ).wait()

    def keys_at(chunk):
        return kv_held[rows_at(chunk, KEY_CHUNK), :head_size]

    def values_at(chunk):
        return kv_held[rows_at(chunk, KEY_CHUNK), head_size:]

    def one_block(i, _):
        here = rows_at(i, block)
        ctx_of = jnp.where(i < own_blocks, ctx, ctx + 1 - 2 * core)
        start = meta[docs + own_blocks * ctx_of + lax.rem(i, own_blocks)] * block
        position = start + lax.rem(lax.broadcasted_iota(jnp.int32, (1, columns), 1), block)
        own_start = jnp.zeros((1, columns), jnp.int32)
        first = jnp.int32(0)
        for d in range(docs):
            doc_start = meta[d]
            own_start = jnp.maximum(own_start, jnp.where(position >= doc_start, doc_start, 0))
            first = jnp.maximum(first, jnp.where(start >= doc_start, doc_start, 0))
        lowest = first // KEY_CHUNK
        count = (start + block - 1) // KEY_CHUNK - lowest + 1

        def score(c, best):
            scores[c] = jnp.dot(
                keys_at(lowest + c),
                q_columns[i],
                preferred_element_type=jnp.float32,
            )
            first_key = (lowest + c) * KEY_CHUNK
            for at in range(0, KEY_CHUNK, STRIP):
                strip = slice(at, at + STRIP)
                key_pos = first_key + at + in_strip
                visible = (key_pos >= own_start) & (key_pos <= position)
                s = jnp.where(visible, scores[c, strip, :] * scale, NEGATIVE)
                scores[c, strip, :] = s
                best = jnp.maximum(best, jnp.max(s.reshape(STRIP // 8, 8, columns), axis=0))
            return best

        best = lax.fori_loop(
            0, count, score, jnp.full((8, columns), NEGATIVE, jnp.float32)
        )
        best = jnp.max(best, axis=0, keepdims=True)

        def mix(c, carried):
            total, acc = carried
            for at in range(0, KEY_CHUNK, STRIP):
                strip = slice(at, at + STRIP)
                w = jnp.exp(scores[c, strip, :] - best)
                scores[c, strip, :] = w
                low[0, strip, :] = w.astype(jnp.bfloat16)
                total = total + jnp.sum(w.reshape(STRIP // 8, 8, columns), axis=0)
            acc = acc + lax.dot_general(
                values_at(lowest + c),
                low[0],
                (((0,), (0,)), ((), ())),
                preferred_element_type=jnp.float32,
            )
            return total, acc

        total, acc = lax.fori_loop(
            0,
            count,
            mix,
            (jnp.zeros((8, columns), jnp.float32), jnp.zeros((head_size, columns), jnp.float32)),
        )
        total = jnp.sum(total, axis=0, keepdims=True)
        mixed = (acc / total).astype(jnp.bfloat16)
        expected = jnp.sum(
            mixed.astype(jnp.float32) * c_columns[i].astype(jnp.float32), axis=0, keepdims=True
        )
        per_total = 1.0 / total
        for h in range(heads):
            mixed_out[here, h * head_size : (h + 1) * head_size] = mixed[
                :, h * block : (h + 1) * block
            ].T

        def back(c, q_acc):
            chunk = rows_at(lowest + c, KEY_CHUNK)
            prob_grad[...] = jnp.dot(
                values_at(lowest + c), c_columns[i], preferred_element_type=jnp.float32
            )
            for at in range(0, KEY_CHUNK, STRIP):
                strip = slice(at, at + STRIP)
                probability = scores[c, strip, :] * per_total
                low[0, strip, :] = probability.astype(jnp.bfloat16)
                low[1, strip, :] = (probability * (prob_grad[strip, :] - expected)).astype(
                    jnp.bfloat16
                )
            value_acc[chunk, :] += jnp.dot(low[0], c_rows[i], preferred_element_type=jnp.float32)
            key_acc[chunk, :] += jnp.dot(low[1], q_rows[i], preferred_element_type=jnp.float32)
            return q_acc + lax.dot_general(
                keys_at(lowest + c),
                low[1],
                (((0,), (0,)), ((), ())),
                preferred_element_type=jnp.float32,
            )

        q_acc = lax.fori_loop(
            0, count, back, jnp.zeros((head_size, columns), jnp.float32)
        )
        q_grad = (q_acc * scale).astype(jnp.bfloat16)
        for h in range(heads):
            query_grad[here, h * head_size : (h + 1) * head_size] = q_grad[
                :, h * block : (h + 1) * block
            ].T
        return 0

    lax.fori_loop(0, 2 * own_blocks, one_block, 0)
    for _, core_of, out in sides:
        for j in range(blocks // 2):
            source = rows_at(true_block(core_of, j), block)
            part = slice(j * block, (j + 1) * block)
            out[part, :head_size] = (key_acc[source, :] * scale).astype(out.dtype)
            out[part, head_size:] = value_acc[source, :].astype(out.dtype)


def attention(meta, queries, cotangent, peer_both, kv_same, kv_other, head_size, docs, blocks):
    rows, width = queries.shape
    heads = width // head_size // 2
    length = kv_same.shape[0] + kv_other.shape[0]
    block = length // blocks
    columns = heads * block
    query_blocks = 2 * rows // block
    in_vmem = pl.BlockSpec(memory_space=pltpu.VMEM)
    most_chunks = 10
    visible = 9 * KEY_CHUNK
    return pl.pallas_call(
        functools.partial(
            attention_kernel, heads=heads, head_size=head_size, block=block, docs=docs, blocks=blocks
        ),
        out_shape=(
            jax.ShapeDtypeStruct((2 * rows, width // 2), jnp.bfloat16),
            jax.ShapeDtypeStruct((2 * rows, width // 2), jnp.bfloat16),
            jax.ShapeDtypeStruct(kv_same.shape, jnp.float32),
            jax.ShapeDtypeStruct(kv_other.shape, jnp.bfloat16),
        ),
        in_specs=[pl.BlockSpec(memory_space=pltpu.SMEM)] + [pl.BlockSpec(memory_space=pl.ANY)] * 5,
        out_specs=(in_vmem,) * 4,
        scratch_shapes=[
            pltpu.VMEM(queries.shape, jnp.bfloat16),
            pltpu.VMEM(cotangent.shape, jnp.bfloat16),
            pltpu.VMEM(peer_both.shape, jnp.bfloat16),
            pltpu.VMEM((length, 2 * head_size), jnp.bfloat16),
            pltpu.VMEM((length, head_size), jnp.float32),
            pltpu.VMEM((length, head_size), jnp.float32),
            pltpu.VMEM((most_chunks, KEY_CHUNK, columns), jnp.float32),
            pltpu.VMEM((KEY_CHUNK, columns), jnp.float32),
            pltpu.VMEM((2, KEY_CHUNK, columns), jnp.bfloat16),
            pltpu.VMEM((query_blocks, head_size, columns), jnp.bfloat16),
            pltpu.VMEM((query_blocks, head_size, columns), jnp.bfloat16),
            pltpu.VMEM((query_blocks, columns, head_size), jnp.bfloat16),
            pltpu.VMEM((query_blocks, columns, head_size), jnp.bfloat16),
            pltpu.SemaphoreType.DMA((5,)),
        ],
        compiler_params=pltpu.CompilerParams(vmem_limit_bytes=26 << 20),
        cost_estimate=pl.CostEstimate(
            flops=28 * rows * heads * visible * head_size,
            bytes_accessed=8 * rows * width + 8 * length * head_size,
            transcendentals=2 * rows * heads * visible,
        ),
        name="masked_attention",
    )(meta, queries, cotangent, peer_both, kv_same, kv_other)


def body(tokens, queries, cotangent, latent_key, latent_value, lengths, block_order):
    token_rows = tokens[0]
    rows_here, features = token_rows.shape
    head_size = latent_key.shape[1]
    docs, blocks = lengths.shape[1], block_order.shape[1]
    me = lax.axis_index(AXES)
    table = lax.dynamic_index_in_dim(jnp.asarray(block_table()), me, keepdims=False)
    before = np.arange(docs)[:, None] < np.arange(docs)[None, :]
    doc_starts = jnp.sum(jnp.where(before, lengths[0][:, None], 0), axis=0)
    meta = jnp.concatenate(
        [
            doc_starts.astype(jnp.int32),
            block_order[0],
            jnp.stack([lax.axis_index(CTX), lax.axis_index("core")]).astype(jnp.int32),
        ]
    )

    core = lax.axis_index("core")
    peer_both = swap_cores(
        jnp.concatenate(
            [
                lax.dynamic_slice_in_dim(a[0], (1 - core) * a.shape[2] // 2, a.shape[2] // 2, 1)
                for a in (queries, cotangent)
            ],
            axis=1,
        )
    )
    latents = jnp.concatenate([latent_key, latent_value], axis=1)
    for phase in range(2):
        latents = jnp.concatenate(gather_ring(latents, phase), axis=0)
    latents, peer_both, meta = lax.optimization_barrier((latents, peer_both, meta))
    sums = jnp.broadcast_to(jnp.sum(jnp.abs(latents), axis=0, keepdims=True), (8, 2 * head_size))
    sums = sum(gather_ring(sums, 2))
    sums = sums + swap_cores(sums)
    entry_count = features * head_size
    key_scale = jnp.sum(sums[0, :head_size]) / entry_count + EPSILON
    value_scale = jnp.sum(sums[0, head_size:]) / entry_count + EPSILON
    weights = jnp.concatenate(
        [
            (scale * levels(latent / scale)).astype(jnp.bfloat16)
            for latent, scale in (
                (latents[:, :head_size], key_scale),
                (latents[:, head_size:], value_scale),
            )
        ],
        axis=1,
    )
    weights, shuffle_table = lax.optimization_barrier((weights, table))
    weight_parts = gather_ring(weights, 2)
    tokens_own, tokens_other = shuffle(shuffle_table, token_rows)
    other_parts = [swap_cores(part) for part in weight_parts]
    part_rows = weights.shape[0]
    projected = 0.0
    for i, (own, other) in enumerate(zip(weight_parts, other_parts)):
        cut = slice(i * part_rows, (i + 1) * part_rows)
        for rows, part in ((tokens_own, own), (tokens_other, other)):
            projected = projected + jnp.dot(
                rows[:, cut], part, preferred_element_type=jnp.float32
            )
    kv_here = projected.astype(jnp.bfloat16)
    groups = lax.axis_size(SAME_CORE_CTX)
    kv_same = lax.all_to_all(
        jnp.broadcast_to(kv_here[None], (groups,) + kv_here.shape).reshape(-1, 2 * head_size),
        SAME_CORE_CTX,
        split_axis=0,
        concat_axis=0,
        tiled=True,
    )
    kv_other = swap_cores(kv_same)
    tokens_peer = swap_cores(tokens_other)

    mixed, query_grad, same_terms, other_terms = attention(
        meta, queries[0], cotangent[0], peer_both, kv_same, kv_other, head_size, docs, blocks
    )
    same_terms, other_terms, tokens_peer = lax.optimization_barrier(
        (same_terms, other_terms, tokens_peer)
    )
    chip_terms = (same_terms + swap_cores(other_terms).astype(jnp.float32)).astype(jnp.bfloat16)
    terms = lax.all_to_all(chip_terms, SAME_CORE_CTX, split_axis=0, concat_axis=0, tiled=True)
    grads = jnp.sum(
        terms.reshape(groups, rows_here, 2 * head_size).astype(jnp.float32), axis=0
    ).astype(jnp.bfloat16)
    peer_grads = swap_cores(grads)

    summed = reduce_ring(weight_terms(grads, peer_grads, tokens_own, tokens_peer), 2)
    token_grad = token_gradient(table, grads, weight_parts + other_parts)
    summed, token_grad = lax.optimization_barrier((summed, token_grad))
    from_peer = swap_cores(jnp.concatenate([mixed[rows_here:], query_grad[rows_here:]], axis=1))

    def both_halves(own, peers):
        return jnp.concatenate(
            [jnp.where(core == 0, own, peers), jnp.where(core == 0, peers, own)], axis=1
        )

    half_width = mixed.shape[1]
    mixed = both_halves(mixed[:rows_here], from_peer[:, :half_width])
    query_grad = both_halves(query_grad[:rows_here], from_peer[:, half_width:])
    for phase in (1, 0):
        summed = reduce_ring(jnp.split(summed, 4, axis=1), phase)
    summed = summed.T
    return (
        mixed[None],
        query_grad[None],
        token_grad[None],
        summed[:, :head_size],
        summed[:, head_size:],
    )


def solution(mesh):
    torus = Mesh(mesh.devices.reshape(SIZES), AXES)
    whole = CTX + DP
    in_specs = (
        P(DP, CTX, None),
        P(DP, CTX, None),
        P(DP, CTX, None),
        P(whole, None),
        P(whole, None),
        P(DP, None),
        P(DP, None),
    )
    out_specs = (
        P(DP, CTX, None),
        P(DP, CTX, None),
        P(DP, CTX, None),
        P(whole, None),
        P(whole, None),
    )
    return jax.shard_map(body, mesh=torus, in_specs=in_specs, out_specs=out_specs, check_vma=False)
```

```python
import functools

import jax
import jax.numpy as jnp
import numpy as np
from jax import lax
from jax.experimental import pallas as pl
from jax.experimental.pallas import tpu as pltpu
from jax.sharding import Mesh
from jax.sharding import PartitionSpec as P

AXES = ("y", "zh", "core", "x", "zl")
SIZES = (4, 2, 2, 4, 2)
CTX = ("y", "zh", "core")
DP = ("x", "zl")
SAME_CORE_CTX = ("y", "zh")
DEVICES = int(np.prod(SIZES))

EPSILON = 1e-05
NEGATIVE = -1e30
KEY_CHUNK = 256
STRIP = 32

RING_ORDER = {0: ("x", "y", "z"), 1: ("y", "z", "x")}
OFFSETS = (0, -1, 1, 2)


def coordinates(device):
    y, zh, core, x, zl = (int(v) for v in np.unravel_index(device, SIZES))
    return {"y": y, "z": zh * 2 + zl, "x": x, "core": core}


def device_of(place):
    return int(
        np.ravel_multi_index(
            (place["y"], place["z"] // 2, place["core"], place["x"], place["z"] % 2), SIZES
        )
    )


def moved(change):
    pairs = []
    for device in range(DEVICES):
        place = coordinates(device)
        change(place)
        pairs.append((device, device_of(place)))
    return pairs


def along_ring(phase, step):
    def change(place):
        axis = RING_ORDER[place["core"]][phase]
        place[axis] = (place[axis] + step) % 4

    return moved(change)


def to_other_core(place):
    place["core"] = 1 - place["core"]


def swap_cores(value):
    return lax.ppermute(value, AXES, moved(to_other_core))


def block_table():
    table = np.zeros((DEVICES, DEVICES), np.int32)
    for device in range(DEVICES):
        here = coordinates(device)
        at = 0
        for core in (here["core"], 1 - here["core"]):
            order = RING_ORDER[core]
            for last in OFFSETS:
                for middle in OFFSETS:
                    for first in OFFSETS:
                        place = dict(here, core=core)
                        for axis, step in zip(order, (first, middle, last)):
                            place[axis] = (place[axis] + step) % 4
                        table[device, at] = device_of(place)
                        at += 1
    return table


def gather_ring(value, phase):
    return [value] + [
        lax.ppermute(value, AXES, along_ring(phase, -offset)) for offset in OFFSETS[1:]
    ]


def sent_along_ring(pieces, phase):
    return [
        lax.ppermute(piece.astype(jnp.bfloat16), AXES, along_ring(phase, offset))
        for piece, offset in zip(pieces, OFFSETS[1:])
    ]


def shuffle_kernel(table, tokens, own, other):
    width = own.shape[1] * 2 // DEVICES
    half = DEVICES // 2

    def move(j, _):
        target = pl.ds(pl.multiple_of(j * width, width), width)
        for first, out in ((0, own), (half, other)):
            source = pl.ds(pl.multiple_of(table[first + j] * width, width), width)
            out[:, target] = tokens[:, source]
        return 0

    lax.fori_loop(0, half, move, 0, unroll=8)


def shuffle(table, tokens):
    rows, features = tokens.shape
    step_rows = 32
    half = jax.ShapeDtypeStruct((rows, features // 2), tokens.dtype)
    half_spec = pl.BlockSpec((step_rows, features // 2), lambda i: (i, 0))
    return pl.pallas_call(
        shuffle_kernel,
        grid=(rows // step_rows,),
        out_shape=(half, half),
        in_specs=[
            pl.BlockSpec(memory_space=pltpu.SMEM),
            pl.BlockSpec((step_rows, features), lambda i: (i, 0)),
        ],
        out_specs=(half_spec, half_spec),
        compiler_params=pltpu.CompilerParams(vmem_limit_bytes=16 << 20),
        cost_estimate=pl.CostEstimate(
            flops=0, bytes_accessed=4 * rows * features, transcendentals=0
        ),
        name="shuffle_tokens",
    )(table, tokens)


def weight_terms_kernel(grads, peer_grads, tokens, peer_tokens, *rest, first, count):
    outs, (turned, held, sems) = rest[:count], rest[count:]
    step = held.shape[2] // (2 * count)
    copies = []
    for n in range(2 * count):
        here, there = slice(n * step, (n + 1) * step), slice(first + n * step, first + (n + 1) * step)
        copies.append(
            [
                pltpu.make_async_copy(source.at[:, there], held.at[side, :, here], sems.at[side, n])
                for side, source in enumerate((tokens, peer_tokens))
            ]
        )
    for pair in copies:
        for copy in pair:
            copy.start()
    turned[0] = grads[...].T
    turned[1] = peer_grads[...].T
    for n, pair in enumerate(copies):
        here = slice(n * step, (n + 1) * step)
        for copy in pair:
            copy.wait()
        term = jnp.dot(turned[0], held[0, :, here], preferred_element_type=jnp.float32) + jnp.dot(
            turned[1], held[1, :, here], preferred_element_type=jnp.float32
        )
        out = outs[n // 2]
        out[:, n % 2 * step : (n % 2 + 1) * step] = term.astype(out.dtype)


def weight_terms(grads, peer_grads, tokens, peer_tokens, first, count, dtype):
    rows, features = tokens.shape
    both = grads.shape[1]
    width = features // len(OFFSETS)
    in_vmem = pl.BlockSpec(memory_space=pltpu.VMEM)
    anywhere = pl.BlockSpec(memory_space=pltpu.HBM)
    return pl.pallas_call(
        functools.partial(weight_terms_kernel, first=first * width, count=count),
        out_shape=(jax.ShapeDtypeStruct((both, width), dtype),) * count,
        in_specs=[in_vmem, in_vmem, anywhere, anywhere],
        out_specs=(in_vmem,) * count,
        scratch_shapes=[
            pltpu.VMEM((2, both, rows), jnp.bfloat16),
            pltpu.VMEM((2, rows, count * width), tokens.dtype),
            pltpu.SemaphoreType.DMA((2, 2 * count)),
        ],
        compiler_params=pltpu.CompilerParams(vmem_limit_bytes=58 << 20),
        cost_estimate=pl.CostEstimate(
            flops=4 * rows * both * count * width,
            bytes_accessed=(4 * rows + 2 * both) * count * width,
            transcendentals=0,
        ),
        name="weight_terms",
    )(grads, peer_grads, tokens, peer_tokens)


def side_by_side_kernel(left, right, out):
    width = left.shape[1]
    out[:, :width] = left[...]
    out[:, width:] = right[...]


def magnitudes_kernel(*refs):
    pieces, out = refs[:-1], refs[-1]
    out[...] = sum(
        jnp.sum(jnp.abs(piece[...]).reshape(-1, *out.shape), axis=0) for piece in pieces
    )


def ternary_kernel(sums, *refs, entries):
    pieces, out = refs[:-1], refs[-1]
    half = out.shape[1] // 2
    for columns in (slice(0, half), slice(half, 2 * half)):
        scale = jnp.sum(sums[:, columns]) / entries + EPSILON
        level = jnp.full((1, half), scale, jnp.float32)
        for n, piece in enumerate(pieces):
            rows = piece.shape[0]
            latent = piece[:, columns]
            out[n * rows : (n + 1) * rows, columns] = jnp.where(
                latent >= 0.5 * level, level, jnp.where(latent <= -0.5 * level, -level, 0.0)
            ).astype(jnp.bfloat16)


def last_sum_kernel(own, first, second, third, key_out, value_out):
    total = own[...]
    for piece in (first, second, third):
        total = total + piece[...].astype(jnp.float32)
    half = key_out.shape[1]
    key_out[...] = total[:half].T
    value_out[...] = total[half:].T


def small(kernel, name, out_shape, *args):
    in_vmem = pl.BlockSpec(memory_space=pltpu.VMEM)
    return pl.pallas_call(
        kernel,
        out_shape=out_shape,
        in_specs=[in_vmem] * len(args),
        out_specs=jax.tree.map(lambda _: in_vmem, out_shape),
        compiler_params=pltpu.CompilerParams(vmem_limit_bytes=12 << 20),
        cost_estimate=pl.CostEstimate(
            flops=0, bytes_accessed=sum(a.size * a.dtype.itemsize for a in args), transcendentals=0
        ),
        name=name,
    )(*args)


def token_grad_kernel(table, grads, *rest, count):
    weights, out = rest[:count], rest[count]
    held, held_sems, buffers, sems = rest[count + 1 :]
    slots, step_width = held.shape[:2]
    width = out.shape[1] // DEVICES
    per_step = step_width // width
    steps_each = weights[0].shape[0] // step_width

    def fetch(step):
        part = (step % steps_each) * step_width
        return pltpu.make_async_copy(
            weights[step // steps_each].at[part : part + step_width, :],
            held.at[step % slots],
            held_sems.at[step % slots],
        )

    for step in range(slots - 1):
        fetch(step).start()
    for step in range(count * steps_each):
        slot = step % 2
        buffer, sem = buffers.at[slot], sems.at[slot]
        if step + slots - 1 < count * steps_each:
            fetch(step + slots - 1).start()
        fetch(step).wait()
        if step >= 2:
            pltpu.make_async_copy(buffer, buffer, sem).wait()
        buffers[slot] = lax.dot_general(
            grads[...],
            held[step % slots],
            (((1,), (1,)), ((), ())),
            preferred_element_type=jnp.float32,
        ).astype(jnp.bfloat16)
        for j in range(per_step):
            target = pl.ds(pl.multiple_of(table[step * per_step + j] * width, width), width)
            pltpu.make_async_copy(
                buffer.at[:, j * width : (j + 1) * width], out.at[:, target], sem
            ).start()
    for slot in range(2):
        pltpu.make_async_copy(buffers.at[slot], buffers.at[slot], sems.at[slot]).wait()


def token_gradient(table, grads, weights):
    rows, both = grads.shape
    features = sum(w.shape[0] for w in weights)
    step_width = 1024
    slots = 4
    return pl.pallas_call(
        functools.partial(token_grad_kernel, count=len(weights)),
        out_shape=jax.ShapeDtypeStruct((rows, features), jnp.bfloat16),
        in_specs=[
            pl.BlockSpec(memory_space=pltpu.SMEM),
            pl.BlockSpec(memory_space=pltpu.VMEM),
        ]
        + [pl.BlockSpec(memory_space=pltpu.HBM)] * len(weights),
        out_specs=pl.BlockSpec(memory_space=pl.ANY),
        scratch_shapes=[
            pltpu.VMEM((slots, step_width, both), jnp.bfloat16),
            pltpu.SemaphoreType.DMA((slots,)),
            pltpu.VMEM((2, rows, step_width), jnp.bfloat16),
            pltpu.SemaphoreType.DMA((2,)),
        ],
        compiler_params=pltpu.CompilerParams(vmem_limit_bytes=58 << 20),
        cost_estimate=pl.CostEstimate(
            flops=2 * rows * both * features,
            bytes_accessed=2 * features * (rows + both),
            transcendentals=0,
        ),
        name="token_gradient",
    )(table, grads, *weights)


def attention_kernel(
    meta, queries, cotangent, peer_both, kv_same, kv_other,
    mixed_out, query_grad, same_out, other_out,
    q_held, c_held, peer_held, kv_held, key_acc, value_acc, scores, prob_grad, low,
    q_columns, c_columns, q_rows, c_rows, sems,
    *, heads, head_size, block, docs, blocks,
):
    scale = head_size ** (-0.5)
    columns = heads * block
    ctx, core = meta[docs + blocks], meta[docs + blocks + 1]
    own_blocks = q_held.shape[0] // block
    in_strip = lax.broadcasted_iota(jnp.int32, (STRIP, columns), 0)
    sides = ((kv_same, core, same_out), (kv_other, 1 - core, other_out))

    def rows_at(index, size):
        return pl.ds(pl.multiple_of(index * size, size), size)

    def true_block(core_of, j):
        return meta[docs + ((j // 2) * 2 + core_of) * 2 + j % 2]

    copies = [
        pltpu.make_async_copy(source, held, sems.at[n])
        for n, (source, held) in enumerate(
            ((queries, q_held), (cotangent, c_held), (peer_both, peer_held))
        )
    ]
    for copy in copies:
        copy.start()
    for n, (ref, core_of, _) in enumerate(sides):
        for j in range(blocks // 2):
            pltpu.make_async_copy(
                ref.at[j * block : (j + 1) * block, :],
                kv_held.at[rows_at(true_block(core_of, j), block), :],
                sems.at[len(copies) + n],
            ).start()
    key_acc[...] = jnp.zeros_like(key_acc)
    value_acc[...] = jnp.zeros_like(value_acc)
    for copy in copies:
        copy.wait()
    for i in range(2 * own_blocks):
        here = slice(i % own_blocks * block, (i % own_blocks + 1) * block)
        for h in range(heads):
            part = slice(h * block, (h + 1) * block)
            if i < own_blocks:
                head = rows_at(core * heads + h, head_size)
                q, c = q_held[here, head], c_held[here, head]
            else:
                q = peer_held[here, h * head_size : (h + 1) * head_size]
                c = peer_held[here, (heads + h) * head_size : (heads + h + 1) * head_size]
            q_rows[i, part, :], c_rows[i, part, :] = q, c
            q_columns[i, :, part], c_columns[i, :, part] = q.T, c.T
    for n, (ref, _, _) in enumerate(sides):
        pltpu.make_async_copy(
            ref, kv_held.at[: blocks // 2 * block, :], sems.at[len(copies) + n]
        ).wait()

    def keys_at(chunk):
        return kv_held[rows_at(chunk, KEY_CHUNK), :head_size]

    def values_at(chunk):
        return kv_held[rows_at(chunk, KEY_CHUNK), head_size:]

    def one_block(i, _):
        here = rows_at(i, block)
        ctx_of = jnp.where(i < own_blocks, ctx, ctx + 1 - 2 * core)
        start = meta[docs + own_blocks * ctx_of + lax.rem(i, own_blocks)] * block
        position = start + lax.rem(lax.broadcasted_iota(jnp.int32, (1, columns), 1), block)
        own_start = jnp.zeros((1, columns), jnp.int32)
        first = jnp.int32(0)
        for d in range(docs):
            doc_start = meta[d]
            own_start = jnp.maximum(own_start, jnp.where(position >= doc_start, doc_start, 0))
            first = jnp.maximum(first, jnp.where(start >= doc_start, doc_start, 0))
        lowest = first // KEY_CHUNK
        count = (start + block - 1) // KEY_CHUNK - lowest + 1

        def score(c, best):
            scores[c] = jnp.dot(
                keys_at(lowest + c),
                q_columns[i],
                preferred_element_type=jnp.float32,
            )
            first_key = (lowest + c) * KEY_CHUNK
            for at in range(0, KEY_CHUNK, STRIP):
                strip = slice(at, at + STRIP)
                key_pos = first_key + at + in_strip
                visible = (key_pos >= own_start) & (key_pos <= position)
                s = jnp.where(visible, scores[c, strip, :] * scale, NEGATIVE)
                scores[c, strip, :] = s
                best = jnp.maximum(best, jnp.max(s.reshape(STRIP // 8, 8, columns), axis=0))
            return best

        best = lax.fori_loop(
            0, count, score, jnp.full((8, columns), NEGATIVE, jnp.float32)
        )
        best = jnp.max(best, axis=0, keepdims=True)

        def mix(c, carried):
            total, acc = carried
            for at in range(0, KEY_CHUNK, STRIP):
                strip = slice(at, at + STRIP)
                w = jnp.exp(scores[c, strip, :] - best)
                scores[c, strip, :] = w
                low[0, strip, :] = w.astype(jnp.bfloat16)
                total = total + jnp.sum(w.reshape(STRIP // 8, 8, columns), axis=0)
            acc = acc + lax.dot_general(
                values_at(lowest + c),
                low[0],
                (((0,), (0,)), ((), ())),
                preferred_element_type=jnp.float32,
            )
            return total, acc

        total, acc = lax.fori_loop(
            0,
            count,
            mix,
            (jnp.zeros((8, columns), jnp.float32), jnp.zeros((head_size, columns), jnp.float32)),
        )
        total = jnp.sum(total, axis=0, keepdims=True)
        mixed = (acc / total).astype(jnp.bfloat16)
        expected = jnp.sum(
            mixed.astype(jnp.float32) * c_columns[i].astype(jnp.float32), axis=0, keepdims=True
        )
        per_total = 1.0 / total
        for h in range(heads):
            mixed_out[here, h * head_size : (h + 1) * head_size] = mixed[
                :, h * block : (h + 1) * block
            ].T

        def back(c, q_acc):
            chunk = rows_at(lowest + c, KEY_CHUNK)
            prob_grad[...] = jnp.dot(
                values_at(lowest + c), c_columns[i], preferred_element_type=jnp.float32
            )
            for at in range(0, KEY_CHUNK, STRIP):
                strip = slice(at, at + STRIP)
                probability = scores[c, strip, :] * per_total
                low[0, strip, :] = probability.astype(jnp.bfloat16)
                low[1, strip, :] = (probability * (prob_grad[strip, :] - expected)).astype(
                    jnp.bfloat16
                )
            value_acc[chunk, :] += jnp.dot(low[0], c_rows[i], preferred_element_type=jnp.float32)
            key_acc[chunk, :] += jnp.dot(low[1], q_rows[i], preferred_element_type=jnp.float32)
            return q_acc + lax.dot_general(
                keys_at(lowest + c),
                low[1],
                (((0,), (0,)), ((), ())),
                preferred_element_type=jnp.float32,
            )

        q_acc = lax.fori_loop(
            0, count, back, jnp.zeros((head_size, columns), jnp.float32)
        )
        q_grad = (q_acc * scale).astype(jnp.bfloat16)
        for h in range(heads):
            query_grad[here, h * head_size : (h + 1) * head_size] = q_grad[
                :, h * block : (h + 1) * block
            ].T
        return 0

    lax.fori_loop(0, 2 * own_blocks, one_block, 0)
    for _, core_of, out in sides:
        for j in range(blocks // 2):
            source = rows_at(true_block(core_of, j), block)
            part = slice(j * block, (j + 1) * block)
            out[part, :head_size] = (key_acc[source, :] * scale).astype(out.dtype)
            out[part, head_size:] = value_acc[source, :].astype(out.dtype)


def attention(meta, queries, cotangent, peer_both, kv_same, kv_other, head_size, docs, blocks):
    rows, width = queries.shape
    heads = width // head_size // 2
    length = kv_same.shape[0] + kv_other.shape[0]
    block = length // blocks
    columns = heads * block
    query_blocks = 2 * rows // block
    in_vmem = pl.BlockSpec(memory_space=pltpu.VMEM)
    most_chunks = 10
    visible = 9 * KEY_CHUNK
    return pl.pallas_call(
        functools.partial(
            attention_kernel, heads=heads, head_size=head_size, block=block, docs=docs, blocks=blocks
        ),
        out_shape=(
            jax.ShapeDtypeStruct((2 * rows, width // 2), jnp.bfloat16),
            jax.ShapeDtypeStruct((2 * rows, width // 2), jnp.bfloat16),
            jax.ShapeDtypeStruct(kv_same.shape, jnp.float32),
            jax.ShapeDtypeStruct(kv_other.shape, jnp.bfloat16),
        ),
        in_specs=[pl.BlockSpec(memory_space=pltpu.SMEM)] + [pl.BlockSpec(memory_space=pl.ANY)] * 5,
        out_specs=(in_vmem,) * 4,
        scratch_shapes=[
            pltpu.VMEM(queries.shape, jnp.bfloat16),
            pltpu.VMEM(cotangent.shape, jnp.bfloat16),
            pltpu.VMEM(peer_both.shape, jnp.bfloat16),
            pltpu.VMEM((length, 2 * head_size), jnp.bfloat16),
            pltpu.VMEM((length, head_size), jnp.float32),
            pltpu.VMEM((length, head_size), jnp.float32),
            pltpu.VMEM((most_chunks, KEY_CHUNK, columns), jnp.float32),
            pltpu.VMEM((KEY_CHUNK, columns), jnp.float32),
            pltpu.VMEM((2, KEY_CHUNK, columns), jnp.bfloat16),
            pltpu.VMEM((query_blocks, head_size, columns), jnp.bfloat16),
            pltpu.VMEM((query_blocks, head_size, columns), jnp.bfloat16),
            pltpu.VMEM((query_blocks, columns, head_size), jnp.bfloat16),
            pltpu.VMEM((query_blocks, columns, head_size), jnp.bfloat16),
            pltpu.SemaphoreType.DMA((5,)),
        ],
        compiler_params=pltpu.CompilerParams(vmem_limit_bytes=26 << 20),
        cost_estimate=pl.CostEstimate(
            flops=28 * rows * heads * visible * head_size,
            bytes_accessed=8 * rows * width + 8 * length * head_size,
            transcendentals=2 * rows * heads * visible,
        ),
        name="masked_attention",
    )(meta, queries, cotangent, peer_both, kv_same, kv_other)


def body(tokens, queries, cotangent, latent_key, latent_value, lengths, block_order):
    token_rows = tokens[0]
    rows_here, features = token_rows.shape
    head_size = latent_key.shape[1]
    docs, blocks = lengths.shape[1], block_order.shape[1]
    me = lax.axis_index(AXES)
    table = lax.dynamic_index_in_dim(jnp.asarray(block_table()), me, keepdims=False)
    before = np.arange(docs)[:, None] < np.arange(docs)[None, :]
    doc_starts = jnp.sum(jnp.where(before, lengths[0][:, None], 0), axis=0)
    meta = jnp.concatenate(
        [
            doc_starts.astype(jnp.int32),
            block_order[0],
            jnp.stack([lax.axis_index(CTX), lax.axis_index("core")]).astype(jnp.int32),
        ]
    )

    core = lax.axis_index("core")
    peer_both = swap_cores(
        jnp.concatenate(
            [
                lax.dynamic_slice_in_dim(a[0], (1 - core) * a.shape[2] // 2, a.shape[2] // 2, 1)
                for a in (queries, cotangent)
            ],
            axis=1,
        )
    )
    head_rows = latent_key.shape[0]
    latents = small(
        side_by_side_kernel,
        "pair_latents",
        jax.ShapeDtypeStruct((head_rows, 2 * head_size), jnp.float32),
        latent_key,
        latent_value,
    )
    latents = gather_ring(jnp.concatenate(gather_ring(latents, 0), axis=0), 1)
    latents[0], peer_both, meta = lax.optimization_barrier((latents[0], peer_both, meta))
    sums = small(
        magnitudes_kernel,
        "magnitudes",
        jax.ShapeDtypeStruct((8, 2 * head_size), jnp.float32),
        *latents,
    )
    sums = sum(gather_ring(sums, 2))
    sums = sums + swap_cores(sums)
    weights = small(
        functools.partial(ternary_kernel, entries=features * head_size),
        "ternarize",
        jax.ShapeDtypeStruct((16 * head_rows, 2 * head_size), jnp.bfloat16),
        sums,
        *latents,
    )
    weights, shuffle_table = lax.optimization_barrier((weights, table))
    weight_parts = gather_ring(weights, 2)
    tokens_own, tokens_other = shuffle(shuffle_table, token_rows)
    other_parts = [swap_cores(part) for part in weight_parts]
    part_rows = weights.shape[0]
    projected = 0.0
    for i, (own, other) in enumerate(zip(weight_parts, other_parts)):
        cut = slice(i * part_rows, (i + 1) * part_rows)
        for rows, part in ((tokens_own, own), (tokens_other, other)):
            projected = projected + jnp.dot(
                rows[:, cut], part, preferred_element_type=jnp.float32
            )
    kv_here = projected.astype(jnp.bfloat16)
    groups = lax.axis_size(SAME_CORE_CTX)
    kv_same = lax.all_to_all(
        jnp.broadcast_to(kv_here[None], (groups,) + kv_here.shape).reshape(-1, 2 * head_size),
        SAME_CORE_CTX,
        split_axis=0,
        concat_axis=0,
        tiled=True,
    )
    kv_other = swap_cores(kv_same)
    tokens_peer = swap_cores(tokens_other)

    mixed, query_grad, same_terms, other_terms = attention(
        meta, queries[0], cotangent[0], peer_both, kv_same, kv_other, head_size, docs, blocks
    )
    same_terms, other_terms, tokens_peer = lax.optimization_barrier(
        (same_terms, other_terms, tokens_peer)
    )
    chip_terms = (same_terms + swap_cores(other_terms).astype(jnp.float32)).astype(jnp.bfloat16)
    terms = lax.all_to_all(chip_terms, SAME_CORE_CTX, split_axis=0, concat_axis=0, tiled=True)
    grads = jnp.sum(
        terms.reshape(groups, rows_here, 2 * head_size).astype(jnp.float32), axis=0
    ).astype(jnp.bfloat16)
    peer_grads = swap_cores(grads)

    arrived = sent_along_ring(
        weight_terms(grads, peer_grads, tokens_own, tokens_peer, 1, 3, jnp.bfloat16), 2
    )
    (summed,) = weight_terms(grads, peer_grads, tokens_own, tokens_peer, 0, 1, jnp.float32)
    summed = summed + sum(piece.astype(jnp.float32) for piece in arrived)
    token_grad = token_gradient(table, grads, weight_parts + other_parts)
    summed, token_grad = lax.optimization_barrier((summed, token_grad))
    from_peer = swap_cores(jnp.concatenate([mixed[rows_here:], query_grad[rows_here:]], axis=1))

    def both_halves(own, peers):
        return jnp.concatenate(
            [jnp.where(core == 0, own, peers), jnp.where(core == 0, peers, own)], axis=1
        )

    half_width = mixed.shape[1]
    mixed = both_halves(mixed[:rows_here], from_peer[:, :half_width])
    query_grad = both_halves(query_grad[:rows_here], from_peer[:, half_width:])
    summed, *pieces = jnp.split(summed, 4, axis=1)
    summed = summed + sum(piece.astype(jnp.float32) for piece in sent_along_ring(pieces, 1))
    summed, *pieces = jnp.split(summed, 4, axis=1)
    half_shape = jax.ShapeDtypeStruct((head_rows, head_size), jnp.float32)
    key_grad, value_grad = small(
        last_sum_kernel, "last_sum", (half_shape, half_shape), summed, *sent_along_ring(pieces, 0)
    )
    return (
        mixed[None],
        query_grad[None],
        token_grad[None],
        key_grad,
        value_grad,
    )


def solution(mesh):
    torus = Mesh(mesh.devices.reshape(SIZES), AXES)
    whole = CTX + DP
    in_specs = (
        P(DP, CTX, None),
        P(DP, CTX, None),
        P(DP, CTX, None),
        P(whole, None),
        P(whole, None),
        P(DP, None),
        P(DP, None),
    )
    out_specs = (
        P(DP, CTX, None),
        P(DP, CTX, None),
        P(DP, CTX, None),
        P(whole, None),
        P(whole, None),
    )
    return jax.shard_map(body, mesh=torus, in_specs=in_specs, out_specs=out_specs, check_vma=False)
```

```python
import functools

import jax
import jax.numpy as jnp
import numpy as np
from jax import lax
from jax.experimental import pallas as pl
from jax.experimental.pallas import tpu as pltpu
from jax.sharding import Mesh
from jax.sharding import PartitionSpec as P

AXES = ("y", "zh", "core", "x", "zl")
SIZES = (4, 2, 2, 4, 2)
CTX = ("y", "zh", "core")
DP = ("x", "zl")
SAME_CORE_CTX = ("y", "zh")
DEVICES = int(np.prod(SIZES))

EPSILON = 1e-05
NEGATIVE = -1e30
KEY_CHUNK = 256
STRIP = 32

RING_ORDER = {0: ("x", "y", "z"), 1: ("y", "z", "x")}
OFFSETS = (0, -1, 1, 2)


def coordinates(device):
    y, zh, core, x, zl = (int(v) for v in np.unravel_index(device, SIZES))
    return {"y": y, "z": zh * 2 + zl, "x": x, "core": core}


def device_of(place):
    return int(
        np.ravel_multi_index(
            (place["y"], place["z"] // 2, place["core"], place["x"], place["z"] % 2), SIZES
        )
    )


def moved(change):
    pairs = []
    for device in range(DEVICES):
        place = coordinates(device)
        change(place)
        pairs.append((device, device_of(place)))
    return pairs


def along_ring(phase, step):
    def change(place):
        axis = RING_ORDER[place["core"]][phase]
        place[axis] = (place[axis] + step) % 4

    return moved(change)


def to_other_core(place):
    place["core"] = 1 - place["core"]


def swap_cores(value):
    return lax.ppermute(value, AXES, moved(to_other_core))


def block_table():
    table = np.zeros((DEVICES, DEVICES), np.int32)
    for device in range(DEVICES):
        here = coordinates(device)
        at = 0
        for core in (here["core"], 1 - here["core"]):
            order = RING_ORDER[core]
            for last in OFFSETS:
                for middle in OFFSETS:
                    for first in OFFSETS:
                        place = dict(here, core=core)
                        for axis, step in zip(order, (first, middle, last)):
                            place[axis] = (place[axis] + step) % 4
                        table[device, at] = device_of(place)
                        at += 1
    return table


def gather_ring(value, phase):
    return [value] + [
        lax.ppermute(value, AXES, along_ring(phase, -offset)) for offset in OFFSETS[1:]
    ]


def sent_along_ring(pieces, phase):
    return [
        lax.ppermute(piece.astype(jnp.bfloat16), AXES, along_ring(phase, offset))
        for piece, offset in zip(pieces, OFFSETS[1:])
    ]


def shuffle_kernel(table, tokens, own, other):
    width = own.shape[1] * 2 // DEVICES
    half = DEVICES // 2

    def move(j, _):
        target = pl.ds(pl.multiple_of(j * width, width), width)
        for first, out in ((0, own), (half, other)):
            source = pl.ds(pl.multiple_of(table[first + j] * width, width), width)
            out[:, target] = tokens[:, source]
        return 0

    lax.fori_loop(0, half, move, 0, unroll=8)


def shuffle(table, tokens):
    rows, features = tokens.shape
    step_rows = 32
    half = jax.ShapeDtypeStruct((rows, features // 2), tokens.dtype)
    half_spec = pl.BlockSpec((step_rows, features // 2), lambda i: (i, 0))
    return pl.pallas_call(
        shuffle_kernel,
        grid=(rows // step_rows,),
        out_shape=(half, half),
        in_specs=[
            pl.BlockSpec(memory_space=pltpu.SMEM),
            pl.BlockSpec((step_rows, features), lambda i: (i, 0)),
        ],
        out_specs=(half_spec, half_spec),
        compiler_params=pltpu.CompilerParams(vmem_limit_bytes=16 << 20),
        cost_estimate=pl.CostEstimate(
            flops=0, bytes_accessed=4 * rows * features, transcendentals=0
        ),
        name="shuffle_tokens",
    )(table, tokens)


def weight_terms_kernel(grads, peer_grads, tokens, peer_tokens, *rest, first, count):
    outs, (held_grads, turned, held, made, grad_sems, sems, out_sems) = rest[:count], rest[count:]
    grad_copies = [
        pltpu.make_async_copy(source, held_grads.at[side], grad_sems.at[side])
        for side, source in enumerate((grads, peer_grads))
    ]
    for copy in grad_copies:
        copy.start()
    step = held.shape[2] // (2 * count)
    copies = []
    for n in range(2 * count):
        here, there = slice(n * step, (n + 1) * step), slice(first + n * step, first + (n + 1) * step)
        copies.append(
            [
                pltpu.make_async_copy(source.at[:, there], held.at[side, :, here], sems.at[side, n])
                for side, source in enumerate((tokens, peer_tokens))
            ]
        )
    for pair in copies:
        for copy in pair:
            copy.start()
    for side, copy in enumerate(grad_copies):
        copy.wait()
        turned[side] = held_grads[side].T
    sends = []
    for n, pair in enumerate(copies):
        here = slice(n * step, (n + 1) * step)
        for copy in pair:
            copy.wait()
        term = jnp.dot(turned[0], held[0, :, here], preferred_element_type=jnp.float32) + jnp.dot(
            turned[1], held[1, :, here], preferred_element_type=jnp.float32
        )
        made[:, here] = term.astype(made.dtype)
        sends.append(
            pltpu.make_async_copy(
                made.at[:, here],
                outs[n // 2].at[:, n % 2 * step : (n % 2 + 1) * step],
                out_sems.at[n],
            )
        )
        sends[-1].start()
    for send in sends:
        send.wait()


def weight_terms(grads, peer_grads, tokens, peer_tokens, first, count, dtype):
    rows, features = tokens.shape
    both = grads.shape[1]
    width = features // len(OFFSETS)
    anywhere = pl.BlockSpec(memory_space=pl.ANY)
    return pl.pallas_call(
        functools.partial(weight_terms_kernel, first=first * width, count=count),
        out_shape=(jax.ShapeDtypeStruct((both, width), dtype),) * count,
        in_specs=[anywhere] * 4,
        out_specs=(anywhere,) * count,
        scratch_shapes=[
            pltpu.VMEM((2, rows, both), jnp.bfloat16),
            pltpu.VMEM((2, both, rows), jnp.bfloat16),
            pltpu.VMEM((2, rows, count * width), tokens.dtype),
            pltpu.VMEM((both, count * width), dtype),
            pltpu.SemaphoreType.DMA((2,)),
            pltpu.SemaphoreType.DMA((2, 2 * count)),
            pltpu.SemaphoreType.DMA((2 * count,)),
        ],
        compiler_params=pltpu.CompilerParams(vmem_limit_bytes=58 << 20),
        cost_estimate=pl.CostEstimate(
            flops=4 * rows * both * count * width,
            bytes_accessed=(4 * rows + 2 * both) * count * width,
            transcendentals=0,
        ),
        name="weight_terms",
    )(grads, peer_grads, tokens, peer_tokens)


def pair_kernel(left, right, out, sems):
    width = left.shape[1]
    copies = [
        pltpu.make_async_copy(source, out.at[:, n * width : (n + 1) * width], sems.at[n])
        for n, source in enumerate((left, right))
    ]
    for copy in copies:
        copy.start()
    for copy in copies:
        copy.wait()


def side_by_side(left, right):
    anywhere = pl.BlockSpec(memory_space=pl.ANY)
    return pl.pallas_call(
        pair_kernel,
        out_shape=jax.ShapeDtypeStruct((left.shape[0], 2 * left.shape[1]), left.dtype),
        in_specs=[anywhere, anywhere],
        out_specs=pl.BlockSpec(memory_space=pltpu.VMEM),
        scratch_shapes=[pltpu.SemaphoreType.DMA((2,))],
        compiler_params=pltpu.CompilerParams(vmem_limit_bytes=58 << 20),
        name="pair_latents",
    )(left, right)


def magnitudes_kernel(*refs):
    pieces, out = refs[:-1], refs[-1]
    out[...] = sum(
        jnp.sum(jnp.abs(piece[...]).reshape(-1, *out.shape), axis=0) for piece in pieces
    )


def ternary_kernel(sums, *refs, entries):
    pieces, out = refs[:-1], refs[-1]
    half = out.shape[1] // 2
    for columns in (slice(0, half), slice(half, 2 * half)):
        scale = jnp.sum(sums[:, columns]) / entries + EPSILON
        level = jnp.full((1, half), scale, jnp.float32)
        for n, piece in enumerate(pieces):
            rows = piece.shape[0]
            latent = piece[:, columns]
            out[n * rows : (n + 1) * rows, columns] = jnp.where(
                latent >= 0.5 * level, level, jnp.where(latent <= -0.5 * level, -level, 0.0)
            ).astype(jnp.bfloat16)


def last_sum_kernel(own, first, second, third, key_out, value_out):
    total = own[...]
    for piece in (first, second, third):
        total = total + piece[...].astype(jnp.float32)
    half = key_out.shape[1]
    key_out[...] = total[:half].T
    value_out[...] = total[half:].T


def small(kernel, name, out_shape, *args):
    in_vmem = pl.BlockSpec(memory_space=pltpu.VMEM)
    return pl.pallas_call(
        kernel,
        out_shape=out_shape,
        in_specs=[in_vmem] * len(args),
        out_specs=jax.tree.map(lambda _: in_vmem, out_shape),
        compiler_params=pltpu.CompilerParams(vmem_limit_bytes=12 << 20),
        cost_estimate=pl.CostEstimate(
            flops=0, bytes_accessed=sum(a.size * a.dtype.itemsize for a in args), transcendentals=0
        ),
        name=name,
    )(*args)


def token_grad_kernel(table, grads, *rest, count):
    weights, out = rest[:count], rest[count]
    held, held_sems, buffers, sems = rest[count + 1 :]
    slots, step_width = held.shape[:2]
    width = out.shape[1] // DEVICES
    per_step = step_width // width
    steps_each = weights[0].shape[0] // step_width

    def fetch(step):
        part = (step % steps_each) * step_width
        return pltpu.make_async_copy(
            weights[step // steps_each].at[part : part + step_width, :],
            held.at[step % slots],
            held_sems.at[step % slots],
        )

    for step in range(slots - 1):
        fetch(step).start()
    for step in range(count * steps_each):
        slot = step % 2
        buffer, sem = buffers.at[slot], sems.at[slot]
        if step + slots - 1 < count * steps_each:
            fetch(step + slots - 1).start()
        fetch(step).wait()
        if step >= 2:
            pltpu.make_async_copy(buffer, buffer, sem).wait()
        buffers[slot] = lax.dot_general(
            grads[...],
            held[step % slots],
            (((1,), (1,)), ((), ())),
            preferred_element_type=jnp.float32,
        ).astype(jnp.bfloat16)
        for j in range(per_step):
            target = pl.ds(pl.multiple_of(table[step * per_step + j] * width, width), width)
            pltpu.make_async_copy(
                buffer.at[:, j * width : (j + 1) * width], out.at[:, target], sem
            ).start()
    for slot in range(2):
        pltpu.make_async_copy(buffers.at[slot], buffers.at[slot], sems.at[slot]).wait()


def token_gradient(table, grads, weights):
    rows, both = grads.shape
    features = sum(w.shape[0] for w in weights)
    step_width = 1024
    slots = 4
    return pl.pallas_call(
        functools.partial(token_grad_kernel, count=len(weights)),
        out_shape=jax.ShapeDtypeStruct((rows, features), jnp.bfloat16),
        in_specs=[
            pl.BlockSpec(memory_space=pltpu.SMEM),
            pl.BlockSpec(memory_space=pltpu.VMEM),
        ]
        + [pl.BlockSpec(memory_space=pltpu.HBM)] * len(weights),
        out_specs=pl.BlockSpec(memory_space=pl.ANY),
        scratch_shapes=[
            pltpu.VMEM((slots, step_width, both), jnp.bfloat16),
            pltpu.SemaphoreType.DMA((slots,)),
            pltpu.VMEM((2, rows, step_width), jnp.bfloat16),
            pltpu.SemaphoreType.DMA((2,)),
        ],
        compiler_params=pltpu.CompilerParams(vmem_limit_bytes=58 << 20),
        cost_estimate=pl.CostEstimate(
            flops=2 * rows * both * features,
            bytes_accessed=2 * features * (rows + both),
            transcendentals=0,
        ),
        name="token_gradient",
    )(table, grads, *weights)


def attention_kernel(
    meta, queries, cotangent, peer_both, kv_same, kv_other,
    mixed_out, query_grad, same_out, other_out,
    q_held, c_held, peer_held, kv_held, key_acc, value_acc, scores, prob_grad, low,
    q_columns, c_columns, q_rows, c_rows, sems,
    *, heads, head_size, block, docs, blocks,
):
    scale = head_size ** (-0.5)
    columns = heads * block
    ctx, core = meta[docs + blocks], meta[docs + blocks + 1]
    own_blocks = q_held.shape[0] // block
    in_strip = lax.broadcasted_iota(jnp.int32, (STRIP, columns), 0)
    sides = ((kv_same, core, same_out), (kv_other, 1 - core, other_out))

    def rows_at(index, size):
        return pl.ds(pl.multiple_of(index * size, size), size)

    def true_block(core_of, j):
        return meta[docs + ((j // 2) * 2 + core_of) * 2 + j % 2]

    copies = [
        pltpu.make_async_copy(source, held, sems.at[n])
        for n, (source, held) in enumerate(
            ((queries, q_held), (cotangent, c_held), (peer_both, peer_held))
        )
    ]
    for copy in copies:
        copy.start()
    for n, (ref, core_of, _) in enumerate(sides):
        for j in range(blocks // 2):
            pltpu.make_async_copy(
                ref.at[j * block : (j + 1) * block, :],
                kv_held.at[rows_at(true_block(core_of, j) + 1, block), :],
                sems.at[len(copies) + n],
            ).start()
    kv_held[:block, :] = jnp.zeros((block, 2 * head_size), kv_held.dtype)
    key_acc[...] = jnp.zeros_like(key_acc)
    value_acc[...] = jnp.zeros_like(value_acc)
    for copy in copies:
        copy.wait()
    for i in range(2 * own_blocks):
        here = slice(i % own_blocks * block, (i % own_blocks + 1) * block)
        for h in range(heads):
            part = slice(h * block, (h + 1) * block)
            if i < own_blocks:
                head = rows_at(core * heads + h, head_size)
                q, c = q_held[here, head], c_held[here, head]
            else:
                q = peer_held[here, h * head_size : (h + 1) * head_size]
                c = peer_held[here, (heads + h) * head_size : (heads + h + 1) * head_size]
            q_rows[i, part, :], c_rows[i, part, :] = q, c
            q_columns[i, :, part], c_columns[i, :, part] = q.T, c.T
    for n, (ref, _, _) in enumerate(sides):
        pltpu.make_async_copy(
            ref, kv_held.at[: blocks // 2 * block, :], sems.at[len(copies) + n]
        ).wait()

    def chunk_rows(last, c):
        return pl.ds(pl.multiple_of((last - 2 * c) * block, block), 2 * block)

    def one_block(i, _):
        here = rows_at(i, block)
        ctx_of = jnp.where(i < own_blocks, ctx, ctx + 1 - 2 * core)
        last = meta[docs + own_blocks * ctx_of + lax.rem(i, own_blocks)]
        start = last * block
        position = start + lax.rem(lax.broadcasted_iota(jnp.int32, (1, columns), 1), block)
        own_start = jnp.zeros((1, columns), jnp.int32)
        first = jnp.int32(0)
        for d in range(docs):
            doc_start = meta[d]
            own_start = jnp.maximum(own_start, jnp.where(position >= doc_start, doc_start, 0))
            first = jnp.maximum(first, jnp.where(start >= doc_start, doc_start, 0))
        count = (last - first // block) // 2 + 1

        def score(c, best):
            scores[c] = jnp.dot(
                kv_held[chunk_rows(last, c), :head_size],
                q_columns[i],
                preferred_element_type=jnp.float32,
            )
            first_key = (last - 2 * c - 1) * block
            for at in range(0, KEY_CHUNK, STRIP):
                strip = slice(at, at + STRIP)
                key_pos = first_key + at + in_strip
                visible = (key_pos >= own_start) & (key_pos <= position)
                s = jnp.where(visible, scores[c, strip, :] * scale, NEGATIVE)
                scores[c, strip, :] = s
                best = jnp.maximum(best, jnp.max(s.reshape(STRIP // 8, 8, columns), axis=0))
            return best

        best = lax.fori_loop(
            0, count, score, jnp.full((8, columns), NEGATIVE, jnp.float32)
        )
        best = jnp.max(best, axis=0, keepdims=True)

        def mix(c, carried):
            total, acc = carried
            for at in range(0, KEY_CHUNK, STRIP):
                strip = slice(at, at + STRIP)
                w = jnp.exp(scores[c, strip, :] - best)
                scores[c, strip, :] = w
                low[0, strip, :] = w.astype(jnp.bfloat16)
                total = total + jnp.sum(w.reshape(STRIP // 8, 8, columns), axis=0)
            acc = acc + lax.dot_general(
                kv_held[chunk_rows(last, c), head_size:],
                low[0],
                (((0,), (0,)), ((), ())),
                preferred_element_type=jnp.float32,
            )
            return total, acc

        total, acc = lax.fori_loop(
            0,
            count,
            mix,
            (jnp.zeros((8, columns), jnp.float32), jnp.zeros((head_size, columns), jnp.float32)),
        )
        total = jnp.sum(total, axis=0, keepdims=True)
        mixed = (acc / total).astype(jnp.bfloat16)
        expected = jnp.sum(
            mixed.astype(jnp.float32) * c_columns[i].astype(jnp.float32), axis=0, keepdims=True
        )
        per_total = 1.0 / total
        for h in range(heads):
            mixed_out[here, h * head_size : (h + 1) * head_size] = mixed[
                :, h * block : (h + 1) * block
            ].T

        def back(c, q_acc):
            chunk = chunk_rows(last, c)
            prob_grad[...] = jnp.dot(
                kv_held[chunk, head_size:], c_columns[i], preferred_element_type=jnp.float32
            )
            for at in range(0, KEY_CHUNK, STRIP):
                strip = slice(at, at + STRIP)
                probability = scores[c, strip, :] * per_total
                low[0, strip, :] = probability.astype(jnp.bfloat16)
                low[1, strip, :] = (probability * (prob_grad[strip, :] - expected)).astype(
                    jnp.bfloat16
                )
            value_acc[chunk, :] += jnp.dot(low[0], c_rows[i], preferred_element_type=jnp.float32)
            key_acc[chunk, :] += jnp.dot(low[1], q_rows[i], preferred_element_type=jnp.float32)
            return q_acc + lax.dot_general(
                kv_held[chunk, :head_size],
                low[1],
                (((0,), (0,)), ((), ())),
                preferred_element_type=jnp.float32,
            )

        q_acc = lax.fori_loop(
            0, count, back, jnp.zeros((head_size, columns), jnp.float32)
        )
        q_grad = (q_acc * scale).astype(jnp.bfloat16)
        for h in range(heads):
            query_grad[here, h * head_size : (h + 1) * head_size] = q_grad[
                :, h * block : (h + 1) * block
            ].T
        return 0

    lax.fori_loop(0, 2 * own_blocks, one_block, 0)
    for _, core_of, out in sides:
        for j in range(blocks // 2):
            source = rows_at(true_block(core_of, j) + 1, block)
            part = slice(j * block, (j + 1) * block)
            out[part, :head_size] = (key_acc[source, :] * scale).astype(out.dtype)
            out[part, head_size:] = value_acc[source, :].astype(out.dtype)


def attention(meta, queries, cotangent, peer_both, kv_same, kv_other, head_size, docs, blocks):
    rows, width = queries.shape
    heads = width // head_size // 2
    length = kv_same.shape[0] + kv_other.shape[0]
    block = length // blocks
    columns = heads * block
    query_blocks = 2 * rows // block
    in_vmem = pl.BlockSpec(memory_space=pltpu.VMEM)
    most_chunks = 10
    visible = 9 * KEY_CHUNK
    return pl.pallas_call(
        functools.partial(
            attention_kernel, heads=heads, head_size=head_size, block=block, docs=docs, blocks=blocks
        ),
        out_shape=(
            jax.ShapeDtypeStruct((2 * rows, width // 2), jnp.bfloat16),
            jax.ShapeDtypeStruct((2 * rows, width // 2), jnp.bfloat16),
            jax.ShapeDtypeStruct(kv_same.shape, jnp.float32),
            jax.ShapeDtypeStruct(kv_other.shape, jnp.bfloat16),
        ),
        in_specs=[pl.BlockSpec(memory_space=pltpu.SMEM)] + [pl.BlockSpec(memory_space=pl.ANY)] * 5,
        out_specs=(in_vmem,) * 4,
        scratch_shapes=[
            pltpu.VMEM(queries.shape, jnp.bfloat16),
            pltpu.VMEM(cotangent.shape, jnp.bfloat16),
            pltpu.VMEM(peer_both.shape, jnp.bfloat16),
            pltpu.VMEM((block + length, 2 * head_size), jnp.bfloat16),
            pltpu.VMEM((block + length, head_size), jnp.float32),
            pltpu.VMEM((block + length, head_size), jnp.float32),
            pltpu.VMEM((most_chunks, KEY_CHUNK, columns), jnp.float32),
            pltpu.VMEM((KEY_CHUNK, columns), jnp.float32),
            pltpu.VMEM((2, KEY_CHUNK, columns), jnp.bfloat16),
            pltpu.VMEM((query_blocks, head_size, columns), jnp.bfloat16),
            pltpu.VMEM((query_blocks, head_size, columns), jnp.bfloat16),
            pltpu.VMEM((query_blocks, columns, head_size), jnp.bfloat16),
            pltpu.VMEM((query_blocks, columns, head_size), jnp.bfloat16),
            pltpu.SemaphoreType.DMA((5,)),
        ],
        compiler_params=pltpu.CompilerParams(vmem_limit_bytes=26 << 20),
        cost_estimate=pl.CostEstimate(
            flops=28 * rows * heads * visible * head_size,
            bytes_accessed=8 * rows * width + 8 * length * head_size,
            transcendentals=2 * rows * heads * visible,
        ),
        name="masked_attention",
    )(meta, queries, cotangent, peer_both, kv_same, kv_other)


def body(tokens, queries, cotangent, latent_key, latent_value, lengths, block_order):
    token_rows = tokens[0]
    rows_here, features = token_rows.shape
    head_size = latent_key.shape[1]
    docs, blocks = lengths.shape[1], block_order.shape[1]
    me = lax.axis_index(AXES)
    table = lax.dynamic_index_in_dim(jnp.asarray(block_table()), me, keepdims=False)
    before = np.arange(docs)[:, None] < np.arange(docs)[None, :]
    doc_starts = jnp.sum(jnp.where(before, lengths[0][:, None], 0), axis=0)
    meta = jnp.concatenate(
        [
            doc_starts.astype(jnp.int32),
            block_order[0],
            jnp.stack([lax.axis_index(CTX), lax.axis_index("core")]).astype(jnp.int32),
        ]
    )

    core = lax.axis_index("core")
    peer_both = swap_cores(
        jnp.concatenate(
            [
                lax.dynamic_slice_in_dim(a[0], (1 - core) * a.shape[2] // 2, a.shape[2] // 2, 1)
                for a in (queries, cotangent)
            ],
            axis=1,
        )
    )
    head_rows = latent_key.shape[0]
    latents = side_by_side(latent_key, latent_value)
    latents = gather_ring(jnp.concatenate(gather_ring(latents, 0), axis=0), 1)
    latents[0], peer_both, meta = lax.optimization_barrier((latents[0], peer_both, meta))
    sums = small(
        magnitudes_kernel,
        "magnitudes",
        jax.ShapeDtypeStruct((8, 2 * head_size), jnp.float32),
        *latents,
    )
    sums = sum(gather_ring(sums, 2))
    sums = sums + swap_cores(sums)
    weights = small(
        functools.partial(ternary_kernel, entries=features * head_size),
        "ternarize",
        jax.ShapeDtypeStruct((16 * head_rows, 2 * head_size), jnp.bfloat16),
        sums,
        *latents,
    )
    weights, shuffle_table = lax.optimization_barrier((weights, table))
    weight_parts = gather_ring(weights, 2)
    tokens_own, tokens_other = shuffle(shuffle_table, token_rows)
    other_parts = [swap_cores(part) for part in weight_parts]
    part_rows = weights.shape[0]
    projected = 0.0
    for i, (own, other) in enumerate(zip(weight_parts, other_parts)):
        cut = slice(i * part_rows, (i + 1) * part_rows)
        for rows, part in ((tokens_own, own), (tokens_other, other)):
            projected = projected + jnp.dot(
                rows[:, cut], part, preferred_element_type=jnp.float32
            )
    kv_here = projected.astype(jnp.bfloat16)
    groups = lax.axis_size(SAME_CORE_CTX)
    kv_same = lax.all_to_all(
        jnp.broadcast_to(kv_here[None], (groups,) + kv_here.shape).reshape(-1, 2 * head_size),
        SAME_CORE_CTX,
        split_axis=0,
        concat_axis=0,
        tiled=True,
    )
    kv_other = swap_cores(kv_same)
    tokens_peer = swap_cores(tokens_other)

    mixed, query_grad, same_terms, other_terms = attention(
        meta, queries[0], cotangent[0], peer_both, kv_same, kv_other, head_size, docs, blocks
    )
    same_terms, other_terms, tokens_peer = lax.optimization_barrier(
        (same_terms, other_terms, tokens_peer)
    )
    chip_terms = (same_terms + swap_cores(other_terms).astype(jnp.float32)).astype(jnp.bfloat16)
    terms = lax.all_to_all(chip_terms, SAME_CORE_CTX, split_axis=0, concat_axis=0, tiled=True)
    grads = jnp.sum(
        terms.reshape(groups, rows_here, 2 * head_size).astype(jnp.float32), axis=0
    ).astype(jnp.bfloat16)
    peer_grads = swap_cores(grads)

    arrived = sent_along_ring(
        weight_terms(grads, peer_grads, tokens_own, tokens_peer, 1, 3, jnp.bfloat16), 2
    )
    (summed,) = weight_terms(grads, peer_grads, tokens_own, tokens_peer, 0, 1, jnp.float32)
    summed = summed + sum(piece.astype(jnp.float32) for piece in arrived)
    token_grad = token_gradient(table, grads, weight_parts + other_parts)
    summed, token_grad = lax.optimization_barrier((summed, token_grad))
    from_peer = swap_cores(jnp.concatenate([mixed[rows_here:], query_grad[rows_here:]], axis=1))

    def both_halves(own, peers):
        return jnp.concatenate(
            [jnp.where(core == 0, own, peers), jnp.where(core == 0, peers, own)], axis=1
        )

    half_width = mixed.shape[1]
    mixed = both_halves(mixed[:rows_here], from_peer[:, :half_width])
    query_grad = both_halves(query_grad[:rows_here], from_peer[:, half_width:])
    summed, *pieces = jnp.split(summed, 4, axis=1)
    summed = summed + sum(piece.astype(jnp.float32) for piece in sent_along_ring(pieces, 1))
    summed, *pieces = jnp.split(summed, 4, axis=1)
    half_shape = jax.ShapeDtypeStruct((head_rows, head_size), jnp.float32)
    key_grad, value_grad = small(
        last_sum_kernel, "last_sum", (half_shape, half_shape), summed, *sent_along_ring(pieces, 0)
    )
    return (
        mixed[None],
        query_grad[None],
        token_grad[None],
        key_grad,
        value_grad,
    )


def solution(mesh):
    torus = Mesh(mesh.devices.reshape(SIZES), AXES)
    whole = CTX + DP
    in_specs = (
        P(DP, CTX, None),
        P(DP, CTX, None),
        P(DP, CTX, None),
        P(whole, None),
        P(whole, None),
        P(DP, None),
        P(DP, None),
    )
    out_specs = (
        P(DP, CTX, None),
        P(DP, CTX, None),
        P(DP, CTX, None),
        P(whole, None),
        P(whole, None),
    )
    return jax.shard_map(body, mesh=torus, in_specs=in_specs, out_specs=out_specs, check_vma=False)
```

```python
import functools

import jax
import jax.numpy as jnp
import numpy as np
from jax import lax
from jax.experimental import pallas as pl
from jax.experimental.pallas import tpu as pltpu
from jax.sharding import Mesh
from jax.sharding import PartitionSpec as P

AXES = ("y", "zh", "core", "x", "zl")
SIZES = (4, 2, 2, 4, 2)
CTX = ("y", "zh", "core")
DP = ("x", "zl")
SAME_CORE_CTX = ("y", "zh")
DEVICES = int(np.prod(SIZES))

EPSILON = 1e-05
NEGATIVE = -1e30
KEY_CHUNK = 256
STRIP = 32

RING_ORDER = {0: ("x", "y", "z"), 1: ("y", "z", "x")}
OFFSETS = (0, -1, 1, 2)


def coordinates(device):
    y, zh, core, x, zl = (int(v) for v in np.unravel_index(device, SIZES))
    return {"y": y, "z": zh * 2 + zl, "x": x, "core": core}


def device_of(place):
    return int(
        np.ravel_multi_index(
            (place["y"], place["z"] // 2, place["core"], place["x"], place["z"] % 2), SIZES
        )
    )


def moved(change):
    pairs = []
    for device in range(DEVICES):
        place = coordinates(device)
        change(place)
        pairs.append((device, device_of(place)))
    return pairs


def along_ring(phase, step):
    def change(place):
        axis = RING_ORDER[place["core"]][phase]
        place[axis] = (place[axis] + step) % 4

    return moved(change)


def to_other_core(place):
    place["core"] = 1 - place["core"]


def swap_cores(value):
    return lax.ppermute(value, AXES, moved(to_other_core))


def block_table():
    table = np.zeros((DEVICES, DEVICES), np.int32)
    for device in range(DEVICES):
        here = coordinates(device)
        at = 0
        for core in (here["core"], 1 - here["core"]):
            order = RING_ORDER[core]
            for last in OFFSETS:
                for middle in OFFSETS:
                    for first in OFFSETS:
                        place = dict(here, core=core)
                        for axis, step in zip(order, (first, middle, last)):
                            place[axis] = (place[axis] + step) % 4
                        table[device, at] = device_of(place)
                        at += 1
    return table


def gather_ring(value, phase):
    return [value] + [
        lax.ppermute(value, AXES, along_ring(phase, -offset)) for offset in OFFSETS[1:]
    ]


def sent_along_ring(pieces, phase, offsets=OFFSETS[1:]):
    return [
        lax.ppermute(piece.astype(jnp.bfloat16), AXES, along_ring(phase, offset))
        for piece, offset in zip(pieces, offsets)
    ]


def shuffle_kernel(table, tokens, own, other):
    width = own.shape[1] * 2 // DEVICES
    half = DEVICES // 2

    def move(j, _):
        target = pl.ds(pl.multiple_of(j * width, width), width)
        for first, out in ((0, own), (half, other)):
            source = pl.ds(pl.multiple_of(table[first + j] * width, width), width)
            out[:, target] = tokens[:, source]
        return 0

    lax.fori_loop(0, half, move, 0, unroll=8)


def shuffle(table, tokens):
    rows, features = tokens.shape
    step_rows = 32
    half = jax.ShapeDtypeStruct((rows, features // 2), tokens.dtype)
    half_spec = pl.BlockSpec((step_rows, features // 2), lambda i: (i, 0))
    return pl.pallas_call(
        shuffle_kernel,
        grid=(rows // step_rows,),
        out_shape=(half, half),
        in_specs=[
            pl.BlockSpec(memory_space=pltpu.SMEM),
            pl.BlockSpec((step_rows, features), lambda i: (i, 0)),
        ],
        out_specs=(half_spec, half_spec),
        compiler_params=pltpu.CompilerParams(vmem_limit_bytes=16 << 20),
        cost_estimate=pl.CostEstimate(
            flops=0, bytes_accessed=4 * rows * features, transcendentals=0
        ),
        name="shuffle_tokens",
    )(table, tokens)


def weight_terms_kernel(grads, peer_grads, tokens, peer_tokens, *rest, first, count):
    outs, (held_grads, turned, held, made, grad_sems, sems, out_sems) = rest[:count], rest[count:]
    grad_copies = [
        pltpu.make_async_copy(source, held_grads.at[side], grad_sems.at[side])
        for side, source in enumerate((grads, peer_grads))
    ]
    for copy in grad_copies:
        copy.start()
    step = held.shape[2] // (2 * count)
    copies = []
    for n in range(2 * count):
        here, there = slice(n * step, (n + 1) * step), slice(first + n * step, first + (n + 1) * step)
        copies.append(
            [
                pltpu.make_async_copy(source.at[:, there], held.at[side, :, here], sems.at[side, n])
                for side, source in enumerate((tokens, peer_tokens))
            ]
        )
    for pair in copies:
        for copy in pair:
            copy.start()
    for side, copy in enumerate(grad_copies):
        copy.wait()
        turned[side] = held_grads[side].T
    sends = []
    for n, pair in enumerate(copies):
        here = slice(n * step, (n + 1) * step)
        for copy in pair:
            copy.wait()
        term = jnp.dot(turned[0], held[0, :, here], preferred_element_type=jnp.float32) + jnp.dot(
            turned[1], held[1, :, here], preferred_element_type=jnp.float32
        )
        made[:, here] = term.astype(made.dtype)
        sends.append(
            pltpu.make_async_copy(
                made.at[:, here],
                outs[n // 2].at[:, n % 2 * step : (n % 2 + 1) * step],
                out_sems.at[n],
            )
        )
        sends[-1].start()
    for send in sends:
        send.wait()


def weight_terms(grads, peer_grads, tokens, peer_tokens, first, count, dtype):
    rows, features = tokens.shape
    both = grads.shape[1]
    width = features // len(OFFSETS)
    anywhere = pl.BlockSpec(memory_space=pl.ANY)
    return pl.pallas_call(
        functools.partial(weight_terms_kernel, first=first * width, count=count),
        out_shape=(jax.ShapeDtypeStruct((both, width), dtype),) * count,
        in_specs=[anywhere] * 4,
        out_specs=(anywhere,) * count,
        scratch_shapes=[
            pltpu.VMEM((2, rows, both), jnp.bfloat16),
            pltpu.VMEM((2, both, rows), jnp.bfloat16),
            pltpu.VMEM((2, rows, count * width), tokens.dtype),
            pltpu.VMEM((both, count * width), dtype),
            pltpu.SemaphoreType.DMA((2,)),
            pltpu.SemaphoreType.DMA((2, 2 * count)),
            pltpu.SemaphoreType.DMA((2 * count,)),
        ],
        compiler_params=pltpu.CompilerParams(vmem_limit_bytes=58 << 20),
        cost_estimate=pl.CostEstimate(
            flops=4 * rows * both * count * width,
            bytes_accessed=(4 * rows + 2 * both) * count * width,
            transcendentals=0,
        ),
        name="weight_terms",
    )(grads, peer_grads, tokens, peer_tokens)


def pair_kernel(left, right, out, sems):
    width = left.shape[1]
    copies = [
        pltpu.make_async_copy(source, out.at[:, n * width : (n + 1) * width], sems.at[n])
        for n, source in enumerate((left, right))
    ]
    for copy in copies:
        copy.start()
    for copy in copies:
        copy.wait()


def side_by_side(left, right):
    anywhere = pl.BlockSpec(memory_space=pl.ANY)
    return pl.pallas_call(
        pair_kernel,
        out_shape=jax.ShapeDtypeStruct((left.shape[0], 2 * left.shape[1]), left.dtype),
        in_specs=[anywhere, anywhere],
        out_specs=pl.BlockSpec(memory_space=pltpu.VMEM),
        scratch_shapes=[pltpu.SemaphoreType.DMA((2,))],
        compiler_params=pltpu.CompilerParams(vmem_limit_bytes=58 << 20),
        name="pair_latents",
    )(left, right)


def magnitudes_kernel(*refs):
    pieces, out = refs[:-1], refs[-1]
    out[...] = sum(
        jnp.sum(jnp.abs(piece[...]).reshape(-1, *out.shape), axis=0) for piece in pieces
    )


def ternary_kernel(sums, *refs, entries):
    pieces, out = refs[:-1], refs[-1]
    half = out.shape[1] // 2
    for columns in (slice(0, half), slice(half, 2 * half)):
        scale = jnp.sum(sums[:, columns]) / entries + EPSILON
        level = jnp.full((1, half), scale, jnp.float32)
        for n, piece in enumerate(pieces):
            rows = piece.shape[0]
            latent = piece[:, columns]
            out[n * rows : (n + 1) * rows, columns] = jnp.where(
                latent >= 0.5 * level, level, jnp.where(latent <= -0.5 * level, -level, 0.0)
            ).astype(jnp.bfloat16)


def last_sum_kernel(own, first, second, third, key_out, value_out):
    total = own[...]
    for piece in (first, second, third):
        total = total + piece[...].astype(jnp.float32)
    half = key_out.shape[1]
    key_out[...] = total[:half].T
    value_out[...] = total[half:].T


def small(kernel, name, out_shape, *args):
    in_vmem = pl.BlockSpec(memory_space=pltpu.VMEM)
    return pl.pallas_call(
        kernel,
        out_shape=out_shape,
        in_specs=[in_vmem] * len(args),
        out_specs=jax.tree.map(lambda _: in_vmem, out_shape),
        compiler_params=pltpu.CompilerParams(vmem_limit_bytes=12 << 20),
        cost_estimate=pl.CostEstimate(
            flops=0, bytes_accessed=sum(a.size * a.dtype.itemsize for a in args), transcendentals=0
        ),
        name=name,
    )(*args)


def token_grad_kernel(table, grads, *rest, count):
    weights, out = rest[:count], rest[count]
    held, held_sems, buffers, sems = rest[count + 1 :]
    slots, step_width = held.shape[:2]
    width = out.shape[1] // DEVICES
    per_step = step_width // width
    steps_each = weights[0].shape[0] // step_width

    def fetch(step):
        part = (step % steps_each) * step_width
        return pltpu.make_async_copy(
            weights[step // steps_each].at[part : part + step_width, :],
            held.at[step % slots],
            held_sems.at[step % slots],
        )

    for step in range(slots - 1):
        fetch(step).start()
    for step in range(count * steps_each):
        slot = step % 2
        buffer, sem = buffers.at[slot], sems.at[slot]
        if step + slots - 1 < count * steps_each:
            fetch(step + slots - 1).start()
        fetch(step).wait()
        if step >= 2:
            pltpu.make_async_copy(buffer, buffer, sem).wait()
        buffers[slot] = lax.dot_general(
            grads[...],
            held[step % slots],
            (((1,), (1,)), ((), ())),
            preferred_element_type=jnp.float32,
        ).astype(jnp.bfloat16)
        for j in range(per_step):
            target = pl.ds(pl.multiple_of(table[step * per_step + j] * width, width), width)
            pltpu.make_async_copy(
                buffer.at[:, j * width : (j + 1) * width], out.at[:, target], sem
            ).start()
    for slot in range(2):
        pltpu.make_async_copy(buffers.at[slot], buffers.at[slot], sems.at[slot]).wait()


def token_gradient(table, grads, weights):
    rows, both = grads.shape
    features = sum(w.shape[0] for w in weights)
    step_width = 1024
    slots = 4
    return pl.pallas_call(
        functools.partial(token_grad_kernel, count=len(weights)),
        out_shape=jax.ShapeDtypeStruct((rows, features), jnp.bfloat16),
        in_specs=[
            pl.BlockSpec(memory_space=pltpu.SMEM),
            pl.BlockSpec(memory_space=pltpu.VMEM),
        ]
        + [pl.BlockSpec(memory_space=pltpu.HBM)] * len(weights),
        out_specs=pl.BlockSpec(memory_space=pl.ANY),
        scratch_shapes=[
            pltpu.VMEM((slots, step_width, both), jnp.bfloat16),
            pltpu.SemaphoreType.DMA((slots,)),
            pltpu.VMEM((2, rows, step_width), jnp.bfloat16),
            pltpu.SemaphoreType.DMA((2,)),
        ],
        compiler_params=pltpu.CompilerParams(vmem_limit_bytes=58 << 20),
        cost_estimate=pl.CostEstimate(
            flops=2 * rows * both * features,
            bytes_accessed=2 * features * (rows + both),
            transcendentals=0,
        ),
        name="token_gradient",
    )(table, grads, *weights)


def attention_kernel(
    meta, queries, cotangent, peer_both, kv_same, kv_other,
    mixed_out, query_grad, same_out, other_out,
    q_held, c_held, peer_held, kv_held, key_acc, value_acc, scores, prob_grad, low,
    q_columns, c_columns, q_rows, c_rows, sems,
    *, heads, head_size, block, docs, blocks,
):
    scale = head_size ** (-0.5)
    columns = heads * block
    ctx, core = meta[docs + blocks], meta[docs + blocks + 1]
    own_blocks = q_held.shape[0] // block
    in_strip = lax.broadcasted_iota(jnp.int32, (STRIP, columns), 0)
    sides = ((kv_same, core, same_out), (kv_other, 1 - core, other_out))

    def rows_at(index, size):
        return pl.ds(pl.multiple_of(index * size, size), size)

    def true_block(core_of, j):
        return meta[docs + ((j // 2) * 2 + core_of) * 2 + j % 2]

    copies = [
        pltpu.make_async_copy(source, held, sems.at[n])
        for n, (source, held) in enumerate(
            ((queries, q_held), (cotangent, c_held), (peer_both, peer_held))
        )
    ]
    for copy in copies:
        copy.start()
    for n, (ref, core_of, _) in enumerate(sides):
        for j in range(blocks // 2):
            pltpu.make_async_copy(
                ref.at[j * block : (j + 1) * block, :],
                kv_held.at[rows_at(true_block(core_of, j) + 1, block), :],
                sems.at[len(copies) + n],
            ).start()
    kv_held[:block, :] = jnp.zeros((block, 2 * head_size), kv_held.dtype)
    key_acc[...] = jnp.zeros_like(key_acc)
    value_acc[...] = jnp.zeros_like(value_acc)
    for copy in copies:
        copy.wait()
    for i in range(2 * own_blocks):
        here = slice(i % own_blocks * block, (i % own_blocks + 1) * block)
        for h in range(heads):
            part = slice(h * block, (h + 1) * block)
            if i < own_blocks:
                head = rows_at(core * heads + h, head_size)
                q, c = q_held[here, head], c_held[here, head]
            else:
                q = peer_held[here, h * head_size : (h + 1) * head_size]
                c = peer_held[here, (heads + h) * head_size : (heads + h + 1) * head_size]
            q_rows[i, part, :], c_rows[i, part, :] = q, c
            q_columns[i, :, part], c_columns[i, :, part] = q.T, c.T
    for n, (ref, _, _) in enumerate(sides):
        pltpu.make_async_copy(
            ref, kv_held.at[: blocks // 2 * block, :], sems.at[len(copies) + n]
        ).wait()

    def chunk_rows(last, c):
        return pl.ds(pl.multiple_of((last - 2 * c) * block, block), 2 * block)

    def one_block(i, _):
        here = rows_at(i, block)
        ctx_of = jnp.where(i < own_blocks, ctx, ctx + 1 - 2 * core)
        last = meta[docs + own_blocks * ctx_of + lax.rem(i, own_blocks)]
        start = last * block
        position = start + lax.rem(lax.broadcasted_iota(jnp.int32, (1, columns), 1), block)
        own_start = jnp.zeros((1, columns), jnp.int32)
        first = jnp.int32(0)
        for d in range(docs):
            doc_start = meta[d]
            own_start = jnp.maximum(own_start, jnp.where(position >= doc_start, doc_start, 0))
            first = jnp.maximum(first, jnp.where(start >= doc_start, doc_start, 0))
        count = (last - first // block) // 2 + 1

        def score(c, best):
            scores[c] = jnp.dot(
                kv_held[chunk_rows(last, c), :head_size],
                q_columns[i],
                preferred_element_type=jnp.float32,
            )
            first_key = (last - 2 * c - 1) * block
            for at in range(0, KEY_CHUNK, STRIP):
                strip = slice(at, at + STRIP)
                key_pos = first_key + at + in_strip
                visible = (key_pos >= own_start) & (key_pos <= position)
                s = jnp.where(visible, scores[c, strip, :] * scale, NEGATIVE)
                scores[c, strip, :] = s
                best = jnp.maximum(best, jnp.max(s.reshape(STRIP // 8, 8, columns), axis=0))
            return best

        best = lax.fori_loop(
            0, count, score, jnp.full((8, columns), NEGATIVE, jnp.float32)
        )
        best = jnp.max(best, axis=0, keepdims=True)

        def mix(c, carried):
            total, acc = carried
            for at in range(0, KEY_CHUNK, STRIP):
                strip = slice(at, at + STRIP)
                w = jnp.exp(scores[c, strip, :] - best)
                scores[c, strip, :] = w
                low[0, strip, :] = w.astype(jnp.bfloat16)
                total = total + jnp.sum(w.reshape(STRIP // 8, 8, columns), axis=0)
            acc = acc + lax.dot_general(
                kv_held[chunk_rows(last, c), head_size:],
                low[0],
                (((0,), (0,)), ((), ())),
                preferred_element_type=jnp.float32,
            )
            return total, acc

        total, acc = lax.fori_loop(
            0,
            count,
            mix,
            (jnp.zeros((8, columns), jnp.float32), jnp.zeros((head_size, columns), jnp.float32)),
        )
        total = jnp.sum(total, axis=0, keepdims=True)
        mixed = (acc / total).astype(jnp.bfloat16)
        expected = jnp.sum(
            mixed.astype(jnp.float32) * c_columns[i].astype(jnp.float32), axis=0, keepdims=True
        )
        per_total = 1.0 / total
        for h in range(heads):
            mixed_out[here, h * head_size : (h + 1) * head_size] = mixed[
                :, h * block : (h + 1) * block
            ].T

        def back(c, q_acc):
            chunk = chunk_rows(last, c)
            prob_grad[...] = jnp.dot(
                kv_held[chunk, head_size:], c_columns[i], preferred_element_type=jnp.float32
            )
            for at in range(0, KEY_CHUNK, STRIP):
                strip = slice(at, at + STRIP)
                probability = scores[c, strip, :] * per_total
                low[0, strip, :] = probability.astype(jnp.bfloat16)
                low[1, strip, :] = (probability * (prob_grad[strip, :] - expected)).astype(
                    jnp.bfloat16
                )
            value_acc[chunk, :] += jnp.dot(low[0], c_rows[i], preferred_element_type=jnp.float32)
            key_acc[chunk, :] += jnp.dot(low[1], q_rows[i], preferred_element_type=jnp.float32)
            return q_acc + lax.dot_general(
                kv_held[chunk, :head_size],
                low[1],
                (((0,), (0,)), ((), ())),
                preferred_element_type=jnp.float32,
            )

        q_acc = lax.fori_loop(
            0, count, back, jnp.zeros((head_size, columns), jnp.float32)
        )
        q_grad = (q_acc * scale).astype(jnp.bfloat16)
        for h in range(heads):
            query_grad[here, h * head_size : (h + 1) * head_size] = q_grad[
                :, h * block : (h + 1) * block
            ].T
        return 0

    lax.fori_loop(0, 2 * own_blocks, one_block, 0)
    for _, core_of, out in sides:
        for j in range(blocks // 2):
            source = rows_at(true_block(core_of, j) + 1, block)
            part = slice(j * block, (j + 1) * block)
            out[part, :head_size] = (key_acc[source, :] * scale).astype(out.dtype)
            out[part, head_size:] = value_acc[source, :].astype(out.dtype)


def attention(meta, queries, cotangent, peer_both, kv_same, kv_other, head_size, docs, blocks):
    rows, width = queries.shape
    heads = width // head_size // 2
    length = kv_same.shape[0] + kv_other.shape[0]
    block = length // blocks
    columns = heads * block
    query_blocks = 2 * rows // block
    in_vmem = pl.BlockSpec(memory_space=pltpu.VMEM)
    most_chunks = 10
    visible = 9 * KEY_CHUNK
    return pl.pallas_call(
        functools.partial(
            attention_kernel, heads=heads, head_size=head_size, block=block, docs=docs, blocks=blocks
        ),
        out_shape=(
            jax.ShapeDtypeStruct((2 * rows, width // 2), jnp.bfloat16),
            jax.ShapeDtypeStruct((2 * rows, width // 2), jnp.bfloat16),
            jax.ShapeDtypeStruct(kv_same.shape, jnp.float32),
            jax.ShapeDtypeStruct(kv_other.shape, jnp.bfloat16),
        ),
        in_specs=[pl.BlockSpec(memory_space=pltpu.SMEM)] + [pl.BlockSpec(memory_space=pl.ANY)] * 5,
        out_specs=(in_vmem,) * 4,
        scratch_shapes=[
            pltpu.VMEM(queries.shape, jnp.bfloat16),
            pltpu.VMEM(cotangent.shape, jnp.bfloat16),
            pltpu.VMEM(peer_both.shape, jnp.bfloat16),
            pltpu.VMEM((block + length, 2 * head_size), jnp.bfloat16),
            pltpu.VMEM((block + length, head_size), jnp.float32),
            pltpu.VMEM((block + length, head_size), jnp.float32),
            pltpu.VMEM((most_chunks, KEY_CHUNK, columns), jnp.float32),
            pltpu.VMEM((KEY_CHUNK, columns), jnp.float32),
            pltpu.VMEM((2, KEY_CHUNK, columns), jnp.bfloat16),
            pltpu.VMEM((query_blocks, head_size, columns), jnp.bfloat16),
            pltpu.VMEM((query_blocks, head_size, columns), jnp.bfloat16),
            pltpu.VMEM((query_blocks, columns, head_size), jnp.bfloat16),
            pltpu.VMEM((query_blocks, columns, head_size), jnp.bfloat16),
            pltpu.SemaphoreType.DMA((5,)),
        ],
        compiler_params=pltpu.CompilerParams(vmem_limit_bytes=26 << 20),
        cost_estimate=pl.CostEstimate(
            flops=28 * rows * heads * visible * head_size,
            bytes_accessed=8 * rows * width + 8 * length * head_size,
            transcendentals=2 * rows * heads * visible,
        ),
        name="masked_attention",
    )(meta, queries, cotangent, peer_both, kv_same, kv_other)


def body(tokens, queries, cotangent, latent_key, latent_value, lengths, block_order):
    token_rows = tokens[0]
    rows_here, features = token_rows.shape
    head_size = latent_key.shape[1]
    docs, blocks = lengths.shape[1], block_order.shape[1]
    me = lax.axis_index(AXES)
    table = lax.dynamic_index_in_dim(jnp.asarray(block_table()), me, keepdims=False)
    before = np.arange(docs)[:, None] < np.arange(docs)[None, :]
    doc_starts = jnp.sum(jnp.where(before, lengths[0][:, None], 0), axis=0)
    meta = jnp.concatenate(
        [
            doc_starts.astype(jnp.int32),
            block_order[0],
            jnp.stack([lax.axis_index(CTX), lax.axis_index("core")]).astype(jnp.int32),
        ]
    )

    core = lax.axis_index("core")
    peer_both = swap_cores(
        jnp.concatenate(
            [
                lax.dynamic_slice_in_dim(a[0], (1 - core) * a.shape[2] // 2, a.shape[2] // 2, 1)
                for a in (queries, cotangent)
            ],
            axis=1,
        )
    )
    head_rows = latent_key.shape[0]
    latents = side_by_side(latent_key, latent_value)
    latents = gather_ring(jnp.concatenate(gather_ring(latents, 0), axis=0), 1)
    latents[0], peer_both, meta = lax.optimization_barrier((latents[0], peer_both, meta))
    sums = small(
        magnitudes_kernel,
        "magnitudes",
        jax.ShapeDtypeStruct((8, 2 * head_size), jnp.float32),
        *latents,
    )
    sums = sum(gather_ring(sums, 2))
    sums = sums + swap_cores(sums)
    weights = small(
        functools.partial(ternary_kernel, entries=features * head_size),
        "ternarize",
        jax.ShapeDtypeStruct((16 * head_rows, 2 * head_size), jnp.bfloat16),
        sums,
        *latents,
    )
    weights, shuffle_table = lax.optimization_barrier((weights, table))
    weight_parts = gather_ring(weights, 2)
    tokens_own, tokens_other = shuffle(shuffle_table, token_rows)
    other_parts = [swap_cores(part) for part in weight_parts]
    part_rows = weights.shape[0]
    projected = 0.0
    for i, (own, other) in enumerate(zip(weight_parts, other_parts)):
        cut = slice(i * part_rows, (i + 1) * part_rows)
        for rows, part in ((tokens_own, own), (tokens_other, other)):
            projected = projected + jnp.dot(
                rows[:, cut], part, preferred_element_type=jnp.float32
            )
    kv_here = projected.astype(jnp.bfloat16)
    groups = lax.axis_size(SAME_CORE_CTX)
    kv_same = lax.all_to_all(
        jnp.broadcast_to(kv_here[None], (groups,) + kv_here.shape).reshape(-1, 2 * head_size),
        SAME_CORE_CTX,
        split_axis=0,
        concat_axis=0,
        tiled=True,
    )
    kv_other = swap_cores(kv_same)
    tokens_peer = swap_cores(tokens_other)

    mixed, query_grad, same_terms, other_terms = attention(
        meta, queries[0], cotangent[0], peer_both, kv_same, kv_other, head_size, docs, blocks
    )
    same_terms, other_terms, tokens_peer = lax.optimization_barrier(
        (same_terms, other_terms, tokens_peer)
    )
    chip_terms = (same_terms + swap_cores(other_terms).astype(jnp.float32)).astype(jnp.bfloat16)
    terms = lax.all_to_all(chip_terms, SAME_CORE_CTX, split_axis=0, concat_axis=0, tiled=True)
    grads = jnp.sum(
        terms.reshape(groups, rows_here, 2 * head_size).astype(jnp.float32), axis=0
    ).astype(jnp.bfloat16)
    peer_grads = swap_cores(grads)

    (opposite,) = sent_along_ring(
        weight_terms(grads, peer_grads, tokens_own, tokens_peer, 3, 1, jnp.bfloat16), 2, OFFSETS[3:]
    )
    arrived = sent_along_ring(
        weight_terms(grads, peer_grads, tokens_own, tokens_peer, 1, 2, jnp.bfloat16), 2, OFFSETS[1:3]
    )
    arrived.append(opposite)
    (summed,) = weight_terms(grads, peer_grads, tokens_own, tokens_peer, 0, 1, jnp.float32)
    summed = summed + sum(piece.astype(jnp.float32) for piece in arrived)
    token_grad = token_gradient(table, grads, weight_parts + other_parts)
    summed, token_grad = lax.optimization_barrier((summed, token_grad))
    from_peer = swap_cores(jnp.concatenate([mixed[rows_here:], query_grad[rows_here:]], axis=1))

    def both_halves(own, peers):
        return jnp.concatenate(
            [jnp.where(core == 0, own, peers), jnp.where(core == 0, peers, own)], axis=1
        )

    half_width = mixed.shape[1]
    mixed = both_halves(mixed[:rows_here], from_peer[:, :half_width])
    query_grad = both_halves(query_grad[:rows_here], from_peer[:, half_width:])
    summed, *pieces = jnp.split(summed, 4, axis=1)
    summed = summed + sum(piece.astype(jnp.float32) for piece in sent_along_ring(pieces, 1))
    summed, *pieces = jnp.split(summed, 4, axis=1)
    half_shape = jax.ShapeDtypeStruct((head_rows, head_size), jnp.float32)
    key_grad, value_grad = small(
        last_sum_kernel, "last_sum", (half_shape, half_shape), summed, *sent_along_ring(pieces, 0)
    )
    return (
        mixed[None],
        query_grad[None],
        token_grad[None],
        key_grad,
        value_grad,
    )


def solution(mesh):
    torus = Mesh(mesh.devices.reshape(SIZES), AXES)
    whole = CTX + DP
    in_specs = (
        P(DP, CTX, None),
        P(DP, CTX, None),
        P(DP, CTX, None),
        P(whole, None),
        P(whole, None),
        P(DP, None),
        P(DP, None),
    )
    out_specs = (
        P(DP, CTX, None),
        P(DP, CTX, None),
        P(DP, CTX, None),
        P(whole, None),
        P(whole, None),
    )
    return jax.shard_map(body, mesh=torus, in_specs=in_specs, out_specs=out_specs, check_vma=False)
```

```python
import functools

import jax
import jax.numpy as jnp
import numpy as np
from jax import lax
from jax.experimental import pallas as pl
from jax.experimental.pallas import tpu as pltpu
from jax.sharding import Mesh
from jax.sharding import PartitionSpec as P

AXES = ("y", "zh", "core", "x", "zl")
SIZES = (4, 2, 2, 4, 2)
CTX = ("y", "zh", "core")
DP = ("x", "zl")
SAME_CORE_CTX = ("y", "zh")
DEVICES = int(np.prod(SIZES))

EPSILON = 1e-05
NEGATIVE = -1e30
KEY_CHUNK = 256
STRIP = 32

RING_ORDER = {0: ("x", "y", "z"), 1: ("y", "z", "x")}
OFFSETS = (0, -1, 1, 2)


def coordinates(device):
    y, zh, core, x, zl = (int(v) for v in np.unravel_index(device, SIZES))
    return {"y": y, "z": zh * 2 + zl, "x": x, "core": core}


def device_of(place):
    return int(
        np.ravel_multi_index(
            (place["y"], place["z"] // 2, place["core"], place["x"], place["z"] % 2), SIZES
        )
    )


def moved(change):
    pairs = []
    for device in range(DEVICES):
        place = coordinates(device)
        change(place)
        pairs.append((device, device_of(place)))
    return pairs


def along_ring(phase, step):
    def change(place):
        axis = RING_ORDER[place["core"]][phase]
        place[axis] = (place[axis] + step) % 4

    return moved(change)


def to_other_core(place):
    place["core"] = 1 - place["core"]


def swap_cores(value):
    return lax.ppermute(value, AXES, moved(to_other_core))


def block_table():
    table = np.zeros((DEVICES, DEVICES), np.int32)
    for device in range(DEVICES):
        here = coordinates(device)
        at = 0
        for core in (here["core"], 1 - here["core"]):
            order = RING_ORDER[core]
            for last in OFFSETS:
                for middle in OFFSETS:
                    for first in OFFSETS:
                        place = dict(here, core=core)
                        for axis, step in zip(order, (first, middle, last)):
                            place[axis] = (place[axis] + step) % 4
                        table[device, at] = device_of(place)
                        at += 1
    return table


def gather_ring(value, phase):
    return [value] + [
        lax.ppermute(value, AXES, along_ring(phase, -offset)) for offset in OFFSETS[1:]
    ]


def sent_along_ring(pieces, phase, offsets=OFFSETS[1:]):
    return [
        lax.ppermute(piece.astype(jnp.bfloat16), AXES, along_ring(phase, offset))
        for piece, offset in zip(pieces, offsets)
    ]


def shuffle_kernel(table, tokens, own, other):
    width = own.shape[1] * 2 // DEVICES
    half = DEVICES // 2

    def move(j, _):
        target = pl.ds(pl.multiple_of(j * width, width), width)
        for first, out in ((0, own), (half, other)):
            source = pl.ds(pl.multiple_of(table[first + j] * width, width), width)
            out[:, target] = tokens[:, source]
        return 0

    lax.fori_loop(0, half, move, 0, unroll=8)


def shuffle(table, tokens):
    rows, features = tokens.shape
    step_rows = 32
    half = jax.ShapeDtypeStruct((rows, features // 2), tokens.dtype)
    half_spec = pl.BlockSpec((step_rows, features // 2), lambda i: (i, 0))
    return pl.pallas_call(
        shuffle_kernel,
        grid=(rows // step_rows,),
        out_shape=(half, half),
        in_specs=[
            pl.BlockSpec(memory_space=pltpu.SMEM),
            pl.BlockSpec((step_rows, features), lambda i: (i, 0)),
        ],
        out_specs=(half_spec, half_spec),
        compiler_params=pltpu.CompilerParams(vmem_limit_bytes=16 << 20),
        cost_estimate=pl.CostEstimate(
            flops=0, bytes_accessed=4 * rows * features, transcendentals=0
        ),
        name="shuffle_tokens",
    )(table, tokens)


def weight_terms_kernel(grads, peer_grads, tokens, peer_tokens, *rest, first, count):
    outs, (held_grads, turned, held, made, grad_sems, sems, out_sems) = rest[:count], rest[count:]
    grad_copies = [
        pltpu.make_async_copy(source, held_grads.at[side], grad_sems.at[side])
        for side, source in enumerate((grads, peer_grads))
    ]
    for copy in grad_copies:
        copy.start()
    step = held.shape[2] // (2 * count)
    copies = []
    for n in range(2 * count):
        here, there = slice(n * step, (n + 1) * step), slice(first + n * step, first + (n + 1) * step)
        copies.append(
            [
                pltpu.make_async_copy(source.at[:, there], held.at[side, :, here], sems.at[side, n])
                for side, source in enumerate((tokens, peer_tokens))
            ]
        )
    for pair in copies:
        for copy in pair:
            copy.start()
    for side, copy in enumerate(grad_copies):
        copy.wait()
        turned[side] = held_grads[side].T
    sends = []
    for n, pair in enumerate(copies):
        here = slice(n * step, (n + 1) * step)
        for copy in pair:
            copy.wait()
        term = jnp.dot(turned[0], held[0, :, here], preferred_element_type=jnp.float32) + jnp.dot(
            turned[1], held[1, :, here], preferred_element_type=jnp.float32
        )
        made[:, here] = term.astype(made.dtype)
        sends.append(
            pltpu.make_async_copy(
                made.at[:, here],
                outs[n // 2].at[:, n % 2 * step : (n % 2 + 1) * step],
                out_sems.at[n],
            )
        )
        sends[-1].start()
    for send in sends:
        send.wait()


def weight_terms(grads, peer_grads, tokens, peer_tokens, first, count, dtype):
    rows, features = tokens.shape
    both = grads.shape[1]
    width = features // len(OFFSETS)
    anywhere = pl.BlockSpec(memory_space=pl.ANY)
    return pl.pallas_call(
        functools.partial(weight_terms_kernel, first=first * width, count=count),
        out_shape=(jax.ShapeDtypeStruct((both, width), dtype),) * count,
        in_specs=[anywhere] * 4,
        out_specs=(anywhere,) * count,
        scratch_shapes=[
            pltpu.VMEM((2, rows, both), jnp.bfloat16),
            pltpu.VMEM((2, both, rows), jnp.bfloat16),
            pltpu.VMEM((2, rows, count * width), tokens.dtype),
            pltpu.VMEM((both, count * width), dtype),
            pltpu.SemaphoreType.DMA((2,)),
            pltpu.SemaphoreType.DMA((2, 2 * count)),
            pltpu.SemaphoreType.DMA((2 * count,)),
        ],
        compiler_params=pltpu.CompilerParams(vmem_limit_bytes=58 << 20),
        cost_estimate=pl.CostEstimate(
            flops=4 * rows * both * count * width,
            bytes_accessed=(4 * rows + 2 * both) * count * width,
            transcendentals=0,
        ),
        name="weight_terms",
    )(grads, peer_grads, tokens, peer_tokens)


def pair_kernel(left, right, out, sems):
    width = left.shape[1]
    copies = [
        pltpu.make_async_copy(source, out.at[:, n * width : (n + 1) * width], sems.at[n])
        for n, source in enumerate((left, right))
    ]
    for copy in copies:
        copy.start()
    for copy in copies:
        copy.wait()


def side_by_side(left, right):
    anywhere = pl.BlockSpec(memory_space=pl.ANY)
    return pl.pallas_call(
        pair_kernel,
        out_shape=jax.ShapeDtypeStruct((left.shape[0], 2 * left.shape[1]), left.dtype),
        in_specs=[anywhere, anywhere],
        out_specs=pl.BlockSpec(memory_space=pltpu.VMEM),
        scratch_shapes=[pltpu.SemaphoreType.DMA((2,))],
        compiler_params=pltpu.CompilerParams(vmem_limit_bytes=58 << 20),
        name="pair_latents",
    )(left, right)


def magnitudes_kernel(*refs):
    pieces, out = refs[:-1], refs[-1]
    out[...] = sum(
        jnp.sum(jnp.abs(piece[...]).reshape(-1, *out.shape), axis=0) for piece in pieces
    )


def ternary_kernel(sums, *refs, entries):
    pieces, out = refs[:-1], refs[-1]
    half = out.shape[1] // 2
    for columns in (slice(0, half), slice(half, 2 * half)):
        scale = jnp.sum(sums[:, columns]) / entries + EPSILON
        level = jnp.full((1, half), scale, jnp.float32)
        for n, piece in enumerate(pieces):
            rows = piece.shape[0]
            latent = piece[:, columns]
            out[n * rows : (n + 1) * rows, columns] = jnp.where(
                latent >= 0.5 * level, level, jnp.where(latent <= -0.5 * level, -level, 0.0)
            ).astype(jnp.bfloat16)


def last_sum_kernel(own, first, second, third, key_out, value_out):
    total = own[...]
    for piece in (first, second, third):
        total = total + piece[...].astype(jnp.float32)
    half = key_out.shape[1]
    key_out[...] = total[:half].T
    value_out[...] = total[half:].T


def small(kernel, name, out_shape, *args):
    in_vmem = pl.BlockSpec(memory_space=pltpu.VMEM)
    return pl.pallas_call(
        kernel,
        out_shape=out_shape,
        in_specs=[in_vmem] * len(args),
        out_specs=jax.tree.map(lambda _: in_vmem, out_shape),
        compiler_params=pltpu.CompilerParams(vmem_limit_bytes=12 << 20),
        cost_estimate=pl.CostEstimate(
            flops=0, bytes_accessed=sum(a.size * a.dtype.itemsize for a in args), transcendentals=0
        ),
        name=name,
    )(*args)


def token_grad_kernel(table, grads, *rest, count):
    weights, out = rest[:count], rest[count]
    held, held_sems, buffers, sems = rest[count + 1 :]
    slots, step_width = held.shape[:2]
    width = out.shape[1] // DEVICES
    per_step = step_width // width
    steps_each = weights[0].shape[0] // step_width

    def fetch(step):
        part = (step % steps_each) * step_width
        return pltpu.make_async_copy(
            weights[step // steps_each].at[part : part + step_width, :],
            held.at[step % slots],
            held_sems.at[step % slots],
        )

    for step in range(slots - 1):
        fetch(step).start()
    for step in range(count * steps_each):
        slot = step % 2
        buffer, sem = buffers.at[slot], sems.at[slot]
        if step + slots - 1 < count * steps_each:
            fetch(step + slots - 1).start()
        fetch(step).wait()
        if step >= 2:
            pltpu.make_async_copy(buffer, buffer, sem).wait()
        buffers[slot] = lax.dot_general(
            grads[...],
            held[step % slots],
            (((1,), (1,)), ((), ())),
            preferred_element_type=jnp.float32,
        ).astype(jnp.bfloat16)
        for j in range(per_step):
            target = pl.ds(pl.multiple_of(table[step * per_step + j] * width, width), width)
            pltpu.make_async_copy(
                buffer.at[:, j * width : (j + 1) * width], out.at[:, target], sem
            ).start()
    for slot in range(2):
        pltpu.make_async_copy(buffers.at[slot], buffers.at[slot], sems.at[slot]).wait()


def token_gradient(table, grads, weights):
    rows, both = grads.shape
    features = sum(w.shape[0] for w in weights)
    step_width = 1024
    slots = 4
    return pl.pallas_call(
        functools.partial(token_grad_kernel, count=len(weights)),
        out_shape=jax.ShapeDtypeStruct((rows, features), jnp.bfloat16),
        in_specs=[
            pl.BlockSpec(memory_space=pltpu.SMEM),
            pl.BlockSpec(memory_space=pltpu.VMEM),
        ]
        + [pl.BlockSpec(memory_space=pltpu.HBM)] * len(weights),
        out_specs=pl.BlockSpec(memory_space=pl.ANY),
        scratch_shapes=[
            pltpu.VMEM((slots, step_width, both), jnp.bfloat16),
            pltpu.SemaphoreType.DMA((slots,)),
            pltpu.VMEM((2, rows, step_width), jnp.bfloat16),
            pltpu.SemaphoreType.DMA((2,)),
        ],
        compiler_params=pltpu.CompilerParams(vmem_limit_bytes=58 << 20),
        cost_estimate=pl.CostEstimate(
            flops=2 * rows * both * features,
            bytes_accessed=2 * features * (rows + both),
            transcendentals=0,
        ),
        name="token_gradient",
    )(table, grads, *weights)


def attention_kernel(
    meta, q_columns, c_columns, q_rows, c_rows, kv_same, kv_other,
    mixed_out, query_grad, same_out, other_out,
    kv_held, key_acc, value_acc, scores, prob_grad, low, sems,
    *, heads, head_size, block, docs, blocks,
):
    scale = head_size ** (-0.5)
    columns = heads * block
    ctx, core = meta[docs + blocks], meta[docs + blocks + 1]
    own_blocks = q_rows.shape[0] // 2
    in_strip = lax.broadcasted_iota(jnp.int32, (STRIP, columns), 0)
    sides = ((kv_same, core, same_out), (kv_other, 1 - core, other_out))

    def rows_at(index, size):
        return pl.ds(pl.multiple_of(index * size, size), size)

    def true_block(core_of, j):
        return meta[docs + ((j // 2) * 2 + core_of) * 2 + j % 2]

    for n, (ref, core_of, _) in enumerate(sides):
        for j in range(blocks // 2):
            pltpu.make_async_copy(
                ref.at[j * block : (j + 1) * block, :],
                kv_held.at[rows_at(true_block(core_of, j) + 1, block), :],
                sems.at[n],
            ).start()
    kv_held[:block, :] = jnp.zeros((block, 2 * head_size), kv_held.dtype)
    key_acc[...] = jnp.zeros_like(key_acc)
    value_acc[...] = jnp.zeros_like(value_acc)
    for n, (ref, _, _) in enumerate(sides):
        pltpu.make_async_copy(
            ref, kv_held.at[: blocks // 2 * block, :], sems.at[n]
        ).wait()

    def chunk_rows(last, c):
        return pl.ds(pl.multiple_of((last - 2 * c) * block, block), 2 * block)

    def one_block(i, _):
        here = rows_at(i, block)
        ctx_of = jnp.where(i < own_blocks, ctx, ctx + 1 - 2 * core)
        last = meta[docs + own_blocks * ctx_of + lax.rem(i, own_blocks)]
        start = last * block
        position = start + lax.rem(lax.broadcasted_iota(jnp.int32, (1, columns), 1), block)
        own_start = jnp.zeros((1, columns), jnp.int32)
        first = jnp.int32(0)
        for d in range(docs):
            doc_start = meta[d]
            own_start = jnp.maximum(own_start, jnp.where(position >= doc_start, doc_start, 0))
            first = jnp.maximum(first, jnp.where(start >= doc_start, doc_start, 0))
        count = (last - first // block) // 2 + 1

        def score(c, best):
            scores[c] = jnp.dot(
                kv_held[chunk_rows(last, c), :head_size],
                q_columns[i],
                preferred_element_type=jnp.float32,
            )
            first_key = (last - 2 * c - 1) * block
            for at in range(0, KEY_CHUNK, STRIP):
                strip = slice(at, at + STRIP)
                key_pos = first_key + at + in_strip
                visible = (key_pos >= own_start) & (key_pos <= position)
                s = jnp.where(visible, scores[c, strip, :] * scale, NEGATIVE)
                scores[c, strip, :] = s
                best = jnp.maximum(best, jnp.max(s.reshape(STRIP // 8, 8, columns), axis=0))
            return best

        best = lax.fori_loop(
            0, count, score, jnp.full((8, columns), NEGATIVE, jnp.float32)
        )
        best = jnp.max(best, axis=0, keepdims=True)

        def mix(c, carried):
            total, acc = carried
            for at in range(0, KEY_CHUNK, STRIP):
                strip = slice(at, at + STRIP)
                w = jnp.exp(scores[c, strip, :] - best)
                scores[c, strip, :] = w
                low[0, strip, :] = w.astype(jnp.bfloat16)
                total = total + jnp.sum(w.reshape(STRIP // 8, 8, columns), axis=0)
            acc = acc + lax.dot_general(
                kv_held[chunk_rows(last, c), head_size:],
                low[0],
                (((0,), (0,)), ((), ())),
                preferred_element_type=jnp.float32,
            )
            return total, acc

        total, acc = lax.fori_loop(
            0,
            count,
            mix,
            (jnp.zeros((8, columns), jnp.float32), jnp.zeros((head_size, columns), jnp.float32)),
        )
        total = jnp.sum(total, axis=0, keepdims=True)
        mixed = (acc / total).astype(jnp.bfloat16)
        expected = jnp.sum(
            mixed.astype(jnp.float32) * c_columns[i].astype(jnp.float32), axis=0, keepdims=True
        )
        per_total = 1.0 / total
        for h in range(heads):
            mixed_out[here, h * head_size : (h + 1) * head_size] = mixed[
                :, h * block : (h + 1) * block
            ].T

        def back(c, q_acc):
            chunk = chunk_rows(last, c)
            prob_grad[...] = jnp.dot(
                kv_held[chunk, head_size:], c_columns[i], preferred_element_type=jnp.float32
            )
            for at in range(0, KEY_CHUNK, STRIP):
                strip = slice(at, at + STRIP)
                probability = scores[c, strip, :] * per_total
                low[0, strip, :] = probability.astype(jnp.bfloat16)
                low[1, strip, :] = (probability * (prob_grad[strip, :] - expected)).astype(
                    jnp.bfloat16
                )
            value_acc[chunk, :] += jnp.dot(low[0], c_rows[i], preferred_element_type=jnp.float32)
            key_acc[chunk, :] += jnp.dot(low[1], q_rows[i], preferred_element_type=jnp.float32)
            return q_acc + lax.dot_general(
                kv_held[chunk, :head_size],
                low[1],
                (((0,), (0,)), ((), ())),
                preferred_element_type=jnp.float32,
            )

        q_acc = lax.fori_loop(
            0, count, back, jnp.zeros((head_size, columns), jnp.float32)
        )
        q_grad = (q_acc * scale).astype(jnp.bfloat16)
        for h in range(heads):
            query_grad[here, h * head_size : (h + 1) * head_size] = q_grad[
                :, h * block : (h + 1) * block
            ].T
        return 0

    lax.fori_loop(0, 2 * own_blocks, one_block, 0)
    for _, core_of, out in sides:
        for j in range(blocks // 2):
            source = rows_at(true_block(core_of, j) + 1, block)
            part = slice(j * block, (j + 1) * block)
            out[part, :head_size] = (key_acc[source, :] * scale).astype(out.dtype)
            out[part, head_size:] = value_acc[source, :].astype(out.dtype)


def arrange_kernel(core_of, queries, cotangent, peer_both, q_columns, c_columns, q_rows, c_rows):
    total, columns, head_size = q_rows.shape
    own_blocks = total // 2
    block = queries.shape[0] // own_blocks
    heads = columns // block
    for i in range(total):
        here = slice(i % own_blocks * block, (i % own_blocks + 1) * block)
        for h in range(heads):
            part = slice(h * block, (h + 1) * block)
            if i < own_blocks:
                at = pl.multiple_of((core_of[0] * heads + h) * head_size, head_size)
                head = pl.ds(at, head_size)
                q, c = queries[here, head], cotangent[here, head]
            else:
                q = peer_both[here, h * head_size : (h + 1) * head_size]
                c = peer_both[here, (heads + h) * head_size : (heads + h + 1) * head_size]
            q_rows[i, part, :], c_rows[i, part, :] = q, c
            q_columns[i, :, part], c_columns[i, :, part] = q.T, c.T


def arrange(core, queries, cotangent, peer_both, head_size, block):
    rows, width = queries.shape
    columns = width // head_size // 2 * block
    count = 2 * rows // block
    across = jax.ShapeDtypeStruct((count, head_size, columns), queries.dtype)
    along = jax.ShapeDtypeStruct((count, columns, head_size), queries.dtype)
    in_vmem = pl.BlockSpec(memory_space=pltpu.VMEM)
    return pl.pallas_call(
        arrange_kernel,
        out_shape=(across, across, along, along),
        in_specs=[pl.BlockSpec(memory_space=pltpu.SMEM)] + [in_vmem] * 3,
        out_specs=(in_vmem,) * 4,
        compiler_params=pltpu.CompilerParams(vmem_limit_bytes=16 << 20),
        cost_estimate=pl.CostEstimate(
            flops=0, bytes_accessed=14 * rows * width, transcendentals=0
        ),
        name="arrange_heads",
    )(core, queries, cotangent, peer_both)


def attention(meta, arranged, kv_same, kv_other, head_size, docs, blocks):
    length = kv_same.shape[0] + kv_other.shape[0]
    block = length // blocks
    query_blocks, _, columns = arranged[0].shape
    heads = columns // block
    rows, width = query_blocks * block // 2, 2 * heads * head_size
    in_vmem = pl.BlockSpec(memory_space=pltpu.VMEM)
    most_chunks = 10
    visible = 9 * KEY_CHUNK
    return pl.pallas_call(
        functools.partial(
            attention_kernel, heads=heads, head_size=head_size, block=block, docs=docs, blocks=blocks
        ),
        out_shape=(
            jax.ShapeDtypeStruct((2 * rows, width // 2), jnp.bfloat16),
            jax.ShapeDtypeStruct((2 * rows, width // 2), jnp.bfloat16),
            jax.ShapeDtypeStruct(kv_same.shape, jnp.float32),
            jax.ShapeDtypeStruct(kv_other.shape, jnp.bfloat16),
        ),
        in_specs=[pl.BlockSpec(memory_space=pltpu.SMEM)]
        + [in_vmem] * 4
        + [pl.BlockSpec(memory_space=pl.ANY)] * 2,
        out_specs=(in_vmem,) * 4,
        scratch_shapes=[
            pltpu.VMEM((block + length, 2 * head_size), jnp.bfloat16),
            pltpu.VMEM((block + length, head_size), jnp.float32),
            pltpu.VMEM((block + length, head_size), jnp.float32),
            pltpu.VMEM((most_chunks, KEY_CHUNK, columns), jnp.float32),
            pltpu.VMEM((KEY_CHUNK, columns), jnp.float32),
            pltpu.VMEM((2, KEY_CHUNK, columns), jnp.bfloat16),
            pltpu.SemaphoreType.DMA((2,)),
        ],
        compiler_params=pltpu.CompilerParams(vmem_limit_bytes=26 << 20),
        cost_estimate=pl.CostEstimate(
            flops=28 * rows * heads * visible * head_size,
            bytes_accessed=8 * rows * width + 8 * length * head_size,
            transcendentals=2 * rows * heads * visible,
        ),
        name="masked_attention",
    )(meta, *arranged, kv_same, kv_other)


def body(tokens, queries, cotangent, latent_key, latent_value, lengths, block_order):
    token_rows = tokens[0]
    rows_here, features = token_rows.shape
    head_size = latent_key.shape[1]
    docs, blocks = lengths.shape[1], block_order.shape[1]
    me = lax.axis_index(AXES)
    table = lax.dynamic_index_in_dim(jnp.asarray(block_table()), me, keepdims=False)
    before = np.arange(docs)[:, None] < np.arange(docs)[None, :]
    doc_starts = jnp.sum(jnp.where(before, lengths[0][:, None], 0), axis=0)
    meta = jnp.concatenate(
        [
            doc_starts.astype(jnp.int32),
            block_order[0],
            jnp.stack([lax.axis_index(CTX), lax.axis_index("core")]).astype(jnp.int32),
        ]
    )

    core = lax.axis_index("core")
    peer_both = swap_cores(
        jnp.concatenate(
            [
                lax.dynamic_slice_in_dim(a[0], (1 - core) * a.shape[2] // 2, a.shape[2] // 2, 1)
                for a in (queries, cotangent)
            ],
            axis=1,
        )
    )
    head_rows = latent_key.shape[0]
    latents = side_by_side(latent_key, latent_value)
    latents = gather_ring(jnp.concatenate(gather_ring(latents, 0), axis=0), 1)
    latents[0], peer_both, meta = lax.optimization_barrier((latents[0], peer_both, meta))
    block = rows_here * lax.axis_size(CTX) // blocks
    arranged = arrange(meta[-1:], queries[0], cotangent[0], peer_both, head_size, block)
    sums = small(
        magnitudes_kernel,
        "magnitudes",
        jax.ShapeDtypeStruct((8, 2 * head_size), jnp.float32),
        *latents,
    )
    sums = sum(gather_ring(sums, 2))
    sums = sums + swap_cores(sums)
    weights = small(
        functools.partial(ternary_kernel, entries=features * head_size),
        "ternarize",
        jax.ShapeDtypeStruct((16 * head_rows, 2 * head_size), jnp.bfloat16),
        sums,
        *latents,
    )
    weights, shuffle_table = lax.optimization_barrier((weights, table))
    weight_parts = gather_ring(weights, 2)
    tokens_own, tokens_other = shuffle(shuffle_table, token_rows)
    other_parts = [swap_cores(part) for part in weight_parts]
    part_rows = weights.shape[0]
    projected = 0.0
    for i, (own, other) in enumerate(zip(weight_parts, other_parts)):
        cut = slice(i * part_rows, (i + 1) * part_rows)
        for rows, part in ((tokens_own, own), (tokens_other, other)):
            projected = projected + jnp.dot(
                rows[:, cut], part, preferred_element_type=jnp.float32
            )
    kv_here = projected.astype(jnp.bfloat16)
    kv_here, arranged = lax.optimization_barrier((kv_here, arranged))
    groups = lax.axis_size(SAME_CORE_CTX)
    kv_same = lax.all_to_all(
        jnp.broadcast_to(kv_here[None], (groups,) + kv_here.shape).reshape(-1, 2 * head_size),
        SAME_CORE_CTX,
        split_axis=0,
        concat_axis=0,
        tiled=True,
    )
    kv_other = swap_cores(kv_same)
    tokens_peer = swap_cores(tokens_other)

    mixed, query_grad, same_terms, other_terms = attention(
        meta, arranged, kv_same, kv_other, head_size, docs, blocks
    )
    same_terms, other_terms, tokens_peer = lax.optimization_barrier(
        (same_terms, other_terms, tokens_peer)
    )
    chip_terms = (same_terms + swap_cores(other_terms).astype(jnp.float32)).astype(jnp.bfloat16)
    terms = lax.all_to_all(chip_terms, SAME_CORE_CTX, split_axis=0, concat_axis=0, tiled=True)
    grads = jnp.sum(
        terms.reshape(groups, rows_here, 2 * head_size).astype(jnp.float32), axis=0
    ).astype(jnp.bfloat16)
    peer_grads = swap_cores(grads)

    (opposite,) = sent_along_ring(
        weight_terms(grads, peer_grads, tokens_own, tokens_peer, 3, 1, jnp.bfloat16), 2, OFFSETS[3:]
    )
    arrived = sent_along_ring(
        weight_terms(grads, peer_grads, tokens_own, tokens_peer, 1, 2, jnp.bfloat16), 2, OFFSETS[1:3]
    )
    arrived.append(opposite)
    (summed,) = weight_terms(grads, peer_grads, tokens_own, tokens_peer, 0, 1, jnp.float32)
    summed = summed + sum(piece.astype(jnp.float32) for piece in arrived)
    token_grad = token_gradient(table, grads, weight_parts + other_parts)
    summed, token_grad = lax.optimization_barrier((summed, token_grad))
    from_peer = swap_cores(jnp.concatenate([mixed[rows_here:], query_grad[rows_here:]], axis=1))

    def both_halves(own, peers):
        return jnp.concatenate(
            [jnp.where(core == 0, own, peers), jnp.where(core == 0, peers, own)], axis=1
        )

    half_width = mixed.shape[1]
    mixed = both_halves(mixed[:rows_here], from_peer[:, :half_width])
    query_grad = both_halves(query_grad[:rows_here], from_peer[:, half_width:])
    summed, *pieces = jnp.split(summed, 4, axis=1)
    summed = summed + sum(piece.astype(jnp.float32) for piece in sent_along_ring(pieces, 1))
    summed, *pieces = jnp.split(summed, 4, axis=1)
    half_shape = jax.ShapeDtypeStruct((head_rows, head_size), jnp.float32)
    key_grad, value_grad = small(
        last_sum_kernel, "last_sum", (half_shape, half_shape), summed, *sent_along_ring(pieces, 0)
    )
    return (
        mixed[None],
        query_grad[None],
        token_grad[None],
        key_grad,
        value_grad,
    )


def solution(mesh):
    torus = Mesh(mesh.devices.reshape(SIZES), AXES)
    whole = CTX + DP
    in_specs = (
        P(DP, CTX, None),
        P(DP, CTX, None),
        P(DP, CTX, None),
        P(whole, None),
        P(whole, None),
        P(DP, None),
        P(DP, None),
    )
    out_specs = (
        P(DP, CTX, None),
        P(DP, CTX, None),
        P(DP, CTX, None),
        P(whole, None),
        P(whole, None),
    )
    return jax.shard_map(body, mesh=torus, in_specs=in_specs, out_specs=out_specs, check_vma=False)
```
